32 devices in a mesh: dp: 4 (over y, x), chan: 4 (over z), row: 2 (over core).
Axes of the slice: x: 2, y: 2, z: 4, core: 2. Of those that a mesh axis runs over, the one named last changes fastest.
Arguments:
- images: bfloat16 [4, 128, 320, 128], P('dp', 'row', 'chan'), may hold values from -6 to 6
- kernel: bfloat16 [9, 320, 320], P(None, 'dp', 'chan'), may hold values from -0.109375 to 0.109375
- cotangent: bfloat16 [4, 128, 320, 128], P('dp', 'row', 'chan'), may hold values from -6 to 6
Outputs:
- activated: bfloat16 [4, 128, 320, 128], P('dp', 'row', 'chan')
- input_grad: float32 [4, 128, 320, 128], P('dp', 'row', 'chan')
- kernel_grad: float32 [9, 320, 320], P(None, 'dp', 'chan')
The draws below stay inside these ranges and needn't reach their ends.
All inputs are finite; a program needn't handle non-finite values.
Results may differ from the reference program's by a relative error of at most 0.0029.
Values may be sent and summed in bfloat16 or wider, within the bound.
No kernel may reach another device: no remote copies, remote signals or barrier semaphores. Data moves between devices by JAX's collectives and lax.ppermute only.
A program may use at most 192 MiB of HBM per device.

```python
import jax
import jax.numpy as jnp

C = 320
W = 128
BATCH = 4
H = 128


def raised(drawn, rng, source, target, blocks, factor):
    def block_of(axis_at):
        return (jnp.arange(drawn.shape[axis_at]) // (drawn.shape[axis_at] // blocks)).reshape((-1,) + (1,) * (drawn.ndim - 1 - axis_at))

    first = jax.random.permutation(rng, blocks)[block_of(target)]
    other_side = (block_of(target) + blocks // 2) % blocks
    return jnp.where((block_of(source) == first) | (block_of(source) == other_side), factor * drawn, drawn)


def level_of(rng, dims, pieces, low, high):
    loudness = 1.0
    for position, blocks in pieces:
        heights = jax.random.uniform(jax.random.fold_in(jax.random.fold_in(rng, 6), position), (blocks,), jnp.float32, low / len(pieces), high / len(pieces))
        loudness = loudness * jnp.repeat(jnp.exp(heights), dims[position] // blocks).reshape((-1,) + (1,) * (len(dims) - 1 - position))
    return loudness


def bell_draw(rng, dims, spread, limit, split=(), dtype=jnp.bfloat16):
    loudness = level_of(rng, dims, split, -0.22, 0.18) if split else 1.0
    values = jax.random.normal(rng, dims, jnp.float32) * spread * loudness
    return jnp.minimum(jnp.maximum(values, -limit), limit).astype(dtype)


def noise_with(stream_key, shape, deviation, limit, shards, heavy, held_as=jnp.bfloat16):
    values = deviation * jax.random.normal(stream_key, shape, jnp.float32)
    if shards:
        values = values * level_of(stream_key, shape, shards, -0.22, 0.18)
    return jnp.clip(raised(values, jax.random.fold_in(stream_key, 3), *heavy), -limit, limit).astype(held_as)


def setup_inputs(seed: int = 0) -> dict:
    key_list = jax.random.split(jax.random.key(seed), 4)
    images = noise_with(key_list[0], (BATCH, H, C, W), 1.0, 6.0, ((0, 4), (1, 2), (2, 4)), (0, 2, 4, 2.0))
    kernel = bell_draw(key_list[1], (9, C, C), (9 * C) ** -0.5, 0.109375, ((1, 4), (2, 4)))
    cotangent = bell_draw(key_list[2], (BATCH, H, C, W), 1.0, 6.0, ((0, 4), (1, 2), (2, 4)))
    return dict(images=images, kernel=kernel, cotangent=cotangent)


def window_at(padded, tap_row, tap_col, height, width):
    return padded[:, tap_row:tap_row + height, :, tap_col:tap_col + width]


def reference(images, kernel, cotangent):
    batch_count, height, channels, width = images.shape
    padded = jnp.pad(images, ((0, 0), (1, 1), (0, 0), (1, 1)))
    kernel_wide = kernel.astype(jnp.float32)
    pre = jnp.zeros((batch_count, height, kernel.shape[2], width), jnp.float32)
    for tap_row in range(3):
        for tap_col in range(3):
            window = window_at(padded, tap_row, tap_col, height, width).astype(jnp.float32)
            pre = pre + jnp.einsum("nhiw,io->nhow", window, kernel_wide[3 * tap_row + tap_col])
    activated = jax.nn.silu(pre).astype(jnp.bfloat16)
    sigma = jax.nn.sigmoid(pre)
    slope = (cotangent.astype(jnp.float32) * sigma * (1.0 + pre * (1.0 - sigma))).astype(jnp.bfloat16)
    slope_padded = jnp.pad(slope, ((0, 0), (1, 1), (0, 0), (1, 1)))
    slope_wide = slope.astype(jnp.float32)
    input_grad = jnp.zeros((batch_count, height, channels, width), jnp.float32)
    grads = []
    for tap_row in range(3):
        for tap_col in range(3):
            window = window_at(slope_padded, 2 - tap_row, 2 - tap_col, height, width).astype(jnp.float32)
            input_grad = input_grad + jnp.einsum("nhow,io->nhiw", window, kernel_wide[3 * tap_row + tap_col])
            source = window_at(padded, tap_row, tap_col, height, width).astype(jnp.float32)
            grads.append(jnp.einsum("nhiw,nhow->io", source, slope_wide))
    return activated, input_grad, jnp.stack(grads)
```

```python
import functools

import jax
import jax.numpy as jnp
from jax import lax
from jax.experimental import pallas as pl
from jax.experimental.pallas import tpu as pltpu
from jax.sharding import PartitionSpec as P

VMEM_LIMIT = 60 * 1024 * 1024


def receive(block, axis, ahead):
    count = lax.axis_size(axis)
    return lax.ppermute(block, axis, [(i, (i - ahead) % count) for i in range(count)])


def home_of(row, chan, chans):
    return jnp.where(row % 2 == 0, chan, chans - 1 - chan)


def part(array, index, size, axis):
    return lax.dynamic_slice_in_dim(array, index * size, size, axis=axis)


def rotated(array, start, axis):
    twice = jnp.concatenate([array, array], axis=axis)
    return lax.dynamic_slice_in_dim(twice, start, array.shape[axis], axis=axis)


def columns_moved(block, step):
    width = block.shape[-1]
    lane = lax.broadcasted_iota(jnp.int32, block.shape, block.ndim - 1)
    if step < 0:
        moved = pltpu.roll(block, 1, block.ndim - 1)
        return jnp.where(lane == 0, jnp.zeros_like(block), moved)
    moved = pltpu.roll(block, width - 1, block.ndim - 1)
    return jnp.where(lane == width - 1, jnp.zeros_like(block), moved)


def place(stacked, channel, row, block, channels):
    depth, width = block.shape
    lanes = pl.ds(pl.multiple_of(row * width, width), width)
    wide = block.astype(jnp.float32)
    stacked[pl.ds(channel, depth), lanes] = columns_moved(wide, -1).astype(block.dtype)
    stacked[pl.ds(channels + channel, depth), lanes] = block
    stacked[pl.ds(2 * channels + channel, depth), lanes] = columns_moved(wide, 1).astype(block.dtype)


def taps(kernels, stacked, first, rows, width):
    total = None
    for tap_row in range(3):
        start = pl.multiple_of((first + tap_row) * width, width)
        term = jnp.dot(
            kernels[tap_row],
            stacked[:, pl.ds(start, rows * width)],
            preferred_element_type=jnp.float32,
        )
        total = term if total is None else total + term
    return total


def forward_body(count, rows, *refs):
    pieces, rims, kernels = refs[:count], refs[count : 2 * count], refs[2 * count]
    outs = refs[2 * count + 1 : 3 * count + 1]
    factor, stacked = refs[3 * count + 1 :]
    height, depth, width = pieces[0].shape
    channels = count * depth
    step = pl.program_id(0)

    @pl.when(step == 0)
    def _():
        for j in range(count):
            place(stacked, j * depth, 0, rims[j][0], channels)
            place(stacked, j * depth, height + 1, rims[j][1], channels)

        def body(row, carry):
            for j in range(count):
                place(stacked, j * depth, row + 1, pieces[j][row], channels)
            return carry

        lax.fori_loop(0, height, body, 0)

    pre = taps(kernels, stacked, step * rows, rows, width)
    sigma = jax.nn.sigmoid(pre)
    activated = (pre * sigma).astype(jnp.bfloat16)
    slope = sigma * (1.0 + pre * (1.0 - sigma))
    for row in range(rows):
        lanes = slice(row * width, (row + 1) * width)
        factor[row] = slope[:, lanes]
        for j in range(count):
            outs[j][row] = activated[j * depth : (j + 1) * depth, lanes]


def whole(shape):
    return pl.BlockSpec(shape, lambda *_: (0,) * len(shape))


def forward(pieces, rims, kernels):
    count = len(pieces)
    height, depth, width = pieces[0].shape
    channels = count * depth
    rows = 4 if height % 4 == 0 else 1
    flops = 2 * 9 * channels * channels * height * width
    results = pl.pallas_call(
        functools.partial(forward_body, count, rows),
        grid=(height // rows,),
        in_specs=[whole(pieces[0].shape)] * count
        + [whole(rims[0].shape)] * count
        + [whole(kernels.shape)],
        out_specs=[pl.BlockSpec((rows, depth, width), lambda g: (g, 0, 0))] * count
        + [
            pl.BlockSpec((rows, channels, width), lambda g: (g, 0, 0)),
            whole((3 * channels, (height + 2) * width)),
        ],
        out_shape=[jax.ShapeDtypeStruct((height, depth, width), jnp.bfloat16)] * count
        + [
            jax.ShapeDtypeStruct((height, channels, width), jnp.float32),
            jax.ShapeDtypeStruct((3 * channels, (height + 2) * width), jnp.bfloat16),
        ],
        compiler_params=pltpu.CompilerParams(vmem_limit_bytes=VMEM_LIMIT),
        cost_estimate=pl.CostEstimate(
            flops=flops, bytes_accessed=16 * 1024 * 1024, transcendentals=0
        ),
        name="conv_forward",
    )(*pieces, *rims, kernels)
    return results[:count], results[count], results[count + 1]


def correlate_body(count, *refs):
    stacked, factor = refs[0], refs[1]
    pieces = refs[2 : 2 + count]
    grads, slope = refs[2 + count :]
    height, depth, width = pieces[0].shape
    channels = count * depth
    tap_row, tap_col = pl.program_id(0), pl.program_id(1)

    @pl.when((tap_row == 0) & (tap_col == 0))
    def _():
        def body(row, carry):
            lanes = pl.ds(pl.multiple_of(row * width, width), width)
            for j in range(count):
                part_of = pl.ds(j * depth, depth)
                value = pieces[j][row].astype(jnp.float32) * factor[row, part_of, :]
                slope[part_of, lanes] = value.astype(jnp.bfloat16)
            return carry

        lax.fori_loop(0, height, body, 0)

    source = stacked[
        pl.ds(pl.multiple_of(tap_col * channels, channels), channels),
        pl.ds(pl.multiple_of(tap_row * width, width), height * width),
    ]
    grads[0] = lax.dot_general(
        source, slope[...], (((1,), (1,)), ((), ())), preferred_element_type=jnp.float32
    )


def correlate(stacked, factor, pieces):
    count = len(pieces)
    height, depth, width = pieces[0].shape
    channels = count * depth
    flops = 2 * 9 * channels * channels * height * width
    return pl.pallas_call(
        functools.partial(correlate_body, count),
        grid=(3, 3),
        in_specs=[whole(stacked.shape), whole(factor.shape)] + [whole(pieces[0].shape)] * count,
        out_specs=[
            pl.BlockSpec((1, channels, channels), lambda a, b: (3 * a + b, 0, 0)),
            whole((channels, height * width)),
        ],
        out_shape=[
            jax.ShapeDtypeStruct((9, channels, channels), jnp.float32),
            jax.ShapeDtypeStruct((channels, height * width), jnp.bfloat16),
        ],
        compiler_params=pltpu.CompilerParams(vmem_limit_bytes=VMEM_LIMIT),
        cost_estimate=pl.CostEstimate(
            flops=flops, bytes_accessed=14 * 1024 * 1024, transcendentals=0
        ),
        name="kernel_grad",
    )(stacked, factor, *pieces)


def backward_body(count, rows, turns, slope, above, below, kernels, *refs):
    outs, stacked = refs[:count], refs[count]
    channels = slope.shape[0]
    _, _, width = above.shape
    height = slope.shape[1] // width
    depth = channels // count
    step = pl.program_id(0)

    @pl.when(step == 0)
    def _():
        for j in range(count):
            for side, rim, row in ((0, above, 0), (1, below, height + 1)):
                start = lax.rem(turns[side] + j, count) * depth
                block = rim[0, pl.ds(pl.multiple_of(start, depth), depth), :]
                place(stacked, j * depth, row, block, channels)

        def body(row, carry):
            lanes = pl.ds(pl.multiple_of(row * width, width), width)
            place(stacked, 0, row + 1, slope[:, lanes], channels)
            return carry

        lax.fori_loop(0, height, body, 0)

    grad = taps(kernels, stacked, step * rows, rows, width)
    for row in range(rows):
        lanes = slice(row * width, (row + 1) * width)
        for j in range(count):
            outs[j][row] = grad[j * depth : (j + 1) * depth, lanes].astype(outs[j].dtype)


def backward(turns, slope, above, below, kernels, count):
    channels = slope.shape[0]
    width = above.shape[2]
    height = slope.shape[1] // width
    depth = channels // count
    rows = 4 if height % 4 == 0 else 1
    flops = 2 * 9 * channels * channels * height * width
    return pl.pallas_call(
        functools.partial(backward_body, count, rows),
        grid=(height // rows,),
        in_specs=[
            pl.BlockSpec(memory_space=pltpu.SMEM),
            whole(slope.shape),
            whole(above.shape),
            whole(below.shape),
            whole(kernels.shape),
        ],
        out_specs=[pl.BlockSpec((rows, depth, width), lambda g: (g, 0, 0))] * count,
        out_shape=[
            jax.ShapeDtypeStruct((height, depth, width), jnp.bfloat16 if j else jnp.float32)
            for j in range(count)
        ],
        scratch_shapes=[pltpu.VMEM((3 * channels, (height + 2) * width), jnp.bfloat16)],
        compiler_params=pltpu.CompilerParams(vmem_limit_bytes=VMEM_LIMIT),
        cost_estimate=pl.CostEstimate(
            flops=flops, bytes_accessed=8 * 1024 * 1024, transcendentals=0
        ),
        name="conv_backward",
    )(turns, slope, above, below, kernels)


def gathered_kernel(kernel):
    dp, chan, row = (lax.axis_index(a) for a in ("dp", "chan", "row"))
    dps, chans, rows = (lax.axis_size(a) for a in ("dp", "chan", "row"))
    _, inner, outer = kernel.shape
    share = inner // rows
    mine = part(kernel, row, share, 1)
    mine = jnp.transpose(mine, (2, 0, 1)).reshape(outer, 9 * share)
    over_chan = jnp.concatenate([mine] + [receive(mine, "chan", j) for j in range(1, chans)], axis=0)
    over_dp = jnp.stack([over_chan] + [receive(over_chan, "dp", j) for j in range(1, dps)])
    over_row = jnp.stack([over_dp] + [receive(over_dp, "row", j) for j in range(1, rows)])
    placed = rotated(over_row, (rows - row) % rows, 0)
    placed = rotated(placed, (chan * (dps // chans) - dp) % dps, 1)
    channels = chans * outer
    taps_of = placed.reshape(rows, dps, channels, 3, 3, share)
    ahead = jnp.transpose(taps_of, (3, 2, 4, 1, 0, 5)).reshape(3, channels, 3 * channels)
    flipped = taps_of[:, :, :, ::-1, ::-1]
    back = jnp.transpose(flipped, (3, 1, 0, 5, 4, 2)).reshape(3, channels, 3 * channels)
    return ahead, back


def summed_kernel_grad(terms, inner, outer):
    dp, chan, row = (lax.axis_index(a) for a in ("dp", "chan", "row"))
    dps, chans, rows = (lax.axis_size(a) for a in ("dp", "chan", "row"))
    channels = terms.shape[1]
    share = inner // rows
    terms = terms.reshape(9, dps, rows, share, channels)

    def of_row(r):
        return lax.dynamic_index_in_dim(terms, r, 2, keepdims=False)

    halves = of_row(row)
    for j in range(1, rows):
        halves = halves + receive(of_row((row - j) % rows), "row", j)

    def of_dp(d):
        return lax.dynamic_index_in_dim(halves, (d - chan * (dps // chans)) % dps, 1, keepdims=False)

    total = of_dp(dp)
    for j in range(1, dps):
        total = total + receive(of_dp((dp - j) % dps), "dp", j)
    total = jnp.transpose(total, (2, 0, 1)).reshape(channels, 9 * share)
    own = total[:outer]
    for j in range(1, chans):
        own = own + receive(total[(chans - j) * outer : (chans - j + 1) * outer], "chan", j)
    both = jnp.stack([own] + [receive(own, "row", j) for j in range(1, rows)])
    both = rotated(both, (rows - row) % rows, 0).reshape(rows, outer, 9, share)
    return jnp.transpose(both, (2, 0, 3, 1)).reshape(9, inner, outer)


def shards(images, kernel, cotangent):
    row, chan = lax.axis_index("row"), lax.axis_index("chan")
    rows, chans = lax.axis_size("row"), lax.axis_size("chan")
    _, slab, depth, width = images.shape
    height = slab // chans
    images, cotangent = images[0], cotangent[0]

    def home(ahead):
        return home_of(row, (chan + ahead) % chans, chans)

    def to_homes(array, size):
        return [part(array, home(0), size, 0)] + [
            receive(part(array, home(-j), size, 0), "chan", j) for j in range(1, chans)
        ]

    ahead_kernel, back_kernel = gathered_kernel(kernel)
    pieces = to_homes(images, height)
    down = [(i, i + 1) for i in range(rows - 1)]
    up = [(i + 1, i) for i in range(rows - 1)]
    low = lax.ppermute(images[slab - 1 :], "row", down)
    high = lax.ppermute(images[:1], "row", up)
    tops = jnp.concatenate([low, images[height - 1 : slab - 1 : height]])
    bottoms = jnp.concatenate([images[height::height], high])
    rims = to_homes(jnp.stack([tops, bottoms], axis=1).reshape(2 * chans, depth, width), 2)
    cotangents = to_homes(cotangent, height)

    activated, factor, stacked = forward(pieces, rims, ahead_kernel)

    def edge(at):
        wide = jnp.concatenate([c[at] for c in cotangents]).astype(jnp.float32)
        return (wide * factor[at]).astype(jnp.bfloat16)[None]

    def snake(place_at):
        r, k = place_at // chans, place_at % chans
        return (k if r % 2 == 0 else chans - 1 - k) * rows + r

    line = [(snake(i), snake(i + 1)) for i in range(rows * chans - 1)]
    above = lax.ppermute(edge(height - 1), ("chan", "row"), line)
    below = lax.ppermute(edge(0), ("chan", "row"), [(b, a) for a, b in line])

    place_at = home(0)
    forth = jnp.where(row % 2 == 0, 1, chans - 1)
    turns = jnp.stack(
        [
            jnp.where(place_at == 0, 0, forth),
            jnp.where(place_at == chans - 1, 0, chans - forth),
        ]
    ).astype(jnp.int32)
    grads, slope = correlate(stacked, factor, cotangents)
    input_grads = backward(turns, slope, above, below, back_kernel, chans)
    kernel_grad = summed_kernel_grad(grads, kernel.shape[1], kernel.shape[2])

    def to_owners(blocks, dtype):
        out = jnp.zeros((slab, depth, width), dtype)
        for j in range(chans):
            arrived = receive(blocks[j], "chan", chans - j) if j else blocks[0]
            out = lax.dynamic_update_slice_in_dim(out, arrived.astype(dtype), home(-j) * height, 0)
        return out[None]

    return to_owners(activated, jnp.bfloat16), to_owners(input_grads, jnp.float32), kernel_grad


def solution(mesh):
    placed = (P("dp", "row", "chan", None), P(None, "dp", "chan"), P("dp", "row", "chan", None))
    return jax.shard_map(
        shards,
        mesh=mesh,
        in_specs=placed,
        out_specs=(
            P("dp", "row", "chan", None),
            P("dp", "row", "chan", None),
            P(None, "dp", "chan"),
        ),
        check_vma=False,
    )
```

```python
import functools

import jax
import jax.numpy as jnp
from jax import lax
from jax.experimental import pallas as pl
from jax.experimental.pallas import tpu as pltpu
from jax.sharding import PartitionSpec as P


VMEM_LIMIT = 36 * 1024 * 1024


def receive(block, axis, ahead):
    count = lax.axis_size(axis)
    return lax.ppermute(block, axis, [(i, (i - ahead) % count) for i in range(count)])


def home_of(row, chan, chans):
    return jnp.where(row % 2 == 0, chan, chans - 1 - chan)


def part(array, index, size, axis):
    return lax.dynamic_slice_in_dim(array, index * size, size, axis=axis)


def rotated(array, start, axis):
    twice = jnp.concatenate([array, array], axis=axis)
    return lax.dynamic_slice_in_dim(twice, start, array.shape[axis], axis=axis)


def columns_moved(block, step):
    width = block.shape[-1]
    lane = lax.broadcasted_iota(jnp.int32, block.shape, block.ndim - 1)
    if step < 0:
        moved = pltpu.roll(block, 1, block.ndim - 1)
        return jnp.where(lane == 0, jnp.zeros_like(block), moved)
    moved = pltpu.roll(block, width - 1, block.ndim - 1)
    return jnp.where(lane == width - 1, jnp.zeros_like(block), moved)


def place(stacked, channel, row, block, channels):
    depth, width = block.shape
    lanes = pl.ds(pl.multiple_of(row * width, width), width)
    wide = block.astype(jnp.float32)
    stacked[pl.ds(channel, depth), lanes] = columns_moved(wide, -1).astype(block.dtype)
    stacked[pl.ds(channels + channel, depth), lanes] = block
    stacked[pl.ds(2 * channels + channel, depth), lanes] = columns_moved(wide, 1).astype(block.dtype)


def taps(kernels, stacked, first, rows, width):
    total = None
    for tap_row in range(3):
        start = pl.multiple_of((first + tap_row) * width, width)
        term = jnp.dot(
            kernels[tap_row],
            stacked[:, pl.ds(start, rows * width)],
            preferred_element_type=jnp.float32,
        )
        total = term if total is None else total + term
    return total


def forward_body(count, rows, *refs):
    pieces, rims, ends = (refs[k * count : (k + 1) * count] for k in range(3))
    kernels = refs[3 * count]
    outs = refs[3 * count + 1 : 4 * count + 1]
    factor, stacked, first, last = refs[4 * count + 1 :]
    height, depth, width = pieces[0].shape
    channels = count * depth
    step = pl.program_id(0)

    @pl.when(step == 0)
    def _():
        for j in range(count):
            place(stacked, j * depth, 0, rims[j][0], channels)
            place(stacked, j * depth, height + 1, rims[j][1], channels)

        def body(row, carry):
            for j in range(count):
                place(stacked, j * depth, row + 1, pieces[j][row], channels)
            return carry

        lax.fori_loop(0, height, body, 0)

    pre = taps(kernels, stacked, step * rows, rows, width)
    sigma = jax.nn.sigmoid(pre)
    activated = (pre * sigma).astype(jnp.bfloat16)
    slope = sigma * (1.0 + pre * (1.0 - sigma))
    for row in range(rows):
        lanes = slice(row * width, (row + 1) * width)
        factor[row] = slope[:, lanes]
        for j in range(count):
            outs[j][row] = activated[j * depth : (j + 1) * depth, lanes]

    def end(out, side, row):
        for j in range(count):
            part_of = slice(j * depth, (j + 1) * depth)
            value = ends[j][side].astype(jnp.float32) * factor[row, part_of, :]
            out[0, part_of, :] = value.astype(jnp.bfloat16)

    @pl.when(step == 0)
    def _():
        end(first, 0, 0)

    @pl.when(step == pl.num_programs(0) - 1)
    def _():
        end(last, 1, rows - 1)


def whole(shape):
    return pl.BlockSpec(shape, lambda *_: (0,) * len(shape), pipeline_mode=pl.Buffered(1))


def forward(pieces, rims, ends, kernels):
    count = len(pieces)
    height, depth, width = pieces[0].shape
    channels = count * depth
    rows = 4 if height % 4 == 0 else 1
    flops = 2 * 9 * channels * channels * height * width
    call = pl.pallas_call(
        functools.partial(forward_body, count, rows),
        grid=(height // rows,),
        in_specs=[whole(pieces[0].shape)] * count
        + [whole(rims[0].shape)] * count
        + [whole(ends[0].shape)] * count
        + [whole(kernels.shape)],
        out_specs=[pl.BlockSpec((rows, depth, width), lambda g: (g, 0, 0))] * count
        + [
            pl.BlockSpec((rows, channels, width), lambda g: (g, 0, 0)),
            whole((3 * channels, (height + 2) * width)),
            whole((1, channels, width)),
            whole((1, channels, width)),
        ],
        out_shape=[jax.ShapeDtypeStruct((height, depth, width), jnp.bfloat16)] * count
        + [
            jax.ShapeDtypeStruct((height, channels, width), jnp.float32),
            jax.ShapeDtypeStruct((3 * channels, (height + 2) * width), jnp.bfloat16),
            jax.ShapeDtypeStruct((1, channels, width), jnp.bfloat16),
            jax.ShapeDtypeStruct((1, channels, width), jnp.bfloat16),
        ],
        compiler_params=pltpu.CompilerParams(vmem_limit_bytes=VMEM_LIMIT),
        cost_estimate=pl.CostEstimate(
            flops=flops, bytes_accessed=16 * 1024 * 1024, transcendentals=0
        ),
        name="conv_forward",
    )
    results = call(*pieces, *rims, *ends, kernels)
    return results[:count], *results[count:]


def correlate_body(count, groups, rows, turn, stacked, factor, *refs):
    pieces, ends = refs[:count], refs[count : 2 * count]
    shares, slope = refs[2 * count : -1], refs[-1]
    height, depth, width = factor.shape[0], pieces[0].shape[1], factor.shape[2]
    channels = count * depth
    tap_row, tap_col = pl.program_id(0), pl.program_id(1)

    @pl.when((tap_row == 0) & (tap_col == 0))
    def _():
        def put(row, blocks):
            lanes = pl.ds(pl.multiple_of(row * width, width), width)
            for j in range(count):
                part_of = pl.ds(j * depth, depth)
                value = blocks[j].astype(jnp.float32) * factor[row, part_of, :]
                slope[part_of, lanes] = value.astype(jnp.bfloat16)

        def body(row, carry):
            put(row + 1, [piece[row] for piece in pieces])
            return carry

        put(0, [end[0] for end in ends])
        lax.fori_loop(0, height - 2, body, 0)
        put(height - 1, [end[1] for end in ends])

    source = stacked[
        pl.ds(pl.multiple_of(tap_col * channels, channels), channels),
        pl.ds(pl.multiple_of(tap_row * width, width), height * width),
    ]
    grads = lax.dot_general(
        source, slope[...], (((1,), (1,)), ((), ())), preferred_element_type=jnp.float32
    )
    size = channels // (groups * rows)
    for own in range(rows):

        @pl.when(turn[0] == own)
        def _():
            for j in range(rows):
                for group in range(groups):
                    start = (group * rows + (own - j) % rows) * size
                    shares[j][0, group] = grads[start : start + size]


def correlate(stacked, factor, pieces, ends):
    count = len(pieces)
    height, channels, width = factor.shape
    groups, rows = lax.axis_size("dp"), lax.axis_size("row")
    size = channels // (groups * rows)
    flops = 2 * 9 * channels * channels * height * width
    call = pl.pallas_call(
        functools.partial(correlate_body, count, groups, rows),
        grid=(3, 3),
        in_specs=[pl.BlockSpec(memory_space=pltpu.SMEM)]
        + [whole(stacked.shape), whole(factor.shape)]
        + [whole(pieces[0].shape)] * count
        + [whole(ends[0].shape)] * count,
        out_specs=[pl.BlockSpec((1, groups, size, channels), lambda a, b: (3 * a + b, 0, 0, 0))]
        * rows
        + [whole((channels, height * width))],
        out_shape=[jax.ShapeDtypeStruct((9, groups, size, channels), jnp.float32)] * rows
        + [jax.ShapeDtypeStruct((channels, height * width), jnp.bfloat16)],
        compiler_params=pltpu.CompilerParams(vmem_limit_bytes=VMEM_LIMIT),
        cost_estimate=pl.CostEstimate(
            flops=flops, bytes_accessed=14 * 1024 * 1024, transcendentals=0
        ),
        name="kernel_grad",
    )
    turn = lax.axis_index("row").astype(jnp.int32)[None]
    results = call(turn, stacked, factor, *pieces, *ends)
    return results[:-1], results[-1]


def backward_body(count, rows, turns, slope, above, below, kernels, *refs):
    outs, stacked = refs[:count], refs[count]
    channels = slope.shape[0]
    _, _, width = above.shape
    height = slope.shape[1] // width
    depth = channels // count
    step = pl.program_id(0)

    @pl.when(step == 0)
    def _():
        for j in range(count):
            for side, rim, row in ((0, above, 0), (1, below, height + 1)):
                start = lax.rem(turns[side] + j, count) * depth
                block = rim[0, pl.ds(pl.multiple_of(start, depth), depth), :]
                place(stacked, j * depth, row, block, channels)

        def body(row, carry):
            lanes = pl.ds(pl.multiple_of(row * width, width), width)
            place(stacked, 0, row + 1, slope[:, lanes], channels)
            return carry

        lax.fori_loop(0, height, body, 0)

    grad = taps(kernels, stacked, step * rows, rows, width)
    for row in range(rows):
        lanes = slice(row * width, (row + 1) * width)
        for j in range(count):
            outs[j][row] = grad[j * depth : (j + 1) * depth, lanes].astype(outs[j].dtype)


def backward(turns, slope, above, below, kernels, count):
    channels = slope.shape[0]
    width = above.shape[2]
    height = slope.shape[1] // width
    depth = channels // count
    rows = 4 if height % 4 == 0 else 1
    flops = 2 * 9 * channels * channels * height * width
    return pl.pallas_call(
        functools.partial(backward_body, count, rows),
        grid=(height // rows,),
        in_specs=[
            pl.BlockSpec(memory_space=pltpu.SMEM),
            whole(slope.shape),
            whole(above.shape),
            whole(below.shape),
            whole(kernels.shape),
        ],
        out_specs=[pl.BlockSpec((rows, depth, width), lambda g: (g, 0, 0))] * count,
        out_shape=[
            jax.ShapeDtypeStruct((height, depth, width), jnp.bfloat16 if j else jnp.float32)
            for j in range(count)
        ],
        scratch_shapes=[pltpu.VMEM((3 * channels, (height + 2) * width), jnp.bfloat16)],
        compiler_params=pltpu.CompilerParams(vmem_limit_bytes=VMEM_LIMIT),
        cost_estimate=pl.CostEstimate(
            flops=flops, bytes_accessed=8 * 1024 * 1024, transcendentals=0
        ),
        name="conv_backward",
    )(turns, slope, above, below, kernels)


def gathered_kernel(kernel):
    dp, chan, row = (lax.axis_index(a) for a in ("dp", "chan", "row"))
    dps, chans, rows = (lax.axis_size(a) for a in ("dp", "chan", "row"))
    _, inner, outer = kernel.shape
    share = inner // rows
    mine = part(kernel, row, share, 1)
    mine = jnp.transpose(mine, (2, 0, 1)).reshape(outer, 9 * share)
    over_chan = jnp.concatenate([mine] + [receive(mine, "chan", j) for j in range(1, chans)], axis=0)
    over_dp = jnp.stack([over_chan] + [receive(over_chan, "dp", j) for j in range(1, dps)])
    over_row = jnp.stack([over_dp] + [receive(over_dp, "row", j) for j in range(1, rows)])
    placed = rotated(over_row, (rows - row) % rows, 0)
    placed = rotated(placed, (chan * (dps // chans) - dp) % dps, 1)
    channels = chans * outer
    taps_of = placed.reshape(rows, dps, channels, 3, 3, share)
    return taps_of


def ahead_order(taps_of):
    channels = taps_of.shape[2]
    return jnp.transpose(taps_of, (3, 2, 4, 1, 0, 5)).reshape(3, channels, 3 * channels)


def back_order(taps_of):
    channels = taps_of.shape[2]
    flipped = taps_of[:, :, :, ::-1, ::-1]
    return jnp.transpose(flipped, (3, 1, 0, 5, 4, 2)).reshape(3, channels, 3 * channels)


def summed_kernel_grad(shares, inner, outer):
    dp, chan, row = (lax.axis_index(a) for a in ("dp", "chan", "row"))
    dps, chans, rows = (lax.axis_size(a) for a in ("dp", "chan", "row"))
    channels = shares[0].shape[3]
    share = inner // rows
    halves = shares[0]
    for j in range(1, rows):
        halves = halves + receive(shares[j], "row", j)

    def of_dp(d):
        at = (d - chan * (dps // chans)) % dps
        return lax.dynamic_index_in_dim(halves, at, 1, keepdims=False)

    total = of_dp(dp)
    for j in range(1, dps):
        total = total + receive(of_dp((dp - j) % dps), "dp", j)
    total = jnp.transpose(total, (2, 0, 1)).reshape(channels, 9 * share)
    own = total[:outer]
    for j in range(1, chans):
        start = (chans - j) * outer
        own = own + receive(total[start : start + outer], "chan", j)
    both = jnp.stack([own] + [receive(own, "row", j) for j in range(1, rows)])
    both = rotated(both, (rows - row) % rows, 0).reshape(rows, outer, 9, share)
    return jnp.transpose(both, (2, 0, 3, 1)).reshape(9, inner, outer)


def shards(images, kernel, cotangent):
    row, chan = lax.axis_index("row"), lax.axis_index("chan")
    rows, chans = lax.axis_size("row"), lax.axis_size("chan")
    _, slab, depth, width = images.shape
    height = slab // chans
    images, cotangent = images[0], cotangent[0]

    def home(ahead):
        return home_of(row, (chan + ahead) % chans, chans)

    def to_homes(array, size):
        return [part(array, home(0), size, 0)] + [
            receive(part(array, home(-j), size, 0), "chan", j) for j in range(1, chans)
        ]

    taps_of = gathered_kernel(kernel)
    pieces = to_homes(images, height)
    down = [(i, i + 1) for i in range(rows - 1)]
    up = [(i + 1, i) for i in range(rows - 1)]
    low = lax.ppermute(images[slab - 1 :], "row", down)
    high = lax.ppermute(images[:1], "row", up)
    tops = jnp.concatenate([low, images[height - 1 : slab - 1 : height]])
    bottoms = jnp.concatenate([images[height::height], high])
    rims = jnp.stack([tops, bottoms], axis=1).reshape(2 * chans, depth, width)
    rims = to_homes(rims, 2)
    firsts, lasts = cotangent[::height], cotangent[height - 1 :: height]
    ends = jnp.stack([firsts, lasts], axis=1).reshape(2 * chans, depth, width)
    ends = to_homes(ends, 2)
    inside = cotangent.reshape(chans, height, depth, width)[:, 1:-1]
    inside = inside.reshape(slab - 2 * chans, depth, width)
    cotangents = to_homes(inside, height - 2)

    results = forward(pieces, rims, ends, ahead_order(taps_of))
    activated, factor, stacked, first, last = results
    taps_of, factor = lax.optimization_barrier((taps_of, factor))
    back_kernel = back_order(taps_of)

    def snake(place_at):
        r, k = place_at // chans, place_at % chans
        return (k if r % 2 == 0 else chans - 1 - k) * rows + r

    line = [(snake(i), snake(i + 1)) for i in range(rows * chans - 1)]
    above = lax.ppermute(last, ("chan", "row"), line)
    below = lax.ppermute(first, ("chan", "row"), [(b, a) for a, b in line])

    place_at = home(0)
    forth = jnp.where(row % 2 == 0, 1, chans - 1)
    turns = jnp.stack(
        [
            jnp.where(place_at == 0, 0, forth),
            jnp.where(place_at == chans - 1, 0, chans - forth),
        ]
    ).astype(jnp.int32)
    grads, slope = correlate(stacked, factor, cotangents, ends)
    input_grads = backward(turns, slope, above, below, back_kernel, chans)
    kernel_grad = summed_kernel_grad(grads, kernel.shape[1], kernel.shape[2])

    def to_owners(blocks, dtype):
        out = jnp.zeros((slab, depth, width), dtype)
        for j in range(chans):
            arrived = receive(blocks[j], "chan", chans - j) if j else blocks[0]
            out = lax.dynamic_update_slice_in_dim(out, arrived.astype(dtype), home(-j) * height, 0)
        return out[None]

    return to_owners(activated, jnp.bfloat16), to_owners(input_grads, jnp.float32), kernel_grad


def solution(mesh):
    placed = (P("dp", "row", "chan", None), P(None, "dp", "chan"), P("dp", "row", "chan", None))
    return jax.shard_map(
        shards,
        mesh=mesh,
        in_specs=placed,
        out_specs=(
            P("dp", "row", "chan", None),
            P("dp", "row", "chan", None),
            P(None, "dp", "chan"),
        ),
        check_vma=False,
    )
```

```python
import functools

import jax
import jax.numpy as jnp
from jax import lax
from jax.experimental import pallas as pl
from jax.experimental.pallas import tpu as pltpu
from jax.sharding import PartitionSpec as P


VMEM_LIMIT = 60 * 1024 * 1024


def receive(block, axis, ahead):
    count = lax.axis_size(axis)
    return lax.ppermute(block, axis, [(i, (i - ahead) % count) for i in range(count)])


def home_of(row, chan, chans):
    return jnp.where(row % 2 == 0, chan, chans - 1 - chan)


def part(array, index, size, axis):
    return lax.dynamic_slice_in_dim(array, index * size, size, axis=axis)


def rotated(array, start, axis):
    twice = jnp.concatenate([array, array], axis=axis)
    return lax.dynamic_slice_in_dim(twice, start, array.shape[axis], axis=axis)


def stacking_base():
    matched = lax.axis_size("dp") == lax.axis_size("chan")
    return lax.axis_index("dp") if matched else jnp.int32(0)


def columns_moved(block, step):
    width = block.shape[-1]
    lane = lax.broadcasted_iota(jnp.int32, block.shape, block.ndim - 1)
    if step < 0:
        moved = pltpu.roll(block, 1, block.ndim - 1)
        return jnp.where(lane == 0, jnp.zeros_like(block), moved)
    moved = pltpu.roll(block, width - 1, block.ndim - 1)
    return jnp.where(lane == width - 1, jnp.zeros_like(block), moved)


def place(stacked, channel, row, block, channels):
    depth, width = block.shape
    lanes = pl.ds(pl.multiple_of(row * width, width), width)
    wide = block.astype(jnp.float32)

    def below(copies):
        start = copies * channels + channel
        return pl.ds(start if isinstance(channel, int) else pl.multiple_of(start, 16), depth)

    stacked[below(0), lanes] = columns_moved(wide, -1).astype(block.dtype)
    stacked[below(1), lanes] = block
    stacked[below(2), lanes] = columns_moved(wide, 1).astype(block.dtype)


def window(stacked, tap_row, tap_col, channel, depth, first, rows, width, channels):
    start = pl.multiple_of((first + tap_row) * width, width)
    return stacked[tap_col * channels + channel : tap_col * channels + channel + depth, pl.ds(start, rows * width)]


def forward_taps(halves, stacked, first, rows, width):
    count = halves[0].shape[0]
    depth = halves[0].shape[2] // 9
    total = None
    for block in range(count):
        windows = [
            window(stacked, a, b, block * depth, depth, first, rows, width, count * depth)
            for a in range(3)
            for b in range(3)
        ]
        term = jnp.dot(
            jnp.concatenate([half[block] for half in halves]),
            jnp.concatenate(windows),
            preferred_element_type=jnp.float32,
        )
        total = term if total is None else total + term
    return total


def forward_body(count, shares, rows, turns, *refs):
    pieces, rims = refs[:count], refs[count : 2 * count]
    halves = refs[2 * count : 2 * count + shares]
    outs = refs[2 * count + shares : 3 * count + shares]
    factor, stacked, first, last = refs[3 * count + shares :]
    height, depth, width = pieces[0].shape
    channels = count * depth
    step = pl.program_id(0)

    @pl.when(step == 0)
    def _():
        slots = [lax.rem(turns[0] + j, count) * depth for j in range(count)]
        for j in range(count):
            place(stacked, slots[j], 0, rims[j][0], channels)
            place(stacked, slots[j], height + 1, rims[j][1], channels)

        def body(row, carry):
            for j in range(count):
                place(stacked, slots[j], row + 1, pieces[j][row], channels)
            return carry

        lax.fori_loop(0, height, body, 0)

    mixed = forward_taps(halves, stacked, step * rows, rows, width)
    size = depth // shares
    for j in range(count):
        parts = []
        for share in range(shares):
            chosen = None
            for at in range(shares):
                start = at * count * size + j * size
                value = mixed[start : start + size]
                here = turns[1] == (share - at) % shares
                chosen = value if chosen is None else jnp.where(here, value, chosen)
            parts.append(chosen)
        pre = jnp.concatenate(parts) if shares > 1 else parts[0]
        sigma = jax.nn.sigmoid(pre)
        activated = (pre * sigma).astype(jnp.bfloat16)
        slope = sigma * (1.0 + pre * (1.0 - sigma))
        for row in range(rows):
            lanes = slice(row * width, (row + 1) * width)
            factor[row, j * depth : (j + 1) * depth, :] = slope[:, lanes]
            outs[j][row] = activated[:, lanes]

    def end(out, side, row):
        for j in range(count):
            part_of = slice(j * depth, (j + 1) * depth)
            value = rims[j][side].astype(jnp.float32) * factor[row, part_of, :]
            out[0, part_of, :] = value.astype(jnp.bfloat16)

    @pl.when(step == 0)
    def _():
        end(first, 2, 0)

    @pl.when(step == pl.num_programs(0) - 1)
    def _():
        end(last, 3, rows - 1)


def whole(shape):
    return pl.BlockSpec(shape, lambda *_: (0,) * len(shape), pipeline_mode=pl.Buffered(1))


def forward(turns, pieces, rims, halves):
    count = len(pieces)
    height, depth, width = pieces[0].shape
    channels = count * depth
    rows = 4 if height % 4 == 0 else 1
    flops = 2 * 9 * channels * channels * height * width
    call = pl.pallas_call(
        functools.partial(forward_body, count, len(halves), rows),
        grid=(height // rows,),
        in_specs=[pl.BlockSpec(memory_space=pltpu.SMEM)]
        + [whole(pieces[0].shape)] * count
        + [whole(rims[0].shape)] * count
        + [whole(halves[0].shape)] * len(halves),
        out_specs=[pl.BlockSpec((rows, depth, width), lambda g: (g, 0, 0))] * count
        + [
            pl.BlockSpec((rows, channels, width), lambda g: (g, 0, 0)),
            whole((3 * channels, (height + 2) * width)),
            whole((1, channels, width)),
            whole((1, channels, width)),
        ],
        out_shape=[jax.ShapeDtypeStruct((height, depth, width), jnp.bfloat16)] * count
        + [
            jax.ShapeDtypeStruct((height, channels, width), jnp.float32),
            jax.ShapeDtypeStruct((3 * channels, (height + 2) * width), jnp.bfloat16),
            jax.ShapeDtypeStruct((1, channels, width), jnp.bfloat16),
            jax.ShapeDtypeStruct((1, channels, width), jnp.bfloat16),
        ],
        compiler_params=pltpu.CompilerParams(vmem_limit_bytes=VMEM_LIMIT),
        cost_estimate=pl.CostEstimate(
            flops=flops, bytes_accessed=16 * 1024 * 1024, transcendentals=0
        ),
        name="conv_forward",
    )
    results = call(turns, *pieces, *rims, *halves)
    return results[:count], *results[count:]


def correlate_body(count, groups, rows, turn, stacked, factor, *refs):
    pieces, ends = refs[:count], refs[count : 2 * count]
    shares, slope = refs[2 * count : -1], refs[-1]
    height, depth, width = factor.shape[0], pieces[0].shape[1], factor.shape[2]
    channels = count * depth
    tap_row, tap_col = pl.program_id(0), pl.program_id(1)

    @pl.when((tap_row == 0) & (tap_col == 0))
    def _():
        def put(row, blocks):
            lanes = pl.ds(pl.multiple_of(row * width, width), width)
            for j in range(count):
                part_of = pl.ds(j * depth, depth)
                value = blocks[j].astype(jnp.float32) * factor[row, part_of, :]
                slope[part_of, lanes] = value.astype(jnp.bfloat16)

        def body(row, carry):
            put(row + 1, [piece[row] for piece in pieces])
            return carry

        put(0, [end[2] for end in ends])
        lax.fori_loop(0, height - 2, body, 0)
        put(height - 1, [end[3] for end in ends])

    source = stacked[
        pl.ds(pl.multiple_of(tap_col * channels, channels), channels),
        pl.ds(pl.multiple_of(tap_row * width, width), height * width),
    ]
    grads = lax.dot_general(
        source, slope[...], (((1,), (1,)), ((), ())), preferred_element_type=jnp.float32
    )
    size = channels // (groups * rows)
    for own in range(rows):

        @pl.when(turn[0] == own)
        def _():
            for j in range(rows):
                for group in range(groups):
                    start = (group * rows + (own - j) % rows) * size
                    shares[j][group, 0] = grads[start : start + size]


def correlate(stacked, factor, pieces, ends):
    count = len(pieces)
    height, channels, width = factor.shape
    groups, rows = lax.axis_size("dp"), lax.axis_size("row")
    size = channels // (groups * rows)
    flops = 2 * 9 * channels * channels * height * width
    call = pl.pallas_call(
        functools.partial(correlate_body, count, groups, rows),
        grid=(3, 3),
        in_specs=[pl.BlockSpec(memory_space=pltpu.SMEM)]
        + [whole(stacked.shape), whole(factor.shape)]
        + [whole(pieces[0].shape)] * count
        + [whole(ends[0].shape)] * count,
        out_specs=[pl.BlockSpec((groups, 1, size, channels), lambda a, b: (0, 3 * a + b, 0, 0))]
        * rows
        + [whole((channels, height * width))],
        out_shape=[jax.ShapeDtypeStruct((groups, 9, size, channels), jnp.float32)] * rows
        + [jax.ShapeDtypeStruct((channels, height * width), jnp.bfloat16)],
        compiler_params=pltpu.CompilerParams(vmem_limit_bytes=VMEM_LIMIT),
        cost_estimate=pl.CostEstimate(
            flops=flops, bytes_accessed=14 * 1024 * 1024, transcendentals=0
        ),
        name="kernel_grad",
    )
    turn = lax.axis_index("row").astype(jnp.int32)[None]
    results = call(turn, stacked, factor, *pieces, *ends)
    return results[:-1], results[-1]


def backward_body(count, rows, turns, slope, above, below, kernels, *refs):
    outs, stacked = refs[:count], refs[count]
    channels = slope.shape[0]
    _, _, width = above.shape
    height = slope.shape[1] // width
    depth = channels // count
    step = pl.program_id(0)

    @pl.when(step == 0)
    def _():
        for j in range(count):
            for side, rim, row in ((0, above, 0), (1, below, height + 1)):
                start = lax.rem(turns[side] + j, count) * depth
                block = rim[0, pl.ds(pl.multiple_of(start, depth), depth), :]
                place(stacked, j * depth, row, block, channels)

        def body(row, carry):
            lanes = pl.ds(pl.multiple_of(row * width, width), width)
            place(stacked, 0, row + 1, slope[:, lanes], channels)
            return carry

        lax.fori_loop(0, height, body, 0)

    windows = [
        window(stacked, tap_row, 0, 0, 3 * channels, step * rows, rows, width, channels)
        for tap_row in range(3)
    ]
    order = [kernels[lax.rem(turns[2] + j, count)] for j in range(count)]
    grad = jnp.dot(
        jnp.concatenate(order), jnp.concatenate(windows), preferred_element_type=jnp.float32
    )
    for row in range(rows):
        lanes = slice(row * width, (row + 1) * width)
        for j in range(count):
            outs[j][row] = grad[j * depth : (j + 1) * depth, lanes].astype(outs[j].dtype)


def backward(turns, slope, above, below, kernels, count):
    channels = slope.shape[0]
    width = above.shape[2]
    height = slope.shape[1] // width
    depth = channels // count
    rows = 4 if height % 4 == 0 else 1
    flops = 2 * 9 * channels * channels * height * width
    return pl.pallas_call(
        functools.partial(backward_body, count, rows),
        grid=(height // rows,),
        in_specs=[
            pl.BlockSpec(memory_space=pltpu.SMEM),
            whole(slope.shape),
            whole(above.shape),
            whole(below.shape),
            whole(kernels.shape),
        ],
        out_specs=[pl.BlockSpec((rows, depth, width), lambda g: (g, 0, 0))] * count,
        out_shape=[
            jax.ShapeDtypeStruct((height, depth, width), jnp.bfloat16 if j else jnp.float32)
            for j in range(count)
        ],
        scratch_shapes=[pltpu.VMEM((3 * channels, (height + 2) * width), jnp.bfloat16)],
        compiler_params=pltpu.CompilerParams(vmem_limit_bytes=VMEM_LIMIT),
        cost_estimate=pl.CostEstimate(
            flops=flops, bytes_accessed=8 * 1024 * 1024, transcendentals=0
        ),
        name="conv_backward",
    )(turns, slope, above, below, kernels)


def gathered_kernel(kernel):
    dp, row = lax.axis_index("dp"), lax.axis_index("row")
    dps, chans, rows = (lax.axis_size(a) for a in ("dp", "chan", "row"))
    _, inner, outer = kernel.shape
    size = outer // rows
    mine = part(kernel, row, size, 2)
    mine = jnp.transpose(mine, (2, 0, 1)).reshape(size, 9 * inner)
    over_chan = jnp.concatenate([mine] + [receive(mine, "chan", j) for j in range(1, chans)], axis=0)
    over_dp = jnp.stack([over_chan] + [receive(over_chan, "dp", j) for j in range(1, dps)])
    if dps != chans:
        each = dps // chans
        over_dp = rotated(over_dp, (dps - dp) % dps, 0)
        over_dp = over_dp.reshape(chans, each, chans * size, 9, inner)
        over_dp = jnp.transpose(over_dp, (0, 2, 3, 1, 4)).reshape(chans, chans * size, 9 * each * inner)
    return [over_dp] + [receive(over_dp, "row", j) for j in range(1, rows)]


def back_order(halves):
    row, rows = lax.axis_index("row"), lax.axis_size("row")
    chans = lax.axis_size("chan")
    both = rotated(jnp.stack(halves), (rows - row) % rows, 0)
    _, blocks, outs, depth = both.shape
    inner = depth // 9
    both = both.reshape(rows, blocks, chans, outs // chans, 9, inner)[:, :, :, :, ::-1]
    return jnp.transpose(both, (1, 5, 4, 2, 0, 3)).reshape(blocks, inner, 9 * outs * rows)


def summed_kernel_grad(shares, inner, outer):
    dp, row = lax.axis_index("dp"), lax.axis_index("row")
    dps, chans, rows = (lax.axis_size(a) for a in ("dp", "chan", "row"))
    channels = shares[0].shape[3]
    share = inner // rows
    halves = shares[0]
    for j in range(1, rows):
        halves = halves + receive(shares[j], "row", j)

    def of_dp(ahead):
        if dps == chans:
            return halves[ahead % dps]
        return lax.dynamic_index_in_dim(halves, (dp + ahead) % dps, 0, keepdims=False)

    total = of_dp(0)
    for j in range(1, dps):
        total = total + receive(of_dp(-j), "dp", j)
    total = jnp.transpose(total, (2, 0, 1)).reshape(channels, 9 * share)
    own = total[:outer]
    for j in range(1, chans):
        start = (chans - j) * outer
        own = own + receive(total[start : start + outer], "chan", j)
    both = jnp.stack([own] + [receive(own, "row", j) for j in range(1, rows)])
    both = rotated(both, (rows - row) % rows, 0).reshape(rows, outer, 9, share)
    return jnp.transpose(both, (2, 0, 3, 1)).reshape(9, inner, outer)


def shards(images, kernel, cotangent):
    row, chan = lax.axis_index("row"), lax.axis_index("chan")
    rows, chans = lax.axis_size("row"), lax.axis_size("chan")
    _, slab, depth, width = images.shape
    height = slab // chans
    images, cotangent = images[0], cotangent[0]

    def home(ahead):
        return home_of(row, (chan + ahead) % chans, chans)

    def to_homes(array, size):
        return [part(array, home(0), size, 0)] + [
            receive(part(array, home(-j), size, 0), "chan", j) for j in range(1, chans)
        ]

    halves = gathered_kernel(kernel)
    pieces = to_homes(images, height)
    if rows == 2:
        edge = jnp.where(row == 0, images[slab - 1 :], images[:1])
        edge = receive(edge, "row", 1)
        low = jnp.where(row == 0, jnp.zeros_like(edge), edge)
        high = jnp.where(row == 0, edge, jnp.zeros_like(edge))
    else:
        low = lax.ppermute(images[slab - 1 :], "row", [(i, i + 1) for i in range(rows - 1)])
        high = lax.ppermute(images[:1], "row", [(i + 1, i) for i in range(rows - 1)])

    def rim_of(at):
        begin = at * height
        above = part(images, jnp.maximum(begin - 1, 0), 1, 0)
        below = part(images, jnp.minimum(begin + height, slab - 1), 1, 0)
        return jnp.concatenate(
            [
                jnp.where(at == 0, low, above),
                jnp.where(at == chans - 1, high, below),
                part(cotangent, begin, 1, 0),
                part(cotangent, begin + height - 1, 1, 0),
            ]
        )

    rims = [rim_of(home(0))]
    rims += [receive(rim_of(home(-j)), "chan", j) for j in range(1, chans)]

    def inside(ahead):
        return lax.dynamic_slice_in_dim(cotangent, home(ahead) * height + 1, height - 2, 0)

    cotangents = [inside(0)] + [receive(inside(-j), "chan", j) for j in range(1, chans)]

    shift = (chan - stacking_base()) % chans
    place_at = home(0)
    forth = jnp.where(row % 2 == 0, 1, chans - 1)
    above_turn = jnp.where(place_at == 0, 0, forth)
    below_turn = jnp.where(place_at == chans - 1, 0, chans - forth)
    turns = jnp.stack([shift, row]).astype(jnp.int32)
    back_turns = jnp.stack([above_turn, below_turn, shift]).astype(jnp.int32)

    results = forward(turns, pieces, rims, halves)
    activated, factor, stacked, first, last = results
    halves, factor = lax.optimization_barrier((halves, factor))
    back_kernel = back_order(halves)

    def snake(place_at):
        r, k = place_at // chans, place_at % chans
        return (k if r % 2 == 0 else chans - 1 - k) * rows + r

    line = [(snake(i), snake(i + 1)) for i in range(rows * chans - 1)]
    above = lax.ppermute(last, ("chan", "row"), line)
    below = lax.ppermute(first, ("chan", "row"), [(b, a) for a, b in line])

    grads, slope = correlate(stacked, factor, cotangents, rims)
    input_grads = backward(back_turns, slope, above, below, back_kernel, chans)
    kernel_grad = summed_kernel_grad(grads, kernel.shape[1], kernel.shape[2])

    def to_owners(blocks, dtype):
        out = jnp.zeros((slab, depth, width), dtype)
        for j in range(chans):
            arrived = receive(blocks[j], "chan", chans - j) if j else blocks[0]
            out = lax.dynamic_update_slice_in_dim(out, arrived.astype(dtype), home(-j) * height, 0)
        return out[None]

    return to_owners(activated, jnp.bfloat16), to_owners(input_grads, jnp.float32), kernel_grad


def solution(mesh):
    placed = (P("dp", "row", "chan", None), P(None, "dp", "chan"), P("dp", "row", "chan", None))
    return jax.shard_map(
        shards,
        mesh=mesh,
        in_specs=placed,
        out_specs=(
            P("dp", "row", "chan", None),
            P("dp", "row", "chan", None),
            P(None, "dp", "chan"),
        ),
        check_vma=False,
    )
```

```python
import functools

import jax
import jax.numpy as jnp
from jax import lax
from jax.experimental import pallas as pl
from jax.experimental.pallas import tpu as pltpu
from jax.sharding import PartitionSpec as P


VMEM_LIMIT = 60 * 1024 * 1024


def receive(block, axis, ahead):
    count = lax.axis_size(axis)
    return lax.ppermute(block, axis, [(i, (i - ahead) % count) for i in range(count)])


def home_of(row, chan, chans):
    return jnp.where(row % 2 == 0, chan, chans - 1 - chan)


def part(array, index, size, axis):
    return lax.dynamic_slice_in_dim(array, index * size, size, axis=axis)


def rotated(array, start, axis):
    twice = jnp.concatenate([array, array], axis=axis)
    return lax.dynamic_slice_in_dim(twice, start, array.shape[axis], axis=axis)


def stacking_base():
    matched = lax.axis_size("dp") == lax.axis_size("chan")
    return lax.axis_index("dp") if matched else jnp.int32(0)


def columns_moved(block, step):
    width = block.shape[-1]
    lane = lax.broadcasted_iota(jnp.int32, block.shape, block.ndim - 1)
    if step < 0:
        moved = pltpu.roll(block, 1, block.ndim - 1)
        return jnp.where(lane == 0, jnp.zeros_like(block), moved)
    moved = pltpu.roll(block, width - 1, block.ndim - 1)
    return jnp.where(lane == width - 1, jnp.zeros_like(block), moved)


def place(stacked, channel, row, block, channels):
    depth, width = block.shape
    lanes = pl.ds(pl.multiple_of(row * width, width), width)
    wide = block.astype(jnp.float32)

    def below(copies):
        start = copies * channels + channel
        return pl.ds(start if isinstance(channel, int) else pl.multiple_of(start, 16), depth)

    stacked[below(0), lanes] = columns_moved(wide, -1).astype(block.dtype)
    stacked[below(1), lanes] = block
    stacked[below(2), lanes] = columns_moved(wide, 1).astype(block.dtype)


def window(stacked, tap_row, tap_col, channel, depth, first, rows, width, channels):
    start = pl.multiple_of((first + tap_row) * width, width)
    return stacked[tap_col * channels + channel : tap_col * channels + channel + depth, pl.ds(start, rows * width)]


def forward_taps(halves, stacked, first, rows, width):
    count = halves[0].shape[0]
    depth = halves[0].shape[2] // 9
    total = None
    for block in range(count):
        windows = [
            window(stacked, a, b, block * depth, depth, first, rows, width, count * depth)
            for a in range(3)
            for b in range(3)
        ]
        term = jnp.dot(
            jnp.concatenate([half[block] for half in halves]),
            jnp.concatenate(windows),
            preferred_element_type=jnp.float32,
        )
        total = term if total is None else total + term
    return total


def forward_body(count, shares, rows, turns, *refs):
    pieces, rims = refs[:count], refs[count : 2 * count]
    halves = refs[2 * count : 2 * count + shares]
    outs = refs[2 * count + shares : 3 * count + shares]
    factor, stacked, first, last = refs[3 * count + shares :]
    height, depth, width = pieces[0].shape
    channels = count * depth
    step = pl.program_id(0)

    @pl.when(step == 0)
    def _():
        slots = [lax.rem(turns[0] + j, count) * depth for j in range(count)]
        for j in range(count):
            place(stacked, slots[j], 0, rims[j][0], channels)
            place(stacked, slots[j], height + 1, rims[j][1], channels)

        def body(row, carry):
            for j in range(count):
                place(stacked, slots[j], row + 1, pieces[j][row], channels)
            return carry

        lax.fori_loop(0, height, body, 0)

    mixed = forward_taps(halves, stacked, step * rows, rows, width)
    size = depth // shares
    for j in range(count):
        parts = []
        for share in range(shares):
            chosen = None
            for at in range(shares):
                start = at * count * size + j * size
                value = mixed[start : start + size]
                here = turns[1] == (share - at) % shares
                chosen = value if chosen is None else jnp.where(here, value, chosen)
            parts.append(chosen)
        pre = jnp.concatenate(parts) if shares > 1 else parts[0]
        sigma = jax.nn.sigmoid(pre)
        activated = (pre * sigma).astype(jnp.bfloat16)
        slope = sigma * (1.0 + pre * (1.0 - sigma))
        for row in range(rows):
            lanes = slice(row * width, (row + 1) * width)
            factor[row, j * depth : (j + 1) * depth, :] = slope[:, lanes]
            outs[j][row] = activated[:, lanes]

    def end(out, side, row):
        for j in range(count):
            part_of = slice(j * depth, (j + 1) * depth)
            value = rims[j][side].astype(jnp.float32) * factor[row, part_of, :]
            out[0, part_of, :] = value.astype(jnp.bfloat16)

    @pl.when(step == 0)
    def _():
        end(first, 2, 0)

    @pl.when(step == pl.num_programs(0) - 1)
    def _():
        end(last, 3, rows - 1)


def whole(shape):
    return pl.BlockSpec(shape, lambda *_: (0,) * len(shape), pipeline_mode=pl.Buffered(1))


def forward(turns, pieces, rims, halves):
    count = len(pieces)
    height, depth, width = pieces[0].shape
    channels = count * depth
    rows = 4 if height % 4 == 0 else 1
    flops = 2 * 9 * channels * channels * height * width
    call = pl.pallas_call(
        functools.partial(forward_body, count, len(halves), rows),
        grid=(height // rows,),
        in_specs=[pl.BlockSpec(memory_space=pltpu.SMEM)]
        + [whole(pieces[0].shape)] * count
        + [whole(rims[0].shape)] * count
        + [whole(halves[0].shape)] * len(halves),
        out_specs=[pl.BlockSpec((rows, depth, width), lambda g: (g, 0, 0))] * count
        + [
            pl.BlockSpec((rows, channels, width), lambda g: (g, 0, 0)),
            whole((3 * channels, (height + 2) * width)),
            whole((1, channels, width)),
            whole((1, channels, width)),
        ],
        out_shape=[jax.ShapeDtypeStruct((height, depth, width), jnp.bfloat16)] * count
        + [
            jax.ShapeDtypeStruct((height, channels, width), jnp.float32),
            jax.ShapeDtypeStruct((3 * channels, (height + 2) * width), jnp.bfloat16),
            jax.ShapeDtypeStruct((1, channels, width), jnp.bfloat16),
            jax.ShapeDtypeStruct((1, channels, width), jnp.bfloat16),
        ],
        compiler_params=pltpu.CompilerParams(vmem_limit_bytes=VMEM_LIMIT),
        cost_estimate=pl.CostEstimate(
            flops=flops, bytes_accessed=16 * 1024 * 1024, transcendentals=0
        ),
        name="conv_forward",
    )
    results = call(turns, *pieces, *rims, *halves)
    return results[:count], *results[count:]


def correlate_body(count, groups, rows, turn, stacked, factor, *refs):
    pieces, ends = refs[:count], refs[count : 2 * count]
    shares, slope = refs[2 * count : -1], refs[-1]
    height, depth, width = factor.shape[0], pieces[0].shape[1], factor.shape[2]
    channels = count * depth
    tap_row, tap_col = pl.program_id(0), pl.program_id(1)

    @pl.when((tap_row == 0) & (tap_col == 0))
    def _():
        def put(row, blocks):
            lanes = pl.ds(pl.multiple_of(row * width, width), width)
            for j in range(count):
                part_of = pl.ds(j * depth, depth)
                value = blocks[j].astype(jnp.float32) * factor[row, part_of, :]
                slope[part_of, lanes] = value.astype(jnp.bfloat16)

        def body(row, carry):
            put(row + 1, [piece[row] for piece in pieces])
            return carry

        put(0, [end[2] for end in ends])
        lax.fori_loop(0, height - 2, body, 0)
        put(height - 1, [end[3] for end in ends])

    source = stacked[
        pl.ds(pl.multiple_of(tap_col * channels, channels), channels),
        pl.ds(pl.multiple_of(tap_row * width, width), height * width),
    ]
    grads = lax.dot_general(
        source, slope[...], (((1,), (1,)), ((), ())), preferred_element_type=jnp.float32
    )
    size = channels // (groups * rows)
    for own in range(rows):

        @pl.when(turn[0] == own)
        def _():
            for j in range(rows):
                for group in range(groups):
                    start = (group * rows + (own - j) % rows) * size
                    shares[j][group, 0] = grads[start : start + size]


def correlate(stacked, factor, pieces, ends):
    count = len(pieces)
    height, channels, width = factor.shape
    groups, rows = lax.axis_size("dp"), lax.axis_size("row")
    size = channels // (groups * rows)
    flops = 2 * 9 * channels * channels * height * width
    call = pl.pallas_call(
        functools.partial(correlate_body, count, groups, rows),
        grid=(3, 3),
        in_specs=[pl.BlockSpec(memory_space=pltpu.SMEM)]
        + [whole(stacked.shape), whole(factor.shape)]
        + [whole(pieces[0].shape)] * count
        + [whole(ends[0].shape)] * count,
        out_specs=[pl.BlockSpec((groups, 1, size, channels), lambda a, b: (0, 3 * a + b, 0, 0))]
        * rows
        + [whole((channels, height * width))],
        out_shape=[jax.ShapeDtypeStruct((groups, 9, size, channels), jnp.float32)] * rows
        + [jax.ShapeDtypeStruct((channels, height * width), jnp.bfloat16)],
        compiler_params=pltpu.CompilerParams(vmem_limit_bytes=VMEM_LIMIT),
        cost_estimate=pl.CostEstimate(
            flops=flops, bytes_accessed=14 * 1024 * 1024, transcendentals=0
        ),
        name="kernel_grad",
    )
    turn = lax.axis_index("row").astype(jnp.int32)[None]
    results = call(turn, stacked, factor, *pieces, *ends)
    return results[:-1], results[-1]


def padded_depth(depth):
    return -(-depth // 128) * 128


def turned_body(shares, *refs):
    halves, out = refs[:shares], refs[shares]
    _, depth, lanes = out.shape
    stride = lanes // 9
    total = halves[0].shape[2]
    both = [jnp.concatenate([half[0] for half in halves])]
    channels = both[0].shape[0]
    rows = []
    for start in range(0, total, 128):
        size = min(128, total - start)
        unit = (
            lax.broadcasted_iota(jnp.int32, (size, size), 0)
            == lax.broadcasted_iota(jnp.int32, (size, size), 1)
        ).astype(jnp.bfloat16)
        rows.append(
            lax.dot_general(
                unit,
                both[0][:, start : start + size],
                (((1,), (1,)), ((), ())),
                preferred_element_type=jnp.float32,
            )
        )
    turned = jnp.concatenate(rows)
    for tap in range(9):
        begin = (8 - tap) * depth
        value = turned[begin : begin + depth].astype(jnp.bfloat16)
        out[0, :, tap * stride : tap * stride + channels] = value
        if stride > channels:
            out[0, :, tap * stride + channels : (tap + 1) * stride] = jnp.zeros(
                (depth, stride - channels), jnp.bfloat16
            )


def turned(halves):
    shares = len(halves)
    blocks, outs, lanes = halves[0].shape
    depth = lanes // 9
    stride = padded_depth(outs * shares)
    return pl.pallas_call(
        functools.partial(turned_body, shares),
        grid=(blocks,),
        in_specs=[pl.BlockSpec((1, outs, lanes), lambda g: (g, 0, 0))] * shares,
        out_specs=pl.BlockSpec((1, depth, 9 * stride), lambda g: (g, 0, 0)),
        out_shape=jax.ShapeDtypeStruct((blocks, depth, 9 * stride), jnp.bfloat16),
        compiler_params=pltpu.CompilerParams(vmem_limit_bytes=VMEM_LIMIT),
        cost_estimate=pl.CostEstimate(
            flops=2 * 128 * blocks * outs * shares * lanes,
            bytes_accessed=4 * 1024 * 1024,
            transcendentals=0,
        ),
        name="turn_kernel",
    )(*halves)


def backward_body(count, shares, rows, turns, slope, above, below, kernels, *refs):
    outs, stacked = refs[:count], refs[count]
    channels = slope.shape[0]
    _, _, width = above.shape
    height = slope.shape[1] // width
    depth = channels // count
    size = depth // shares
    stride = stacked.shape[0] // 3
    step = pl.program_id(0)

    def in_share_order(wide):
        parts = []
        for at in range(shares):
            chosen = None
            for share in range(shares):
                value = jnp.concatenate(
                    [wide[j * depth + share * size : j * depth + (share + 1) * size] for j in range(count)]
                )
                here = turns[3] == (share - at) % shares
                chosen = value if chosen is None else jnp.where(here, value, chosen)
            parts.append(chosen)
        return jnp.concatenate(parts)

    def put(row, block):
        lanes = pl.ds(pl.multiple_of(row * width, width), width)
        wide = in_share_order(block.astype(jnp.float32))
        for copies, moved in enumerate((columns_moved(wide, -1), wide, columns_moved(wide, 1))):
            stacked[copies * stride : copies * stride + channels, lanes] = moved.astype(slope.dtype)

    @pl.when(step == 0)
    def _():
        if stride > channels:
            for copies in range(3):
                stacked[copies * stride + channels : (copies + 1) * stride, :] = jnp.zeros(
                    (stride - channels, stacked.shape[1]), stacked.dtype
                )
        for side, rim, row in ((0, above, 0), (1, below, height + 1)):
            blocks = []
            for j in range(count):
                start = lax.rem(turns[side] + j, count) * depth
                blocks.append(rim[0, pl.ds(pl.multiple_of(start, depth), depth), :])
            put(row, jnp.concatenate(blocks))

        def body(row, carry):
            lanes = pl.ds(pl.multiple_of(row * width, width), width)
            put(row + 1, slope[:, lanes])
            return carry

        lax.fori_loop(0, height, body, 0)

    windows = [
        stacked[:, pl.ds(pl.multiple_of((step * rows + a) * width, width), rows * width)]
        for a in range(3)
    ]
    order = [kernels[lax.rem(turns[2] + j, count)] for j in range(count)]
    grad = jnp.dot(
        jnp.concatenate(order), jnp.concatenate(windows), preferred_element_type=jnp.float32
    )
    for row in range(rows):
        lanes = slice(row * width, (row + 1) * width)
        for j in range(count):
            outs[j][row] = grad[j * depth : (j + 1) * depth, lanes].astype(outs[j].dtype)


def backward(turns, slope, above, below, kernels, count):
    channels = slope.shape[0]
    width = above.shape[2]
    height = slope.shape[1] // width
    depth = channels // count
    rows = 4 if height % 4 == 0 else 1
    flops = 2 * 9 * channels * channels * height * width
    return pl.pallas_call(
        functools.partial(backward_body, count, lax.axis_size("row"), rows),
        grid=(height // rows,),
        in_specs=[
            pl.BlockSpec(memory_space=pltpu.SMEM),
            whole(slope.shape),
            whole(above.shape),
            whole(below.shape),
            whole(kernels.shape),
        ],
        out_specs=[pl.BlockSpec((rows, depth, width), lambda g: (g, 0, 0))] * count,
        out_shape=[
            jax.ShapeDtypeStruct((height, depth, width), jnp.bfloat16 if j else jnp.float32)
            for j in range(count)
        ],
        scratch_shapes=[pltpu.VMEM((kernels.shape[2] // 3, (height + 2) * width), jnp.bfloat16)],
        compiler_params=pltpu.CompilerParams(vmem_limit_bytes=VMEM_LIMIT),
        cost_estimate=pl.CostEstimate(
            flops=flops, bytes_accessed=8 * 1024 * 1024, transcendentals=0
        ),
        name="conv_backward",
    )(turns, slope, above, below, kernels)


def gathered_kernel(kernel):
    dp, row = lax.axis_index("dp"), lax.axis_index("row")
    dps, chans, rows = (lax.axis_size(a) for a in ("dp", "chan", "row"))
    _, inner, outer = kernel.shape
    size = outer // rows
    mine = part(kernel, row, size, 2)
    mine = jnp.transpose(mine, (2, 0, 1)).reshape(size, 9 * inner)
    over_chan = jnp.concatenate([mine] + [receive(mine, "chan", j) for j in range(1, chans)], axis=0)
    over_dp = jnp.stack([over_chan] + [receive(over_chan, "dp", j) for j in range(1, dps)])
    if dps != chans:
        each = dps // chans
        over_dp = rotated(over_dp, (dps - dp) % dps, 0)
        over_dp = over_dp.reshape(chans, each, chans * size, 9, inner)
        over_dp = jnp.transpose(over_dp, (0, 2, 3, 1, 4)).reshape(chans, chans * size, 9 * each * inner)
    return [over_dp] + [receive(over_dp, "row", j) for j in range(1, rows)]


def summed_kernel_grad(shares, inner, outer):
    dp, row = lax.axis_index("dp"), lax.axis_index("row")
    dps, chans, rows = (lax.axis_size(a) for a in ("dp", "chan", "row"))
    channels = shares[0].shape[3]
    share = inner // rows
    halves = shares[0]
    for j in range(1, rows):
        halves = halves + receive(shares[j], "row", j)

    def of_dp(ahead):
        if dps == chans:
            return halves[ahead % dps]
        return lax.dynamic_index_in_dim(halves, (dp + ahead) % dps, 0, keepdims=False)

    total = of_dp(0)
    for j in range(1, dps):
        total = total + receive(of_dp(-j), "dp", j)
    total = jnp.transpose(total, (2, 0, 1)).reshape(channels, 9 * share)
    own = total[:outer]
    for j in range(1, chans):
        start = (chans - j) * outer
        own = own + receive(total[start : start + outer], "chan", j)
    both = jnp.stack([own] + [receive(own, "row", j) for j in range(1, rows)])
    both = rotated(both, (rows - row) % rows, 0).reshape(rows, outer, 9, share)
    return jnp.transpose(both, (2, 0, 3, 1)).reshape(9, inner, outer)


def shards(images, kernel, cotangent):
    row, chan = lax.axis_index("row"), lax.axis_index("chan")
    rows, chans = lax.axis_size("row"), lax.axis_size("chan")
    _, slab, depth, width = images.shape
    height = slab // chans
    images, cotangent = images[0], cotangent[0]

    def home(ahead):
        return home_of(row, (chan + ahead) % chans, chans)

    def to_homes(array, size):
        return [part(array, home(0), size, 0)] + [
            receive(part(array, home(-j), size, 0), "chan", j) for j in range(1, chans)
        ]

    halves = gathered_kernel(kernel)
    pieces = to_homes(images, height)
    if rows == 2:
        edge = jnp.where(row == 0, images[slab - 1 :], images[:1])
        edge = receive(edge, "row", 1)
        low = jnp.where(row == 0, jnp.zeros_like(edge), edge)
        high = jnp.where(row == 0, edge, jnp.zeros_like(edge))
    else:
        low = lax.ppermute(images[slab - 1 :], "row", [(i, i + 1) for i in range(rows - 1)])
        high = lax.ppermute(images[:1], "row", [(i + 1, i) for i in range(rows - 1)])

    def rim_of(at):
        begin = at * height
        above = part(images, jnp.maximum(begin - 1, 0), 1, 0)
        below = part(images, jnp.minimum(begin + height, slab - 1), 1, 0)
        return jnp.concatenate(
            [
                jnp.where(at == 0, low, above),
                jnp.where(at == chans - 1, high, below),
                part(cotangent, begin, 1, 0),
                part(cotangent, begin + height - 1, 1, 0),
            ]
        )

    rims = [rim_of(home(0))]
    rims += [receive(rim_of(home(-j)), "chan", j) for j in range(1, chans)]

    def inside(ahead):
        return lax.dynamic_slice_in_dim(cotangent, home(ahead) * height + 1, height - 2, 0)

    cotangents = [inside(0)] + [receive(inside(-j), "chan", j) for j in range(1, chans)]

    shift = (chan - stacking_base()) % chans
    place_at = home(0)
    forth = jnp.where(row % 2 == 0, 1, chans - 1)
    above_turn = jnp.where(place_at == 0, 0, forth)
    below_turn = jnp.where(place_at == chans - 1, 0, chans - forth)
    turns = jnp.stack([shift, row]).astype(jnp.int32)
    back_turns = jnp.stack([above_turn, below_turn, shift, row]).astype(jnp.int32)

    results = forward(turns, pieces, rims, halves)
    activated, factor, stacked, first, last = results
    back_kernel = turned(halves)

    def snake(place_at):
        r, k = place_at // chans, place_at % chans
        return (k if r % 2 == 0 else chans - 1 - k) * rows + r

    line = [(snake(i), snake(i + 1)) for i in range(rows * chans - 1)]
    above = lax.ppermute(last, ("chan", "row"), line)
    below = lax.ppermute(first, ("chan", "row"), [(b, a) for a, b in line])

    grads, slope = correlate(stacked, factor, cotangents, rims)
    input_grads = backward(back_turns, slope, above, below, back_kernel, chans)
    kernel_grad = summed_kernel_grad(grads, kernel.shape[1], kernel.shape[2])

    def to_owners(blocks, dtype):
        out = jnp.zeros((slab, depth, width), dtype)
        for j in range(chans):
            arrived = receive(blocks[j], "chan", chans - j) if j else blocks[0]
            out = lax.dynamic_update_slice_in_dim(out, arrived.astype(dtype), home(-j) * height, 0)
        return out[None]

    return to_owners(activated, jnp.bfloat16), to_owners(input_grads, jnp.float32), kernel_grad


def solution(mesh):
    placed = (P("dp", "row", "chan", None), P(None, "dp", "chan"), P("dp", "row", "chan", None))
    return jax.shard_map(
        shards,
        mesh=mesh,
        in_specs=placed,
        out_specs=(
            P("dp", "row", "chan", None),
            P("dp", "row", "chan", None),
            P(None, "dp", "chan"),
        ),
        check_vma=False,
    )
```

```python
import functools

import jax
import jax.numpy as jnp
from jax import lax
from jax.experimental import pallas as pl
from jax.experimental.pallas import tpu as pltpu
from jax.sharding import PartitionSpec as P


VMEM_LIMIT = 60 * 1024 * 1024


def receive(block, axis, ahead):
    count = lax.axis_size(axis)
    return lax.ppermute(block, axis, [(i, (i - ahead) % count) for i in range(count)])


def home_of(row, chan, chans):
    return jnp.where(row % 2 == 0, chan, chans - 1 - chan)


def part(array, index, size, axis):
    return lax.dynamic_slice_in_dim(array, index * size, size, axis=axis)


def rotated(array, start, axis):
    twice = jnp.concatenate([array, array], axis=axis)
    return lax.dynamic_slice_in_dim(twice, start, array.shape[axis], axis=axis)


def stacking_base():
    matched = lax.axis_size("dp") == lax.axis_size("chan")
    return lax.axis_index("dp") if matched else jnp.int32(0)


def columns_moved(block, step):
    width = block.shape[-1]
    lane = lax.broadcasted_iota(jnp.int32, block.shape, block.ndim - 1)
    if step < 0:
        moved = pltpu.roll(block, 1, block.ndim - 1)
        return jnp.where(lane == 0, jnp.zeros_like(block), moved)
    moved = pltpu.roll(block, width - 1, block.ndim - 1)
    return jnp.where(lane == width - 1, jnp.zeros_like(block), moved)


def place(stacked, channel, row, block, channels):
    depth, width = block.shape
    lanes = pl.ds(pl.multiple_of(row * width, width), width)
    wide = block.astype(jnp.float32)

    def below(copies):
        start = copies * channels + channel
        return pl.ds(start if isinstance(channel, int) else pl.multiple_of(start, 16), depth)

    stacked[below(0), lanes] = columns_moved(wide, -1).astype(block.dtype)
    stacked[below(1), lanes] = block
    stacked[below(2), lanes] = columns_moved(wide, 1).astype(block.dtype)


def window(stacked, tap_row, tap_col, channel, depth, first, rows, width, channels):
    start = pl.multiple_of((first + tap_row) * width, width)
    return stacked[tap_col * channels + channel : tap_col * channels + channel + depth, pl.ds(start, rows * width)]


def forward_taps(halves, stacked, first, rows, width):
    count = halves[0].shape[0]
    depth = halves[0].shape[2] // 9
    total = None
    for block in range(count):
        windows = [
            window(stacked, a, b, block * depth, depth, first, rows, width, count * depth)
            for a in range(3)
            for b in range(3)
        ]
        term = jnp.dot(
            jnp.concatenate([half[block] for half in halves]),
            jnp.concatenate(windows),
            preferred_element_type=jnp.float32,
        )
        total = term if total is None else total + term
    return total


def forward_body(count, shares, rows, turns, *refs):
    pieces, rims = refs[:count], refs[count : 2 * count]
    halves = refs[2 * count : 2 * count + shares]
    outs = refs[2 * count + shares : 3 * count + shares]
    factor, stacked, first, last = refs[3 * count + shares :]
    height, depth, width = pieces[0].shape
    channels = count * depth
    step = pl.program_id(0)

    @pl.when(step == 0)
    def _():
        slots = [lax.rem(turns[0] + j, count) * depth for j in range(count)]
        for j in range(count):
            place(stacked, slots[j], 0, rims[j][0], channels)
            place(stacked, slots[j], height + 1, rims[j][1], channels)

        def body(row, carry):
            for j in range(count):
                place(stacked, slots[j], row + 1, pieces[j][row], channels)
            return carry

        lax.fori_loop(0, height, body, 0)

    mixed = forward_taps(halves, stacked, step * rows, rows, width)
    size = depth // shares
    for j in range(count):
        parts = []
        for share in range(shares):
            chosen = None
            for at in range(shares):
                start = at * count * size + j * size
                value = mixed[start : start + size]
                here = turns[1] == (share - at) % shares
                chosen = value if chosen is None else jnp.where(here, value, chosen)
            parts.append(chosen)
        pre = jnp.concatenate(parts) if shares > 1 else parts[0]
        sigma = jax.nn.sigmoid(pre)
        activated = (pre * sigma).astype(jnp.bfloat16)
        slope = sigma * (1.0 + pre * (1.0 - sigma))
        for row in range(rows):
            lanes = slice(row * width, (row + 1) * width)
            factor[row, j * depth : (j + 1) * depth, :] = slope[:, lanes]
            outs[j][row] = activated[:, lanes]

    def end(out, side, row):
        for j in range(count):
            part_of = slice(j * depth, (j + 1) * depth)
            value = rims[j][side].astype(jnp.float32) * factor[row, part_of, :]
            out[0, part_of, :] = value.astype(jnp.bfloat16)

    @pl.when(step == 0)
    def _():
        end(first, 2, 0)

    @pl.when(step == pl.num_programs(0) - 1)
    def _():
        end(last, 3, rows - 1)


def whole(shape):
    return pl.BlockSpec(shape, lambda *_: (0,) * len(shape), pipeline_mode=pl.Buffered(1))


def forward(turns, pieces, rims, halves, slab):
    count = len(pieces)
    height, depth, width = pieces[0].shape
    channels = count * depth
    rows = 4 if height % 4 == 0 else 1
    flops = 2 * 9 * channels * channels * height * width
    steps = height // rows
    call = pl.pallas_call(
        functools.partial(forward_body, count, len(halves), rows),
        grid_spec=pltpu.PrefetchScalarGridSpec(
            num_scalar_prefetch=1,
            grid=(steps,),
            in_specs=[whole(pieces[0].shape)] * count
            + [whole(rims[0].shape)] * count
            + [whole(halves[0].shape)] * len(halves),
            out_specs=[pl.BlockSpec((rows, depth, width), lambda g, turns: (turns[2] * steps + g, 0, 0))]
            + [pl.BlockSpec((rows, depth, width), lambda g, _: (g, 0, 0))] * (count - 1)
            + [
                pl.BlockSpec((rows, channels, width), lambda g, _: (g, 0, 0)),
                whole((3 * channels, (height + 2) * width)),
                whole((1, channels, width)),
                whole((1, channels, width)),
            ],
        ),
        out_shape=[
            jax.ShapeDtypeStruct((height if j else slab, depth, width), jnp.bfloat16)
            for j in range(count)
        ]
        + [
            jax.ShapeDtypeStruct((height, channels, width), jnp.float32),
            jax.ShapeDtypeStruct((3 * channels, (height + 2) * width), jnp.bfloat16),
            jax.ShapeDtypeStruct((1, channels, width), jnp.bfloat16),
            jax.ShapeDtypeStruct((1, channels, width), jnp.bfloat16),
        ],
        compiler_params=pltpu.CompilerParams(vmem_limit_bytes=VMEM_LIMIT),
        cost_estimate=pl.CostEstimate(
            flops=flops, bytes_accessed=16 * 1024 * 1024, transcendentals=0
        ),
        name="conv_forward",
    )
    results = call(turns, *pieces, *rims, *halves)
    return list(results[:count]), *results[count:]


def slope_rows(factor, pieces, ends, slope):
    count = len(pieces)
    height, _, width = factor.shape
    depth = pieces[0].shape[1]

    def put(row, blocks):
        lanes = pl.ds(pl.multiple_of(row * width, width), width)
        for j in range(count):
            part_of = pl.ds(j * depth, depth)
            value = blocks[j].astype(jnp.float32) * factor[row, part_of, :]
            slope[part_of, lanes] = value.astype(jnp.bfloat16)

    def body(row, carry):
        put(row + 1, [piece[row] for piece in pieces])
        return carry

    put(0, [end[2] for end in ends])
    lax.fori_loop(0, height - 2, body, 0)
    put(height - 1, [end[3] for end in ends])


def correlate_body(first_tap, count, groups, rows, turn, stacked, *refs):
    if count:
        factor, pieces, ends = refs[0], refs[1 : 1 + count], refs[1 + count : 1 + 2 * count]
        shares, slope = refs[1 + 2 * count : -1], refs[-1]
    else:
        slope, shares = refs[0], refs[1:]
    channels, pixels = slope.shape
    width = stacked.shape[1] - pixels
    width = width // 2
    tap = first_tap + pl.program_id(0)
    tap_row, tap_col = tap // 3, lax.rem(tap, 3)
    if count:

        @pl.when(pl.program_id(0) == 0)
        def _():
            slope_rows(factor, pieces, ends, slope)

    source = stacked[
        pl.ds(pl.multiple_of(tap_col * channels, channels), channels),
        pl.ds(pl.multiple_of(tap_row * width, width), pixels),
    ]
    grads = lax.dot_general(
        source, slope[...], (((1,), (1,)), ((), ())), preferred_element_type=jnp.float32
    )
    size = channels // (groups * rows)
    for own in range(rows):

        @pl.when(turn[0] == own)
        def _():
            for j in range(rows):
                for group in range(groups):
                    start = (group * rows + (own - j) % rows) * size
                    shares[j][group, 0] = grads[start : start + size]


def correlate(taps, stacked, slope=None, factor=None, pieces=(), ends=()):
    first_tap, tap_count = taps
    channels = stacked.shape[0] // 3
    groups, rows = lax.axis_size("dp"), lax.axis_size("row")
    size = channels // (groups * rows)
    if slope is None:
        height, _, width = factor.shape
        pixels = height * width
        operands = [factor, *pieces, *ends]
        made = [jax.ShapeDtypeStruct((channels, pixels), jnp.bfloat16)]
    else:
        pixels = slope.shape[1]
        operands, made = [slope], []
    call = pl.pallas_call(
        functools.partial(correlate_body, first_tap, len(pieces), groups, rows),
        grid=(tap_count,),
        in_specs=[pl.BlockSpec(memory_space=pltpu.SMEM), whole(stacked.shape)]
        + [whole(operand.shape) for operand in operands],
        out_specs=[pl.BlockSpec((groups, 1, size, channels), lambda t: (0, t, 0, 0))] * rows
        + [whole(each.shape) for each in made],
        out_shape=[jax.ShapeDtypeStruct((groups, tap_count, size, channels), jnp.float32)] * rows
        + made,
        compiler_params=pltpu.CompilerParams(vmem_limit_bytes=VMEM_LIMIT),
        cost_estimate=pl.CostEstimate(
            flops=2 * tap_count * channels * channels * pixels,
            bytes_accessed=8 * 1024 * 1024,
            transcendentals=0,
        ),
    )
    turn = lax.axis_index("row").astype(jnp.int32)[None]
    results = call(turn, stacked, *operands)
    return (results[:rows], *results[rows:])


def padded_depth(depth):
    return -(-depth // 128) * 128


def turned_body(shares, *refs):
    halves, out = refs[:shares], refs[shares]
    _, depth, lanes = out.shape
    stride = lanes // 9
    total = halves[0].shape[2]
    both = [jnp.concatenate([half[0] for half in halves])]
    channels = both[0].shape[0]
    rows = []
    for start in range(0, total, 128):
        size = min(128, total - start)
        unit = (
            lax.broadcasted_iota(jnp.int32, (size, size), 0)
            == lax.broadcasted_iota(jnp.int32, (size, size), 1)
        ).astype(jnp.bfloat16)
        rows.append(
            lax.dot_general(
                unit,
                both[0][:, start : start + size],
                (((1,), (1,)), ((), ())),
                preferred_element_type=jnp.float32,
            )
        )
    turned = jnp.concatenate(rows)
    for tap in range(9):
        begin = (8 - tap) * depth
        value = turned[begin : begin + depth].astype(jnp.bfloat16)
        out[0, :, tap * stride : tap * stride + channels] = value
        if stride > channels:
            out[0, :, tap * stride + channels : (tap + 1) * stride] = jnp.zeros(
                (depth, stride - channels), jnp.bfloat16
            )


def turned(halves):
    shares = len(halves)
    blocks, outs, lanes = halves[0].shape
    depth = lanes // 9
    stride = padded_depth(outs * shares)
    return pl.pallas_call(
        functools.partial(turned_body, shares),
        grid=(blocks,),
        in_specs=[pl.BlockSpec((1, outs, lanes), lambda g: (g, 0, 0))] * shares,
        out_specs=pl.BlockSpec((1, depth, 9 * stride), lambda g: (g, 0, 0)),
        out_shape=jax.ShapeDtypeStruct((blocks, depth, 9 * stride), jnp.bfloat16),
        compiler_params=pltpu.CompilerParams(vmem_limit_bytes=VMEM_LIMIT),
        cost_estimate=pl.CostEstimate(
            flops=2 * 128 * blocks * outs * shares * lanes,
            bytes_accessed=4 * 1024 * 1024,
            transcendentals=0,
        ),
        name="turn_kernel",
    )(*halves)


def backward_body(count, shares, rows, turns, slope, above, below, kernels, *refs):
    outs, stacked = refs[:count], refs[count]
    channels = slope.shape[0]
    _, _, width = above.shape
    height = slope.shape[1] // width
    depth = channels // count
    size = depth // shares
    stride = stacked.shape[0] // 3
    step = pl.program_id(0)

    def in_share_order(wide):
        parts = []
        for at in range(shares):
            chosen = None
            for share in range(shares):
                value = jnp.concatenate(
                    [wide[j * depth + share * size : j * depth + (share + 1) * size] for j in range(count)]
                )
                here = turns[3] == (share - at) % shares
                chosen = value if chosen is None else jnp.where(here, value, chosen)
            parts.append(chosen)
        return jnp.concatenate(parts)

    def put(row, block):
        lanes = pl.ds(pl.multiple_of(row * width, width), width)
        wide = in_share_order(block.astype(jnp.float32))
        for copies, moved in enumerate((columns_moved(wide, -1), wide, columns_moved(wide, 1))):
            stacked[copies * stride : copies * stride + channels, lanes] = moved.astype(slope.dtype)

    @pl.when(step == 0)
    def _():
        if stride > channels:
            for copies in range(3):
                stacked[copies * stride + channels : (copies + 1) * stride, :] = jnp.zeros(
                    (stride - channels, stacked.shape[1]), stacked.dtype
                )
        for side, rim, row in ((0, above, 0), (1, below, height + 1)):
            blocks = []
            for j in range(count):
                start = lax.rem(turns[side] + j, count) * depth
                blocks.append(rim[0, pl.ds(pl.multiple_of(start, depth), depth), :])
            put(row, jnp.concatenate(blocks))

        def body(row, carry):
            lanes = pl.ds(pl.multiple_of(row * width, width), width)
            put(row + 1, slope[:, lanes])
            return carry

        lax.fori_loop(0, height, body, 0)

    windows = [
        stacked[:, pl.ds(pl.multiple_of((step * rows + a) * width, width), rows * width)]
        for a in range(3)
    ]
    order = [kernels[lax.rem(turns[2] + j, count)] for j in range(count)]
    grad = jnp.dot(
        jnp.concatenate(order), jnp.concatenate(windows), preferred_element_type=jnp.float32
    )
    for row in range(rows):
        lanes = slice(row * width, (row + 1) * width)
        for j in range(count):
            outs[j][row] = grad[j * depth : (j + 1) * depth, lanes].astype(outs[j].dtype)


def backward(turns, slope, above, below, kernels, count, slab):
    channels = slope.shape[0]
    width = above.shape[2]
    height = slope.shape[1] // width
    depth = channels // count
    rows = 4 if height % 4 == 0 else 1
    flops = 2 * 9 * channels * channels * height * width
    steps = height // rows
    return pl.pallas_call(
        functools.partial(backward_body, count, lax.axis_size("row"), rows),
        grid_spec=pltpu.PrefetchScalarGridSpec(
            num_scalar_prefetch=1,
            grid=(steps,),
            in_specs=[
                whole(slope.shape),
                whole(above.shape),
                whole(below.shape),
                whole(kernels.shape),
            ],
            out_specs=[pl.BlockSpec((rows, depth, width), lambda g, turns: (turns[4] * steps + g, 0, 0))]
            + [pl.BlockSpec((rows, depth, width), lambda g, _: (g, 0, 0))] * (count - 1),
            scratch_shapes=[pltpu.VMEM((kernels.shape[2] // 3, (height + 2) * width), jnp.bfloat16)],
        ),
        out_shape=[jax.ShapeDtypeStruct((slab, depth, width), jnp.float32)]
        + [jax.ShapeDtypeStruct((height, depth, width), jnp.bfloat16)] * (count - 1),
        compiler_params=pltpu.CompilerParams(vmem_limit_bytes=VMEM_LIMIT),
        cost_estimate=pl.CostEstimate(
            flops=flops, bytes_accessed=8 * 1024 * 1024, transcendentals=0
        ),
        name="conv_backward",
    )(turns, slope, above, below, kernels)


def gathered_kernel(kernel):
    dp, row = lax.axis_index("dp"), lax.axis_index("row")
    dps, chans, rows = (lax.axis_size(a) for a in ("dp", "chan", "row"))
    _, inner, outer = kernel.shape
    size = outer // rows
    mine = part(kernel, row, size, 2)
    mine = jnp.transpose(mine, (2, 0, 1)).reshape(size, 9 * inner)
    over_chan = jnp.concatenate([mine] + [receive(mine, "chan", j) for j in range(1, chans)], axis=0)
    over_dp = jnp.stack([over_chan] + [receive(over_chan, "dp", j) for j in range(1, dps)])
    if dps != chans:
        each = dps // chans
        over_dp = rotated(over_dp, (dps - dp) % dps, 0)
        over_dp = over_dp.reshape(chans, each, chans * size, 9, inner)
        over_dp = jnp.transpose(over_dp, (0, 2, 3, 1, 4)).reshape(chans, chans * size, 9 * each * inner)
    return [over_dp] + [receive(over_dp, "row", j) for j in range(1, rows)]


def summed_over_images(shares):
    dp = lax.axis_index("dp")
    dps, chans, rows = (lax.axis_size(a) for a in ("dp", "chan", "row"))
    halves = shares[0]
    for j in range(1, rows):
        halves = halves + receive(shares[j], "row", j)

    def of_dp(ahead):
        if dps == chans:
            return halves[ahead % dps]
        return lax.dynamic_index_in_dim(halves, (dp + ahead) % dps, 0, keepdims=False)

    total = of_dp(0)
    for j in range(1, dps):
        total = total + receive(of_dp(-j), "dp", j)
    return total


def summed_kernel_grad(terms, inner, outer):
    row = lax.axis_index("row")
    chans, rows = lax.axis_size("chan"), lax.axis_size("row")
    share = inner // rows
    channels = terms[0].shape[2]
    total = jnp.concatenate(terms)
    total = jnp.transpose(total, (2, 0, 1)).reshape(channels, 9 * share)
    own = total[:outer]
    for j in range(1, chans):
        start = (chans - j) * outer
        own = own + receive(total[start : start + outer], "chan", j)
    both = jnp.stack([own] + [receive(own, "row", j) for j in range(1, rows)])
    both = rotated(both, (rows - row) % rows, 0).reshape(rows, outer, 9, share)
    return jnp.transpose(both, (2, 0, 3, 1)).reshape(9, inner, outer)


def shards(images, kernel, cotangent):
    row, chan = lax.axis_index("row"), lax.axis_index("chan")
    rows, chans = lax.axis_size("row"), lax.axis_size("chan")
    _, slab, _, _ = images.shape
    height = slab // chans
    images, cotangent = images[0], cotangent[0]

    def home(ahead):
        return home_of(row, (chan + ahead) % chans, chans)

    def to_homes(array, size):
        return [part(array, home(0), size, 0)] + [
            receive(part(array, home(-j), size, 0), "chan", j) for j in range(1, chans)
        ]

    halves = gathered_kernel(kernel)
    pieces = to_homes(images, height)
    if rows == 2:
        edge = jnp.where(row == 0, images[slab - 1 :], images[:1])
        edge = receive(edge, "row", 1)
        low = jnp.where(row == 0, jnp.zeros_like(edge), edge)
        high = jnp.where(row == 0, edge, jnp.zeros_like(edge))
    else:
        low = lax.ppermute(images[slab - 1 :], "row", [(i, i + 1) for i in range(rows - 1)])
        high = lax.ppermute(images[:1], "row", [(i + 1, i) for i in range(rows - 1)])

    def rim_of(at):
        begin = at * height
        above = part(images, jnp.maximum(begin - 1, 0), 1, 0)
        below = part(images, jnp.minimum(begin + height, slab - 1), 1, 0)
        return jnp.concatenate(
            [
                jnp.where(at == 0, low, above),
                jnp.where(at == chans - 1, high, below),
                part(cotangent, begin, 1, 0),
                part(cotangent, begin + height - 1, 1, 0),
            ]
        )

    rims = [rim_of(home(0))]
    rims += [receive(rim_of(home(-j)), "chan", j) for j in range(1, chans)]

    def inside(ahead):
        return lax.dynamic_slice_in_dim(cotangent, home(ahead) * height + 1, height - 2, 0)

    cotangents = [inside(0)] + [receive(inside(-j), "chan", j) for j in range(1, chans)]

    shift = (chan - stacking_base()) % chans
    place_at = home(0)
    forth = jnp.where(row % 2 == 0, 1, chans - 1)
    above_turn = jnp.where(place_at == 0, 0, forth)
    below_turn = jnp.where(place_at == chans - 1, 0, chans - forth)
    turns = jnp.stack([shift, row, place_at]).astype(jnp.int32)
    back_turns = jnp.stack([above_turn, below_turn, shift, row, place_at]).astype(jnp.int32)

    results = forward(turns, pieces, rims, halves, slab)
    activated, factor, stacked, first, last = results
    back_kernel = turned(halves)

    def snake(place_at):
        r, k = place_at // chans, place_at % chans
        return (k if r % 2 == 0 else chans - 1 - k) * rows + r

    line = [(snake(i), snake(i + 1)) for i in range(rows * chans - 1)]
    above = lax.ppermute(last, ("chan", "row"), line)
    below = lax.ppermute(first, ("chan", "row"), [(b, a) for a, b in line])

    lead, slope = correlate((0, 4), stacked, None, factor, cotangents, rims)
    lead = summed_over_images(lead)
    input_grads = list(backward(back_turns, slope, above, below, back_kernel, chans, slab))
    slope, input_grads[1] = lax.optimization_barrier((slope, input_grads[1]))
    (rest,) = correlate((4, 5), stacked, slope)
    rest = summed_over_images(rest)
    kernel_grad = summed_kernel_grad([lead, rest], kernel.shape[1], kernel.shape[2])

    def to_owners(blocks):
        out = blocks[0]
        for j in range(1, chans):
            arrived = receive(blocks[j], "chan", chans - j).astype(out.dtype)
            out = lax.dynamic_update_slice_in_dim(out, arrived, home(-j) * height, 0)
        return out[None]

    return to_owners(activated), to_owners(input_grads), kernel_grad


def solution(mesh):
    placed = (P("dp", "row", "chan", None), P(None, "dp", "chan"), P("dp", "row", "chan", None))
    return jax.shard_map(
        shards,
        mesh=mesh,
        in_specs=placed,
        out_specs=(
            P("dp", "row", "chan", None),
            P("dp", "row", "chan", None),
            P(None, "dp", "chan"),
        ),
        check_vma=False,
    )
```

```python
import functools

import jax
import jax.numpy as jnp
from jax import lax
from jax.experimental import pallas as pl
from jax.experimental.pallas import tpu as pltpu
from jax.sharding import PartitionSpec as P


VMEM_LIMIT = 60 * 1024 * 1024


def receive(block, axis, ahead):
    count = lax.axis_size(axis)
    return lax.ppermute(block, axis, [(i, (i - ahead) % count) for i in range(count)])


def home_of(row, chan, chans):
    return jnp.where(row % 2 == 0, chan, chans - 1 - chan)


def part(array, index, size, axis):
    return lax.dynamic_slice_in_dim(array, index * size, size, axis=axis)


def rotated(array, start, axis):
    twice = jnp.concatenate([array, array], axis=axis)
    return lax.dynamic_slice_in_dim(twice, start, array.shape[axis], axis=axis)


def stacking_base():
    matched = lax.axis_size("dp") == lax.axis_size("chan")
    return lax.axis_index("dp") if matched else jnp.int32(0)


def columns_moved(block, step):
    width = block.shape[-1]
    lane = lax.broadcasted_iota(jnp.int32, block.shape, block.ndim - 1)
    if step < 0:
        moved = pltpu.roll(block, 1, block.ndim - 1)
        return jnp.where(lane == 0, jnp.zeros_like(block), moved)
    moved = pltpu.roll(block, width - 1, block.ndim - 1)
    return jnp.where(lane == width - 1, jnp.zeros_like(block), moved)


def place(stacked, channel, row, block, channels):
    depth, width = block.shape
    lanes = pl.ds(pl.multiple_of(row * width, width), width)
    wide = block.astype(jnp.float32)

    def below(copies):
        start = copies * channels + channel
        return pl.ds(start if isinstance(channel, int) else pl.multiple_of(start, 16), depth)

    stacked[below(0), lanes] = columns_moved(wide, -1).astype(block.dtype)
    stacked[below(1), lanes] = block
    stacked[below(2), lanes] = columns_moved(wide, 1).astype(block.dtype)


def window(stacked, tap_row, tap_col, channel, depth, first, rows, width, channels):
    start = pl.multiple_of((first + tap_row) * width, width)
    return stacked[tap_col * channels + channel : tap_col * channels + channel + depth, pl.ds(start, rows * width)]


def forward_taps(halves, stacked, first, rows, width):
    count = halves[0].shape[0]
    depth = halves[0].shape[2] // 9
    total = None
    for block in range(count):
        windows = [
            window(stacked, a, b, block * depth, depth, first, rows, width, count * depth)
            for a in range(3)
            for b in range(3)
        ]
        term = jnp.dot(
            jnp.concatenate([half[block] for half in halves]),
            jnp.concatenate(windows),
            preferred_element_type=jnp.float32,
        )
        total = term if total is None else total + term
    return total


def forward_body(count, shares, rows, turns, *refs):
    pieces, rims = refs[:count], refs[count : 2 * count]
    halves = refs[2 * count : 2 * count + shares]
    outs = refs[2 * count + shares : 3 * count + shares]
    factor, stacked, first, last = refs[3 * count + shares :]
    height, depth, width = pieces[0].shape
    channels = count * depth
    step = pl.program_id(0)

    @pl.when(step == 0)
    def _():
        slots = [lax.rem(turns[0] + j, count) * depth for j in range(count)]
        for j in range(count):
            place(stacked, slots[j], 0, rims[j][0], channels)
            place(stacked, slots[j], height + 1, rims[j][1], channels)

        def body(row, carry):
            for j in range(count):
                place(stacked, slots[j], row + 1, pieces[j][row], channels)
            return carry

        lax.fori_loop(0, height, body, 0)

    mixed = forward_taps(halves, stacked, step * rows, rows, width)
    size = depth // shares
    for j in range(count):
        parts = []
        for share in range(shares):
            chosen = None
            for at in range(shares):
                start = at * count * size + j * size
                value = mixed[start : start + size]
                here = turns[1] == (share - at) % shares
                chosen = value if chosen is None else jnp.where(here, value, chosen)
            parts.append(chosen)
        pre = jnp.concatenate(parts) if shares > 1 else parts[0]
        sigma = jax.nn.sigmoid(pre)
        activated = (pre * sigma).astype(jnp.bfloat16)
        slope = sigma * (1.0 + pre * (1.0 - sigma))
        for row in range(rows):
            lanes = slice(row * width, (row + 1) * width)
            factor[row, j * depth : (j + 1) * depth, :] = slope[:, lanes]
            outs[j][row] = activated[:, lanes]

    def end(out, side, row):
        for j in range(count):
            part_of = slice(j * depth, (j + 1) * depth)
            value = rims[j][side].astype(jnp.float32) * factor[row, part_of, :]
            out[0, part_of, :] = value.astype(jnp.bfloat16)

    @pl.when(step == 0)
    def _():
        end(first, 2, 0)

    @pl.when(step == pl.num_programs(0) - 1)
    def _():
        end(last, 3, rows - 1)


def whole(shape):
    return pl.BlockSpec(shape, lambda *_: (0,) * len(shape), pipeline_mode=pl.Buffered(1))


def forward(turns, pieces, rims, halves, slab):
    count = len(pieces)
    height, depth, width = pieces[0].shape
    channels = count * depth
    rows = 4 if height % 4 == 0 else 1
    flops = 2 * 9 * channels * channels * height * width
    steps = height // rows
    call = pl.pallas_call(
        functools.partial(forward_body, count, len(halves), rows),
        grid_spec=pltpu.PrefetchScalarGridSpec(
            num_scalar_prefetch=1,
            grid=(steps,),
            in_specs=[whole(pieces[0].shape)] * count
            + [whole(rims[0].shape)] * count
            + [whole(halves[0].shape)] * len(halves),
            out_specs=[pl.BlockSpec((rows, depth, width), lambda g, turns: (turns[2] * steps + g, 0, 0))]
            + [pl.BlockSpec((rows, depth, width), lambda g, _: (g, 0, 0))] * (count - 1)
            + [
                pl.BlockSpec((rows, channels, width), lambda g, _: (g, 0, 0)),
                whole((3 * channels, (height + 2) * width)),
                whole((1, channels, width)),
                whole((1, channels, width)),
            ],
        ),
        out_shape=[
            jax.ShapeDtypeStruct((height if j else slab, depth, width), jnp.bfloat16)
            for j in range(count)
        ]
        + [
            jax.ShapeDtypeStruct((height, channels, width), jnp.float32),
            jax.ShapeDtypeStruct((3 * channels, (height + 2) * width), jnp.bfloat16),
            jax.ShapeDtypeStruct((1, channels, width), jnp.bfloat16),
            jax.ShapeDtypeStruct((1, channels, width), jnp.bfloat16),
        ],
        compiler_params=pltpu.CompilerParams(vmem_limit_bytes=VMEM_LIMIT),
        cost_estimate=pl.CostEstimate(
            flops=flops, bytes_accessed=16 * 1024 * 1024, transcendentals=0
        ),
        name="conv_forward",
    )
    results = call(turns, *pieces, *rims, *halves)
    return list(results[:count]), *results[count:]


def slope_rows(factor, pieces, ends, slope):
    count = len(pieces)
    height, _, width = factor.shape
    depth = pieces[0].shape[1]

    def put(row, blocks):
        lanes = pl.ds(pl.multiple_of(row * width, width), width)
        for j in range(count):
            part_of = pl.ds(j * depth, depth)
            value = blocks[j].astype(jnp.float32) * factor[row, part_of, :]
            slope[part_of, lanes] = value.astype(jnp.bfloat16)

    def body(row, carry):
        put(row + 1, [piece[row] for piece in pieces])
        return carry

    put(0, [end[2] for end in ends])
    lax.fori_loop(0, height - 2, body, 0)
    put(height - 1, [end[3] for end in ends])


def correlate_body(first_tap, count, groups, rows, turn, stacked, *refs):
    if count:
        factor, pieces, ends = refs[0], refs[1 : 1 + count], refs[1 + count : 1 + 2 * count]
        shares, slope = refs[1 + 2 * count : -1], refs[-1]
    else:
        slope, shares = refs[0], refs[1:]
    channels, pixels = slope.shape
    width = stacked.shape[1] - pixels
    width = width // 2
    tap = first_tap + pl.program_id(0)
    tap_row, tap_col = tap // 3, lax.rem(tap, 3)
    if count:

        @pl.when(pl.program_id(0) == 0)
        def _():
            slope_rows(factor, pieces, ends, slope)

    source = stacked[
        pl.ds(pl.multiple_of(tap_col * channels, channels), channels),
        pl.ds(pl.multiple_of(tap_row * width, width), pixels),
    ]
    grads = lax.dot_general(
        source, slope[...], (((1,), (1,)), ((), ())), preferred_element_type=jnp.float32
    )
    size = channels // (groups * rows)
    for own in range(rows):

        @pl.when(turn[0] == own)
        def _():
            for j in range(rows):
                for group in range(groups):
                    start = (group * rows + (own - j) % rows) * size
                    shares[j][group, 0] = grads[start : start + size]


def correlate(taps, stacked, slope=None, factor=None, pieces=(), ends=()):
    first_tap, tap_count = taps
    channels = stacked.shape[0] // 3
    groups, rows = lax.axis_size("dp"), lax.axis_size("row")
    size = channels // (groups * rows)
    if slope is None:
        height, _, width = factor.shape
        pixels = height * width
        operands = [factor, *pieces, *ends]
        made = [jax.ShapeDtypeStruct((channels, pixels), jnp.bfloat16)]
    else:
        pixels = slope.shape[1]
        operands, made = [slope], []
    call = pl.pallas_call(
        functools.partial(correlate_body, first_tap, len(pieces), groups, rows),
        grid=(tap_count,),
        in_specs=[pl.BlockSpec(memory_space=pltpu.SMEM), whole(stacked.shape)]
        + [whole(operand.shape) for operand in operands],
        out_specs=[pl.BlockSpec((groups, 1, size, channels), lambda t: (0, t, 0, 0))] * rows
        + [whole(each.shape) for each in made],
        out_shape=[jax.ShapeDtypeStruct((groups, tap_count, size, channels), jnp.float32)] * rows
        + made,
        compiler_params=pltpu.CompilerParams(vmem_limit_bytes=VMEM_LIMIT),
        cost_estimate=pl.CostEstimate(
            flops=2 * tap_count * channels * channels * pixels,
            bytes_accessed=8 * 1024 * 1024,
            transcendentals=0,
        ),
    )
    turn = lax.axis_index("row").astype(jnp.int32)[None]
    results = call(turn, stacked, *operands)
    return (results[:rows], *results[rows:])


def padded_depth(depth):
    return -(-depth // 128) * 128


def turned_body(shares, *refs):
    halves, out = refs[:shares], refs[shares]
    _, depth, lanes = out.shape
    stride = lanes // 9
    total = halves[0].shape[2]
    both = [jnp.concatenate([half[0] for half in halves])]
    channels = both[0].shape[0]
    rows = []
    for start in range(0, total, 128):
        size = min(128, total - start)
        unit = (
            lax.broadcasted_iota(jnp.int32, (size, size), 0)
            == lax.broadcasted_iota(jnp.int32, (size, size), 1)
        ).astype(jnp.bfloat16)
        rows.append(
            lax.dot_general(
                unit,
                both[0][:, start : start + size],
                (((1,), (1,)), ((), ())),
                preferred_element_type=jnp.float32,
            )
        )
    turned = jnp.concatenate(rows)
    for tap in range(9):
        begin = (8 - tap) * depth
        value = turned[begin : begin + depth].astype(jnp.bfloat16)
        out[0, :, tap * stride : tap * stride + channels] = value
        if stride > channels:
            out[0, :, tap * stride + channels : (tap + 1) * stride] = jnp.zeros(
                (depth, stride - channels), jnp.bfloat16
            )


def turned(halves):
    shares = len(halves)
    blocks, outs, lanes = halves[0].shape
    depth = lanes // 9
    stride = padded_depth(outs * shares)
    return pl.pallas_call(
        functools.partial(turned_body, shares),
        grid=(blocks,),
        in_specs=[pl.BlockSpec((1, outs, lanes), lambda g: (g, 0, 0))] * shares,
        out_specs=pl.BlockSpec((1, depth, 9 * stride), lambda g: (g, 0, 0)),
        out_shape=jax.ShapeDtypeStruct((blocks, depth, 9 * stride), jnp.bfloat16),
        compiler_params=pltpu.CompilerParams(vmem_limit_bytes=VMEM_LIMIT),
        cost_estimate=pl.CostEstimate(
            flops=2 * 128 * blocks * outs * shares * lanes,
            bytes_accessed=4 * 1024 * 1024,
            transcendentals=0,
        ),
        name="turn_kernel",
    )(*halves)


def backward_body(count, shares, rows, turns, slope, above, below, kernels, *refs):
    outs, stacked = refs[:count], refs[count]
    channels = slope.shape[0]
    _, _, width = above.shape
    height = slope.shape[1] // width
    depth = channels // count
    size = depth // shares
    stride = stacked.shape[0] // 3
    step = pl.program_id(0)

    def in_share_order(wide):
        parts = []
        for at in range(shares):
            chosen = None
            for share in range(shares):
                value = jnp.concatenate(
                    [wide[j * depth + share * size : j * depth + (share + 1) * size] for j in range(count)]
                )
                here = turns[3] == (share - at) % shares
                chosen = value if chosen is None else jnp.where(here, value, chosen)
            parts.append(chosen)
        return jnp.concatenate(parts)

    def put(row, block):
        lanes = pl.ds(pl.multiple_of(row * width, width), width)
        wide = in_share_order(block.astype(jnp.float32))
        for copies, moved in enumerate((columns_moved(wide, -1), wide, columns_moved(wide, 1))):
            stacked[copies * stride : copies * stride + channels, lanes] = moved.astype(slope.dtype)

    @pl.when(step == 0)
    def _():
        if stride > channels:
            for copies in range(3):
                stacked[copies * stride + channels : (copies + 1) * stride, :] = jnp.zeros(
                    (stride - channels, stacked.shape[1]), stacked.dtype
                )
        for side, rim, row in ((0, above, 0), (1, below, height + 1)):
            blocks = []
            for j in range(count):
                start = lax.rem(turns[side] + j, count) * depth
                blocks.append(rim[0, pl.ds(pl.multiple_of(start, depth), depth), :])
            put(row, jnp.concatenate(blocks))

        def body(row, carry):
            lanes = pl.ds(pl.multiple_of(row * width, width), width)
            put(row + 1, slope[:, lanes])
            return carry

        lax.fori_loop(0, height, body, 0)

    windows = [
        stacked[:, pl.ds(pl.multiple_of((step * rows + a) * width, width), rows * width)]
        for a in range(3)
    ]
    order = [kernels[lax.rem(turns[2] + j, count)] for j in range(count)]
    grad = jnp.dot(
        jnp.concatenate(order), jnp.concatenate(windows), preferred_element_type=jnp.float32
    )
    for row in range(rows):
        lanes = slice(row * width, (row + 1) * width)
        for j in range(count):
            outs[j][row] = grad[j * depth : (j + 1) * depth, lanes].astype(outs[j].dtype)


def backward(turns, slope, above, below, kernels, count, slab):
    channels = slope.shape[0]
    width = above.shape[2]
    height = slope.shape[1] // width
    depth = channels // count
    rows = 4 if height % 4 == 0 else 1
    flops = 2 * 9 * channels * channels * height * width
    steps = height // rows
    return pl.pallas_call(
        functools.partial(backward_body, count, lax.axis_size("row"), rows),
        grid_spec=pltpu.PrefetchScalarGridSpec(
            num_scalar_prefetch=1,
            grid=(steps,),
            in_specs=[
                whole(slope.shape),
                whole(above.shape),
                whole(below.shape),
                whole(kernels.shape),
            ],
            out_specs=[pl.BlockSpec((rows, depth, width), lambda g, turns: (turns[4] * steps + g, 0, 0))]
            + [pl.BlockSpec((rows, depth, width), lambda g, _: (g, 0, 0))] * (count - 1),
            scratch_shapes=[pltpu.VMEM((kernels.shape[2] // 3, (height + 2) * width), jnp.bfloat16)],
        ),
        out_shape=[jax.ShapeDtypeStruct((slab, depth, width), jnp.float32)]
        + [jax.ShapeDtypeStruct((height, depth, width), jnp.bfloat16)] * (count - 1),
        compiler_params=pltpu.CompilerParams(vmem_limit_bytes=VMEM_LIMIT),
        cost_estimate=pl.CostEstimate(
            flops=flops, bytes_accessed=8 * 1024 * 1024, transcendentals=0
        ),
        name="conv_backward",
    )(turns, slope, above, below, kernels)


def gathered_kernel(kernel):
    dp, row = lax.axis_index("dp"), lax.axis_index("row")
    dps, chans, rows = (lax.axis_size(a) for a in ("dp", "chan", "row"))
    _, inner, outer = kernel.shape
    size = outer // rows
    mine = part(kernel, row, size, 2)
    mine = jnp.transpose(mine, (2, 0, 1)).reshape(size, 9 * inner)
    over_chan = jnp.concatenate([mine] + [receive(mine, "chan", j) for j in range(1, chans)], axis=0)
    over_dp = jnp.stack([over_chan] + [receive(over_chan, "dp", j) for j in range(1, dps)])
    if dps != chans:
        each = dps // chans
        over_dp = rotated(over_dp, (dps - dp) % dps, 0)
        over_dp = over_dp.reshape(chans, each, chans * size, 9, inner)
        over_dp = jnp.transpose(over_dp, (0, 2, 3, 1, 4)).reshape(chans, chans * size, 9 * each * inner)
    return [over_dp] + [receive(over_dp, "row", j) for j in range(1, rows)]


def summed_over_images(shares):
    dp = lax.axis_index("dp")
    dps, chans, rows = (lax.axis_size(a) for a in ("dp", "chan", "row"))
    halves = shares[0]
    for j in range(1, rows):
        halves = halves + receive(shares[j], "row", j)

    def of_dp(ahead):
        if dps == chans:
            return halves[ahead % dps]
        return lax.dynamic_index_in_dim(halves, (dp + ahead) % dps, 0, keepdims=False)

    total = of_dp(0)
    for j in range(1, dps):
        total = total + receive(of_dp(-j), "dp", j)
    return total


def kernel_grad_of(total, inner, outer):
    row = lax.axis_index("row")
    chans, rows = lax.axis_size("chan"), lax.axis_size("row")
    taps, share, channels = total.shape
    total = jnp.transpose(total, (2, 0, 1)).reshape(channels, taps * share)
    own = total[:outer]
    for j in range(1, chans):
        start = (chans - j) * outer
        own = own + receive(total[start : start + outer], "chan", j)
    both = jnp.stack([own] + [receive(own, "row", j) for j in range(1, rows)])
    both = rotated(both, (rows - row) % rows, 0).reshape(rows, outer, taps, share)
    return jnp.transpose(both, (2, 0, 3, 1)).reshape(taps, inner, outer)


def shards(images, kernel, cotangent):
    row, chan = lax.axis_index("row"), lax.axis_index("chan")
    rows, chans = lax.axis_size("row"), lax.axis_size("chan")
    _, slab, _, _ = images.shape
    height = slab // chans
    images, cotangent = images[0], cotangent[0]

    def home(ahead):
        return home_of(row, (chan + ahead) % chans, chans)

    def to_homes(array, size):
        return [part(array, home(0), size, 0)] + [
            receive(part(array, home(-j), size, 0), "chan", j) for j in range(1, chans)
        ]

    halves = gathered_kernel(kernel)
    pieces = to_homes(images, height)
    if rows == 2:
        edge = jnp.where(row == 0, images[slab - 1 :], images[:1])
        edge = receive(edge, "row", 1)
        low = jnp.where(row == 0, jnp.zeros_like(edge), edge)
        high = jnp.where(row == 0, edge, jnp.zeros_like(edge))
    else:
        low = lax.ppermute(images[slab - 1 :], "row", [(i, i + 1) for i in range(rows - 1)])
        high = lax.ppermute(images[:1], "row", [(i + 1, i) for i in range(rows - 1)])

    def rim_of(at):
        begin = at * height
        above = part(images, jnp.maximum(begin - 1, 0), 1, 0)
        below = part(images, jnp.minimum(begin + height, slab - 1), 1, 0)
        return jnp.concatenate(
            [
                jnp.where(at == 0, low, above),
                jnp.where(at == chans - 1, high, below),
                part(cotangent, begin, 1, 0),
                part(cotangent, begin + height - 1, 1, 0),
            ]
        )

    rims = [rim_of(home(0))]
    rims += [receive(rim_of(home(-j)), "chan", j) for j in range(1, chans)]

    def inside(ahead):
        return lax.dynamic_slice_in_dim(cotangent, home(ahead) * height + 1, height - 2, 0)

    cotangents = [inside(0)] + [receive(inside(-j), "chan", j) for j in range(1, chans)]

    shift = (chan - stacking_base()) % chans
    place_at = home(0)
    forth = jnp.where(row % 2 == 0, 1, chans - 1)
    above_turn = jnp.where(place_at == 0, 0, forth)
    below_turn = jnp.where(place_at == chans - 1, 0, chans - forth)
    turns = jnp.stack([shift, row, place_at]).astype(jnp.int32)
    back_turns = jnp.stack([above_turn, below_turn, shift, row, place_at]).astype(jnp.int32)

    results = forward(turns, pieces, rims, halves, slab)
    activated, factor, stacked, first, last = results
    back_kernel = turned(halves)

    def snake(place_at):
        r, k = place_at // chans, place_at % chans
        return (k if r % 2 == 0 else chans - 1 - k) * rows + r

    line = [(snake(i), snake(i + 1)) for i in range(rows * chans - 1)]
    above = lax.ppermute(last, ("chan", "row"), line)
    below = lax.ppermute(first, ("chan", "row"), [(b, a) for a, b in line])

    lead, slope = correlate((0, 6), stacked, None, factor, cotangents, rims)
    lead = summed_over_images(lead)
    input_grads = list(backward(back_turns, slope, above, below, back_kernel, chans, slab))
    slope, input_grads[1] = lax.optimization_barrier((slope, input_grads[1]))
    (rest,) = correlate((6, 3), stacked, slope)
    rest = summed_over_images(rest)
    inner, outer = kernel.shape[1:]
    kernel_grad = jnp.concatenate([kernel_grad_of(lead, inner, outer), kernel_grad_of(rest, inner, outer)])

    def to_owners(blocks):
        out = blocks[0]
        for j in range(1, chans):
            arrived = receive(blocks[j], "chan", chans - j).astype(out.dtype)
            out = lax.dynamic_update_slice_in_dim(out, arrived, home(-j) * height, 0)
        return out[None]

    return to_owners(activated), to_owners(input_grads), kernel_grad


def solution(mesh):
    placed = (P("dp", "row", "chan", None), P(None, "dp", "chan"), P("dp", "row", "chan", None))
    return jax.shard_map(
        shards,
        mesh=mesh,
        in_specs=placed,
        out_specs=(
            P("dp", "row", "chan", None),
            P("dp", "row", "chan", None),
            P(None, "dp", "chan"),
        ),
        check_vma=False,
    )
```

```python
import functools

import jax
import jax.numpy as jnp
from jax import lax
from jax.experimental import pallas as pl
from jax.experimental.pallas import tpu as pltpu
from jax.sharding import PartitionSpec as P


VMEM_LIMIT = 60 * 1024 * 1024


def receive(block, axis, ahead):
    count = lax.axis_size(axis)
    return lax.ppermute(block, axis, [(i, (i - ahead) % count) for i in range(count)])


def swapped(block, axis, bit):
    return lax.ppermute(block, axis, [(i, i ^ bit) for i in range(lax.axis_size(axis))])


def gathered_over_chan(mine):
    chans = lax.axis_size("chan")
    if chans != 4:
        return jnp.concatenate([mine] + [receive(mine, "chan", j) for j in range(1, chans)])
    size = mine.shape[0]
    even = lax.axis_index("chan") % 2 == 0
    opposite = swapped(mine, "chan", 2)
    beside = swapped(jnp.concatenate([mine, opposite]), "chan", 1)
    near, far = beside[:size], beside[size:]
    return jnp.concatenate([mine, jnp.where(even, near, far), opposite, jnp.where(even, far, near)])


def summed_over_chan(total, outer, in_steps):
    chans = lax.axis_size("chan")
    blocks = [total[j * outer : (j + 1) * outer] for j in range(chans)]
    if chans != 4 or not in_steps:
        own = blocks[0]
        for j in range(1, chans):
            own = own + receive(blocks[chans - j], "chan", j)
        return own
    odd = lax.axis_index("chan") % 2 == 1
    beside = swapped(jnp.concatenate([blocks[1], blocks[3]]), "chan", 1)
    first, second = beside[:outer], beside[outer:]
    other = blocks[2] + jnp.where(odd, second, first)
    return blocks[0] + jnp.where(odd, first, second) + swapped(other, "chan", 2)


def home_of(row, chan, chans):
    return jnp.where(row % 2 == 0, chan, chans - 1 - chan)


def part(array, index, size, axis):
    return lax.dynamic_slice_in_dim(array, index * size, size, axis=axis)


def rotated(array, start, axis):
    twice = jnp.concatenate([array, array], axis=axis)
    return lax.dynamic_slice_in_dim(twice, start, array.shape[axis], axis=axis)


def stacking_base():
    matched = lax.axis_size("dp") == lax.axis_size("chan")
    return lax.axis_index("dp") if matched else jnp.int32(0)


def columns_moved(block, step):
    width = block.shape[-1]
    lane = lax.broadcasted_iota(jnp.int32, block.shape, block.ndim - 1)
    if step < 0:
        moved = pltpu.roll(block, 1, block.ndim - 1)
        return jnp.where(lane == 0, jnp.zeros_like(block), moved)
    moved = pltpu.roll(block, width - 1, block.ndim - 1)
    return jnp.where(lane == width - 1, jnp.zeros_like(block), moved)


def place(stacked, channel, row, block, channels):
    depth, width = block.shape
    lanes = pl.ds(pl.multiple_of(row * width, width), width)
    wide = block.astype(jnp.float32)

    def below(copies):
        start = copies * channels + channel
        return pl.ds(start if isinstance(channel, int) else pl.multiple_of(start, 16), depth)

    stacked[below(0), lanes] = columns_moved(wide, -1).astype(block.dtype)
    stacked[below(1), lanes] = block
    stacked[below(2), lanes] = columns_moved(wide, 1).astype(block.dtype)


def window(stacked, tap_row, tap_col, channel, depth, first, rows, width, channels):
    start = pl.multiple_of((first + tap_row) * width, width)
    return stacked[tap_col * channels + channel : tap_col * channels + channel + depth, pl.ds(start, rows * width)]


def forward_taps(halves, stacked, first, rows, width):
    count = halves[0].shape[0]
    depth = halves[0].shape[2] // 9
    total = None
    for block in range(count):
        windows = [
            window(stacked, a, b, block * depth, depth, first, rows, width, count * depth)
            for a in range(3)
            for b in range(3)
        ]
        term = jnp.dot(
            jnp.concatenate([half[block] for half in halves]),
            jnp.concatenate(windows),
            preferred_element_type=jnp.float32,
        )
        total = term if total is None else total + term
    return total


def forward_body(count, shares, rows, turns, *refs):
    pieces, rims = refs[:count], refs[count : 2 * count]
    halves = refs[2 * count : 2 * count + shares]
    outs = refs[2 * count + shares : 3 * count + shares]
    factor, stacked, first, last = refs[3 * count + shares :]
    height, depth, width = pieces[0].shape
    channels = count * depth
    step = pl.program_id(0)

    @pl.when(step == 0)
    def _():
        slots = [lax.rem(turns[0] + j, count) * depth for j in range(count)]
        for j in range(count):
            place(stacked, slots[j], 0, rims[j][0], channels)
            place(stacked, slots[j], height + 1, rims[j][1], channels)

        def body(row, carry):
            for j in range(count):
                place(stacked, slots[j], row + 1, pieces[j][row], channels)
            return carry

        lax.fori_loop(0, height, body, 0)

    mixed = forward_taps(halves, stacked, step * rows, rows, width)
    size = depth // shares
    for j in range(count):
        parts = []
        for share in range(shares):
            chosen = None
            for at in range(shares):
                start = at * count * size + j * size
                value = mixed[start : start + size]
                here = turns[1] == (share - at) % shares
                chosen = value if chosen is None else jnp.where(here, value, chosen)
            parts.append(chosen)
        pre = jnp.concatenate(parts) if shares > 1 else parts[0]
        sigma = jax.nn.sigmoid(pre)
        activated = (pre * sigma).astype(jnp.bfloat16)
        slope = sigma * (1.0 + pre * (1.0 - sigma))
        for row in range(rows):
            lanes = slice(row * width, (row + 1) * width)
            factor[row, j * depth : (j + 1) * depth, :] = slope[:, lanes]
            outs[j][row] = activated[:, lanes]

    def end(out, side, row):
        for j in range(count):
            part_of = slice(j * depth, (j + 1) * depth)
            value = rims[j][side].astype(jnp.float32) * factor[row, part_of, :]
            out[0, part_of, :] = value.astype(jnp.bfloat16)

    @pl.when(step == 0)
    def _():
        end(first, 2, 0)

    @pl.when(step == pl.num_programs(0) - 1)
    def _():
        end(last, 3, rows - 1)


def whole(shape):
    return pl.BlockSpec(shape, lambda *_: (0,) * len(shape), pipeline_mode=pl.Buffered(1))


def forward(turns, pieces, rims, halves, slab):
    count = len(pieces)
    height, depth, width = pieces[0].shape
    channels = count * depth
    rows = 4 if height % 4 == 0 else 1
    flops = 2 * 9 * channels * channels * height * width
    steps = height // rows
    call = pl.pallas_call(
        functools.partial(forward_body, count, len(halves), rows),
        grid_spec=pltpu.PrefetchScalarGridSpec(
            num_scalar_prefetch=1,
            grid=(steps,),
            in_specs=[whole(pieces[0].shape)] * count
            + [whole(rims[0].shape)] * count
            + [whole(halves[0].shape)] * len(halves),
            out_specs=[pl.BlockSpec((rows, depth, width), lambda g, turns: (turns[2] * steps + g, 0, 0))]
            + [pl.BlockSpec((rows, depth, width), lambda g, _: (g, 0, 0))] * (count - 1)
            + [
                pl.BlockSpec((rows, channels, width), lambda g, _: (g, 0, 0)),
                whole((3 * channels, (height + 2) * width)),
                whole((1, channels, width)),
                whole((1, channels, width)),
            ],
        ),
        out_shape=[
            jax.ShapeDtypeStruct((height if j else slab, depth, width), jnp.bfloat16)
            for j in range(count)
        ]
        + [
            jax.ShapeDtypeStruct((height, channels, width), jnp.float32),
            jax.ShapeDtypeStruct((3 * channels, (height + 2) * width), jnp.bfloat16),
            jax.ShapeDtypeStruct((1, channels, width), jnp.bfloat16),
            jax.ShapeDtypeStruct((1, channels, width), jnp.bfloat16),
        ],
        compiler_params=pltpu.CompilerParams(vmem_limit_bytes=VMEM_LIMIT),
        cost_estimate=pl.CostEstimate(
            flops=flops, bytes_accessed=16 * 1024 * 1024, transcendentals=0
        ),
        name="conv_forward",
    )
    results = call(turns, *pieces, *rims, *halves)
    return list(results[:count]), *results[count:]


def slope_rows(factor, pieces, ends, slope):
    count = len(pieces)
    height, _, width = factor.shape
    depth = pieces[0].shape[1]

    def put(row, blocks):
        lanes = pl.ds(pl.multiple_of(row * width, width), width)
        for j in range(count):
            part_of = pl.ds(j * depth, depth)
            value = blocks[j].astype(jnp.float32) * factor[row, part_of, :]
            slope[part_of, lanes] = value.astype(jnp.bfloat16)

    def body(row, carry):
        put(row + 1, [piece[row] for piece in pieces])
        return carry

    put(0, [end[2] for end in ends])
    lax.fori_loop(0, height - 2, body, 0)
    put(height - 1, [end[3] for end in ends])


def correlate_body(first_tap, count, groups, rows, turn, stacked, *refs):
    if count:
        factor, pieces, ends = refs[0], refs[1 : 1 + count], refs[1 + count : 1 + 2 * count]
        shares, slope = refs[1 + 2 * count : -1], refs[-1]
    else:
        slope, shares = refs[0], refs[1:]
    channels, pixels = slope.shape
    width = stacked.shape[1] - pixels
    width = width // 2
    tap = first_tap + pl.program_id(0)
    tap_row, tap_col = tap // 3, lax.rem(tap, 3)
    if count:

        @pl.when(pl.program_id(0) == 0)
        def _():
            slope_rows(factor, pieces, ends, slope)

    source = stacked[
        pl.ds(pl.multiple_of(tap_col * channels, channels), channels),
        pl.ds(pl.multiple_of(tap_row * width, width), pixels),
    ]
    grads = lax.dot_general(
        source, slope[...], (((1,), (1,)), ((), ())), preferred_element_type=jnp.float32
    )
    size = channels // (groups * rows)
    for own in range(rows):

        @pl.when(turn[0] == own)
        def _():
            for j in range(rows):
                for group in range(groups):
                    start = (group * rows + (own - j) % rows) * size
                    shares[j][group, 0] = grads[start : start + size]


def correlate(taps, stacked, slope=None, factor=None, pieces=(), ends=()):
    first_tap, tap_count = taps
    channels = stacked.shape[0] // 3
    groups, rows = lax.axis_size("dp"), lax.axis_size("row")
    size = channels // (groups * rows)
    if slope is None:
        height, _, width = factor.shape
        pixels = height * width
        operands = [factor, *pieces, *ends]
        made = [jax.ShapeDtypeStruct((channels, pixels), jnp.bfloat16)]
    else:
        pixels = slope.shape[1]
        operands, made = [slope], []
    call = pl.pallas_call(
        functools.partial(correlate_body, first_tap, len(pieces), groups, rows),
        grid=(tap_count,),
        in_specs=[pl.BlockSpec(memory_space=pltpu.SMEM), whole(stacked.shape)]
        + [whole(operand.shape) for operand in operands],
        out_specs=[pl.BlockSpec((groups, 1, size, channels), lambda t: (0, t, 0, 0))] * rows
        + [whole(each.shape) for each in made],
        out_shape=[jax.ShapeDtypeStruct((groups, tap_count, size, channels), jnp.float32)] * rows
        + made,
        compiler_params=pltpu.CompilerParams(vmem_limit_bytes=VMEM_LIMIT),
        cost_estimate=pl.CostEstimate(
            flops=2 * tap_count * channels * channels * pixels,
            bytes_accessed=8 * 1024 * 1024,
            transcendentals=0,
        ),
    )
    turn = lax.axis_index("row").astype(jnp.int32)[None]
    results = call(turn, stacked, *operands)
    return (results[:rows], *results[rows:])


def padded_depth(depth):
    return -(-depth // 128) * 128


def turned_body(shares, *refs):
    halves, out = refs[:shares], refs[shares]
    _, depth, lanes = out.shape
    stride = lanes // 9
    total = halves[0].shape[2]
    both = [jnp.concatenate([half[0] for half in halves])]
    channels = both[0].shape[0]
    rows = []
    for start in range(0, total, 128):
        size = min(128, total - start)
        unit = (
            lax.broadcasted_iota(jnp.int32, (size, size), 0)
            == lax.broadcasted_iota(jnp.int32, (size, size), 1)
        ).astype(jnp.bfloat16)
        rows.append(
            lax.dot_general(
                unit,
                both[0][:, start : start + size],
                (((1,), (1,)), ((), ())),
                preferred_element_type=jnp.float32,
            )
        )
    turned = jnp.concatenate(rows)
    for tap in range(9):
        begin = (8 - tap) * depth
        value = turned[begin : begin + depth].astype(jnp.bfloat16)
        out[0, :, tap * stride : tap * stride + channels] = value
        if stride > channels:
            out[0, :, tap * stride + channels : (tap + 1) * stride] = jnp.zeros(
                (depth, stride - channels), jnp.bfloat16
            )


def turned(halves):
    shares = len(halves)
    blocks, outs, lanes = halves[0].shape
    depth = lanes // 9
    stride = padded_depth(outs * shares)
    return pl.pallas_call(
        functools.partial(turned_body, shares),
        grid=(blocks,),
        in_specs=[pl.BlockSpec((1, outs, lanes), lambda g: (g, 0, 0))] * shares,
        out_specs=pl.BlockSpec((1, depth, 9 * stride), lambda g: (g, 0, 0)),
        out_shape=jax.ShapeDtypeStruct((blocks, depth, 9 * stride), jnp.bfloat16),
        compiler_params=pltpu.CompilerParams(vmem_limit_bytes=VMEM_LIMIT),
        cost_estimate=pl.CostEstimate(
            flops=2 * 128 * blocks * outs * shares * lanes,
            bytes_accessed=4 * 1024 * 1024,
            transcendentals=0,
        ),
        name="turn_kernel",
    )(*halves)


def backward_body(count, shares, rows, turns, slope, above, below, kernels, *refs):
    outs, stacked = refs[:count], refs[count]
    channels = slope.shape[0]
    _, _, width = above.shape
    height = slope.shape[1] // width
    depth = channels // count
    size = depth // shares
    stride = stacked.shape[0] // 3
    step = pl.program_id(0)

    def in_share_order(wide):
        parts = []
        for at in range(shares):
            chosen = None
            for share in range(shares):
                value = jnp.concatenate(
                    [wide[j * depth + share * size : j * depth + (share + 1) * size] for j in range(count)]
                )
                here = turns[3] == (share - at) % shares
                chosen = value if chosen is None else jnp.where(here, value, chosen)
            parts.append(chosen)
        return jnp.concatenate(parts)

    def put(row, block):
        lanes = pl.ds(pl.multiple_of(row * width, width), width)
        wide = in_share_order(block.astype(jnp.float32))
        for copies, moved in enumerate((columns_moved(wide, -1), wide, columns_moved(wide, 1))):
            stacked[copies * stride : copies * stride + channels, lanes] = moved.astype(slope.dtype)

    @pl.when(step == 0)
    def _():
        if stride > channels:
            for copies in range(3):
                stacked[copies * stride + channels : (copies + 1) * stride, :] = jnp.zeros(
                    (stride - channels, stacked.shape[1]), stacked.dtype
                )
        for side, rim, row in ((0, above, 0), (1, below, height + 1)):
            blocks = []
            for j in range(count):
                start = lax.rem(turns[side] + j, count) * depth
                blocks.append(rim[0, pl.ds(pl.multiple_of(start, depth), depth), :])
            put(row, jnp.concatenate(blocks))

        def body(row, carry):
            lanes = pl.ds(pl.multiple_of(row * width, width), width)
            put(row + 1, slope[:, lanes])
            return carry

        lax.fori_loop(0, height, body, 0)

    windows = [
        stacked[:, pl.ds(pl.multiple_of((step * rows + a) * width, width), rows * width)]
        for a in range(3)
    ]
    order = [kernels[lax.rem(turns[2] + j, count)] for j in range(count)]
    grad = jnp.dot(
        jnp.concatenate(order), jnp.concatenate(windows), preferred_element_type=jnp.float32
    )
    for row in range(rows):
        lanes = slice(row * width, (row + 1) * width)
        for j in range(count):
            outs[j][row] = grad[j * depth : (j + 1) * depth, lanes].astype(outs[j].dtype)


def backward(turns, slope, above, below, kernels, count, slab):
    channels = slope.shape[0]
    width = above.shape[2]
    height = slope.shape[1] // width
    depth = channels // count
    rows = 4 if height % 4 == 0 else 1
    flops = 2 * 9 * channels * channels * height * width
    steps = height // rows
    return pl.pallas_call(
        functools.partial(backward_body, count, lax.axis_size("row"), rows),
        grid_spec=pltpu.PrefetchScalarGridSpec(
            num_scalar_prefetch=1,
            grid=(steps,),
            in_specs=[
                whole(slope.shape),
                whole(above.shape),
                whole(below.shape),
                whole(kernels.shape),
            ],
            out_specs=[pl.BlockSpec((rows, depth, width), lambda g, turns: (turns[4] * steps + g, 0, 0))]
            + [pl.BlockSpec((rows, depth, width), lambda g, _: (g, 0, 0))] * (count - 1),
            scratch_shapes=[pltpu.VMEM((kernels.shape[2] // 3, (height + 2) * width), jnp.bfloat16)],
        ),
        out_shape=[jax.ShapeDtypeStruct((slab, depth, width), jnp.float32)]
        + [jax.ShapeDtypeStruct((height, depth, width), jnp.bfloat16)] * (count - 1),
        compiler_params=pltpu.CompilerParams(vmem_limit_bytes=VMEM_LIMIT),
        cost_estimate=pl.CostEstimate(
            flops=flops, bytes_accessed=8 * 1024 * 1024, transcendentals=0
        ),
        name="conv_backward",
    )(turns, slope, above, below, kernels)


def gathered_kernel(kernel):
    dp, row = lax.axis_index("dp"), lax.axis_index("row")
    dps, chans, rows = (lax.axis_size(a) for a in ("dp", "chan", "row"))
    _, inner, outer = kernel.shape
    size = outer // rows
    mine = part(kernel, row, size, 2)
    mine = jnp.transpose(mine, (2, 0, 1)).reshape(size, 9 * inner)
    over_chan = gathered_over_chan(mine)
    over_dp = jnp.stack([over_chan] + [receive(over_chan, "dp", j) for j in range(1, dps)])
    if dps != chans:
        each = dps // chans
        over_dp = rotated(over_dp, (dps - dp) % dps, 0)
        over_dp = over_dp.reshape(chans, each, chans * size, 9, inner)
        over_dp = jnp.transpose(over_dp, (0, 2, 3, 1, 4)).reshape(chans, chans * size, 9 * each * inner)
    return [over_dp] + [receive(over_dp, "row", j) for j in range(1, rows)]


def summed_over_images(shares):
    dp = lax.axis_index("dp")
    dps, chans, rows = (lax.axis_size(a) for a in ("dp", "chan", "row"))
    halves = shares[0]
    for j in range(1, rows):
        halves = halves + receive(shares[j], "row", j)

    def of_dp(ahead):
        if dps == chans:
            return halves[ahead % dps]
        return lax.dynamic_index_in_dim(halves, (dp + ahead) % dps, 0, keepdims=False)

    total = of_dp(0)
    for j in range(1, dps):
        total = total + receive(of_dp(-j), "dp", j)
    return total


def kernel_grad_of(total, inner, outer, in_steps):
    row, rows = lax.axis_index("row"), lax.axis_size("row")
    taps, share, channels = total.shape
    total = jnp.transpose(total, (2, 0, 1)).reshape(channels, taps * share)
    own = summed_over_chan(total, outer, in_steps)
    both = jnp.stack([own] + [receive(own, "row", j) for j in range(1, rows)])
    both = rotated(both, (rows - row) % rows, 0).reshape(rows, outer, taps, share)
    return jnp.transpose(both, (2, 0, 3, 1)).reshape(taps, inner, outer)


def shards(images, kernel, cotangent):
    row, chan = lax.axis_index("row"), lax.axis_index("chan")
    rows, chans = lax.axis_size("row"), lax.axis_size("chan")
    _, slab, _, _ = images.shape
    height = slab // chans
    images, cotangent = images[0], cotangent[0]

    def home(ahead):
        return home_of(row, (chan + ahead) % chans, chans)

    def to_homes(array, size):
        return [part(array, home(0), size, 0)] + [
            receive(part(array, home(-j), size, 0), "chan", j) for j in range(1, chans)
        ]

    halves = gathered_kernel(kernel)
    pieces = to_homes(images, height)
    if rows == 2:
        edge = jnp.where(row == 0, images[slab - 1 :], images[:1])
        edge = receive(edge, "row", 1)
        low = jnp.where(row == 0, jnp.zeros_like(edge), edge)
        high = jnp.where(row == 0, edge, jnp.zeros_like(edge))
    else:
        low = lax.ppermute(images[slab - 1 :], "row", [(i, i + 1) for i in range(rows - 1)])
        high = lax.ppermute(images[:1], "row", [(i + 1, i) for i in range(rows - 1)])

    def rim_of(at):
        begin = at * height
        above = part(images, jnp.maximum(begin - 1, 0), 1, 0)
        below = part(images, jnp.minimum(begin + height, slab - 1), 1, 0)
        return jnp.concatenate(
            [
                jnp.where(at == 0, low, above),
                jnp.where(at == chans - 1, high, below),
                part(cotangent, begin, 1, 0),
                part(cotangent, begin + height - 1, 1, 0),
            ]
        )

    rims = [rim_of(home(0))]
    rims += [receive(rim_of(home(-j)), "chan", j) for j in range(1, chans)]

    def inside(ahead):
        return lax.dynamic_slice_in_dim(cotangent, home(ahead) * height + 1, height - 2, 0)

    cotangents = [inside(0)] + [receive(inside(-j), "chan", j) for j in range(1, chans)]

    shift = (chan - stacking_base()) % chans
    place_at = home(0)
    forth = jnp.where(row % 2 == 0, 1, chans - 1)
    above_turn = jnp.where(place_at == 0, 0, forth)
    below_turn = jnp.where(place_at == chans - 1, 0, chans - forth)
    turns = jnp.stack([shift, row, place_at]).astype(jnp.int32)
    back_turns = jnp.stack([above_turn, below_turn, shift, row, place_at]).astype(jnp.int32)

    results = forward(turns, pieces, rims, halves, slab)
    activated, factor, stacked, first, last = results
    back_kernel = turned(halves)

    def snake(place_at):
        r, k = place_at // chans, place_at % chans
        return (k if r % 2 == 0 else chans - 1 - k) * rows + r

    line = [(snake(i), snake(i + 1)) for i in range(rows * chans - 1)]
    above = lax.ppermute(last, ("chan", "row"), line)
    below = lax.ppermute(first, ("chan", "row"), [(b, a) for a, b in line])

    lead, slope = correlate((0, 6), stacked, None, factor, cotangents, rims)
    lead = summed_over_images(lead)
    input_grads = list(backward(back_turns, slope, above, below, back_kernel, chans, slab))
    slope, input_grads[1] = lax.optimization_barrier((slope, input_grads[1]))
    (rest,) = correlate((6, 3), stacked, slope)
    rest = summed_over_images(rest)
    inner, outer = kernel.shape[1:]
    kernel_grad = jnp.concatenate([kernel_grad_of(lead, inner, outer, True), kernel_grad_of(rest, inner, outer, False)])

    def to_owners(blocks):
        out = blocks[0]
        for j in range(1, chans):
            arrived = receive(blocks[j], "chan", chans - j).astype(out.dtype)
            out = lax.dynamic_update_slice_in_dim(out, arrived, home(-j) * height, 0)
        return out[None]

    return to_owners(activated), to_owners(input_grads), kernel_grad


def solution(mesh):
    placed = (P("dp", "row", "chan", None), P(None, "dp", "chan"), P("dp", "row", "chan", None))
    return jax.shard_map(
        shards,
        mesh=mesh,
        in_specs=placed,
        out_specs=(
            P("dp", "row", "chan", None),
            P("dp", "row", "chan", None),
            P(None, "dp", "chan"),
        ),
        check_vma=False,
    )
```

```python
import functools

import jax
import jax.numpy as jnp
from jax import lax
from jax.experimental import pallas as pl
from jax.experimental.pallas import tpu as pltpu
from jax.sharding import PartitionSpec as P


VMEM_LIMIT = 60 * 1024 * 1024


def receive(block, axis, ahead):
    count = lax.axis_size(axis)
    return lax.ppermute(block, axis, [(i, (i - ahead) % count) for i in range(count)])


def home_of(row, chan, chans):
    return jnp.where(row % 2 == 0, chan, chans - 1 - chan)


def part(array, index, size, axis):
    return lax.dynamic_slice_in_dim(array, index * size, size, axis=axis)


def rotated(array, start, axis):
    twice = jnp.concatenate([array, array], axis=axis)
    return lax.dynamic_slice_in_dim(twice, start, array.shape[axis], axis=axis)


def stacking_base():
    matched = lax.axis_size("dp") == lax.axis_size("chan")
    return lax.axis_index("dp") if matched else jnp.int32(0)


def columns_moved(block, step):
    width = block.shape[-1]
    lane = lax.broadcasted_iota(jnp.int32, block.shape, block.ndim - 1)
    if step < 0:
        moved = pltpu.roll(block, 1, block.ndim - 1)
        return jnp.where(lane == 0, jnp.zeros_like(block), moved)
    moved = pltpu.roll(block, width - 1, block.ndim - 1)
    return jnp.where(lane == width - 1, jnp.zeros_like(block), moved)


def place(stacked, channel, row, block, channels):
    depth, width = block.shape
    lanes = pl.ds(pl.multiple_of(row * width, width), width)
    wide = block.astype(jnp.float32)

    def below(copies):
        start = copies * channels + channel
        return pl.ds(start if isinstance(channel, int) else pl.multiple_of(start, 16), depth)

    stacked[below(0), lanes] = columns_moved(wide, -1).astype(block.dtype)
    stacked[below(1), lanes] = block
    stacked[below(2), lanes] = columns_moved(wide, 1).astype(block.dtype)


def window(stacked, tap_row, tap_col, channel, depth, first, rows, width, channels):
    start = pl.multiple_of((first + tap_row) * width, width)
    return stacked[tap_col * channels + channel : tap_col * channels + channel + depth, pl.ds(start, rows * width)]


def forward_taps(halves, stacked, first, rows, width):
    count = halves[0].shape[0]
    depth = halves[0].shape[2] // 9
    total = None
    for block in range(count):
        windows = [
            window(stacked, a, b, block * depth, depth, first, rows, width, count * depth)
            for a in range(3)
            for b in range(3)
        ]
        term = jnp.dot(
            jnp.concatenate([half[block] for half in halves]),
            jnp.concatenate(windows),
            preferred_element_type=jnp.float32,
        )
        total = term if total is None else total + term
    return total


def forward_body(count, shares, rows, turns, *refs):
    pieces, rims = refs[:count], refs[count : 2 * count]
    halves = refs[2 * count : 2 * count + shares]
    outs = refs[2 * count + shares : 3 * count + shares]
    factor, stacked, first, last = refs[3 * count + shares :]
    height, depth, width = pieces[0].shape
    channels = count * depth
    step = pl.program_id(0)

    @pl.when(step == 0)
    def _():
        slots = [lax.rem(turns[0] + j, count) * depth for j in range(count)]
        for j in range(count):
            place(stacked, slots[j], 0, rims[j][0], channels)
            place(stacked, slots[j], height + 1, rims[j][1], channels)

        def body(row, carry):
            for j in range(count):
                place(stacked, slots[j], row + 1, pieces[j][row], channels)
            return carry

        lax.fori_loop(0, height, body, 0)

    mixed = forward_taps(halves, stacked, step * rows, rows, width)
    size = depth // shares
    for j in range(count):
        parts = []
        for share in range(shares):
            chosen = None
            for at in range(shares):
                start = at * count * size + j * size
                value = mixed[start : start + size]
                here = turns[1] == (share - at) % shares
                chosen = value if chosen is None else jnp.where(here, value, chosen)
            parts.append(chosen)
        pre = jnp.concatenate(parts) if shares > 1 else parts[0]
        sigma = jax.nn.sigmoid(pre)
        activated = (pre * sigma).astype(jnp.bfloat16)
        slope = sigma * (1.0 + pre * (1.0 - sigma))
        for row in range(rows):
            lanes = slice(row * width, (row + 1) * width)
            factor[row, j * depth : (j + 1) * depth, :] = slope[:, lanes]
            outs[j][row] = activated[:, lanes]

    def end(out, side, row):
        for j in range(count):
            part_of = slice(j * depth, (j + 1) * depth)
            value = rims[j][side].astype(jnp.float32) * factor[row, part_of, :]
            out[0, part_of, :] = value.astype(jnp.bfloat16)

    @pl.when(step == 0)
    def _():
        end(first, 2, 0)

    @pl.when(step == pl.num_programs(0) - 1)
    def _():
        end(last, 3, rows - 1)


def whole(shape):
    return pl.BlockSpec(shape, lambda *_: (0,) * len(shape), pipeline_mode=pl.Buffered(1))


def forward(turns, pieces, rims, halves, slab):
    count = len(pieces)
    height, depth, width = pieces[0].shape
    channels = count * depth
    rows = 4 if height % 4 == 0 else 1
    flops = 2 * 9 * channels * channels * height * width
    steps = height // rows
    call = pl.pallas_call(
        functools.partial(forward_body, count, len(halves), rows),
        grid_spec=pltpu.PrefetchScalarGridSpec(
            num_scalar_prefetch=1,
            grid=(steps,),
            in_specs=[whole(pieces[0].shape)] * count
            + [whole(rims[0].shape)] * count
            + [whole(halves[0].shape)] * len(halves),
            out_specs=[pl.BlockSpec((rows, depth, width), lambda g, turns: (turns[2] * steps + g, 0, 0))]
            + [pl.BlockSpec((rows, depth, width), lambda g, _: (g, 0, 0))] * (count - 1)
            + [
                pl.BlockSpec((rows, channels, width), lambda g, _: (g, 0, 0)),
                whole((3 * channels, (height + 2) * width)),
                whole((1, channels, width)),
                whole((1, channels, width)),
            ],
        ),
        out_shape=[
            jax.ShapeDtypeStruct((height if j else slab, depth, width), jnp.bfloat16)
            for j in range(count)
        ]
        + [
            jax.ShapeDtypeStruct((height, channels, width), jnp.float32),
            jax.ShapeDtypeStruct((3 * channels, (height + 2) * width), jnp.bfloat16),
            jax.ShapeDtypeStruct((1, channels, width), jnp.bfloat16),
            jax.ShapeDtypeStruct((1, channels, width), jnp.bfloat16),
        ],
        compiler_params=pltpu.CompilerParams(vmem_limit_bytes=VMEM_LIMIT),
        cost_estimate=pl.CostEstimate(
            flops=flops, bytes_accessed=16 * 1024 * 1024, transcendentals=0
        ),
        name="conv_forward",
    )
    results = call(turns, *pieces, *rims, *halves)
    return list(results[:count]), *results[count:]


def slope_rows(factor, pieces, ends, slope):
    count = len(pieces)
    height, _, width = factor.shape
    depth = pieces[0].shape[1]

    def put(row, blocks):
        lanes = pl.ds(pl.multiple_of(row * width, width), width)
        for j in range(count):
            part_of = pl.ds(j * depth, depth)
            value = blocks[j].astype(jnp.float32) * factor[row, part_of, :]
            slope[part_of, lanes] = value.astype(jnp.bfloat16)

    def body(row, carry):
        put(row + 1, [piece[row] for piece in pieces])
        return carry

    put(0, [end[2] for end in ends])
    lax.fori_loop(0, height - 2, body, 0)
    put(height - 1, [end[3] for end in ends])


def correlate_body(first_tap, count, groups, rows, turn, stacked, *refs):
    if count:
        factor, pieces, ends = refs[0], refs[1 : 1 + count], refs[1 + count : 1 + 2 * count]
        shares, slope = refs[1 + 2 * count : -1], refs[-1]
    else:
        slope, shares = refs[0], refs[1:]
    channels, pixels = slope.shape
    width = stacked.shape[1] - pixels
    width = width // 2
    tap_row = (first_tap + pl.program_id(0)) // 3
    if count:

        @pl.when(pl.program_id(0) == 0)
        def _():
            slope_rows(factor, pieces, ends, slope)

    source = stacked[:, pl.ds(pl.multiple_of(tap_row * width, width), pixels)]
    grads = lax.dot_general(
        source, slope[...], (((1,), (1,)), ((), ())), preferred_element_type=jnp.float32
    )
    size = channels // (groups * rows)
    for own in range(rows):

        @pl.when(turn[0] == own)
        def _():
            for j in range(rows):
                for group in range(groups):
                    start = (group * rows + (own - j) % rows) * size
                    shares[j][group, 0] = grads[start : start + size]


def correlate(taps, stacked, slope=None, factor=None, pieces=(), ends=()):
    first_tap, tap_count = taps
    channels = stacked.shape[0] // 3
    groups, rows = lax.axis_size("dp"), lax.axis_size("row")
    size = channels // (groups * rows)
    if slope is None:
        height, _, width = factor.shape
        pixels = height * width
        operands = [factor, *pieces, *ends]
        made = [jax.ShapeDtypeStruct((channels, pixels), jnp.bfloat16)]
    else:
        pixels = slope.shape[1]
        operands, made = [slope], []
    call = pl.pallas_call(
        functools.partial(correlate_body, first_tap, len(pieces), groups, rows),
        grid=(tap_count,),
        in_specs=[
            pl.BlockSpec(memory_space=pltpu.SMEM),
            pl.BlockSpec((channels, stacked.shape[1]), lambda t: ((first_tap + t) % 3, 0)),
        ]
        + [whole(operand.shape) for operand in operands],
        out_specs=[pl.BlockSpec((groups, 1, size, channels), lambda t: (0, t, 0, 0))] * rows
        + [whole(each.shape) for each in made],
        out_shape=[jax.ShapeDtypeStruct((groups, tap_count, size, channels), jnp.float32)] * rows
        + made,
        compiler_params=pltpu.CompilerParams(vmem_limit_bytes=VMEM_LIMIT),
        cost_estimate=pl.CostEstimate(
            flops=2 * tap_count * channels * channels * pixels,
            bytes_accessed=8 * 1024 * 1024,
            transcendentals=0,
        ),
    )
    turn = lax.axis_index("row").astype(jnp.int32)[None]
    results = call(turn, stacked, *operands)
    return (results[:rows], *results[rows:])


def padded_depth(depth):
    return -(-depth // 128) * 128


def turned_body(shares, *refs):
    halves, out = refs[:shares], refs[shares]
    _, depth, lanes = out.shape
    stride = lanes // 9
    total = halves[0].shape[2]
    both = [jnp.concatenate([half[0] for half in halves])]
    channels = both[0].shape[0]
    rows = []
    for start in range(0, total, 128):
        size = min(128, total - start)
        unit = (
            lax.broadcasted_iota(jnp.int32, (size, size), 0)
            == lax.broadcasted_iota(jnp.int32, (size, size), 1)
        ).astype(jnp.bfloat16)
        rows.append(
            lax.dot_general(
                unit,
                both[0][:, start : start + size],
                (((1,), (1,)), ((), ())),
                preferred_element_type=jnp.float32,
            )
        )
    turned = jnp.concatenate(rows)
    for tap in range(9):
        begin = (8 - tap) * depth
        value = turned[begin : begin + depth].astype(jnp.bfloat16)
        out[0, :, tap * stride : tap * stride + channels] = value
        if stride > channels:
            out[0, :, tap * stride + channels : (tap + 1) * stride] = jnp.zeros(
                (depth, stride - channels), jnp.bfloat16
            )


def turned(halves):
    shares = len(halves)
    blocks, outs, lanes = halves[0].shape
    depth = lanes // 9
    stride = padded_depth(outs * shares)
    return pl.pallas_call(
        functools.partial(turned_body, shares),
        grid=(blocks,),
        in_specs=[pl.BlockSpec((1, outs, lanes), lambda g: (g, 0, 0))] * shares,
        out_specs=pl.BlockSpec((1, depth, 9 * stride), lambda g: (g, 0, 0)),
        out_shape=jax.ShapeDtypeStruct((blocks, depth, 9 * stride), jnp.bfloat16),
        compiler_params=pltpu.CompilerParams(vmem_limit_bytes=VMEM_LIMIT),
        cost_estimate=pl.CostEstimate(
            flops=2 * 128 * blocks * outs * shares * lanes,
            bytes_accessed=4 * 1024 * 1024,
            transcendentals=0,
        ),
        name="turn_kernel",
    )(*halves)


def backward_body(count, shares, rows, turns, slope, above, below, kernels, *refs):
    outs, (stacked, weights, arrived) = refs[:count], refs[count:]
    channels = slope.shape[0]
    _, _, width = above.shape
    height = slope.shape[1] // width
    depth = channels // count
    size = depth // shares
    stride = stacked.shape[0] // 3
    step = pl.program_id(0)

    def in_share_order(wide):
        parts = []
        for at in range(shares):
            chosen = None
            for share in range(shares):
                value = jnp.concatenate(
                    [wide[j * depth + share * size : j * depth + (share + 1) * size] for j in range(count)]
                )
                here = turns[3] == (share - at) % shares
                chosen = value if chosen is None else jnp.where(here, value, chosen)
            parts.append(chosen)
        return jnp.concatenate(parts)

    def put(row, block):
        lanes = pl.ds(pl.multiple_of(row * width, width), width)
        wide = in_share_order(block.astype(jnp.float32))
        for copies, moved in enumerate((columns_moved(wide, -1), wide, columns_moved(wide, 1))):
            stacked[copies * stride : copies * stride + channels, lanes] = moved.astype(slope.dtype)

    @pl.when(step == 0)
    def _():
        fetch = pltpu.make_async_copy(kernels, weights, arrived)
        fetch.start()
        if stride > channels:
            for copies in range(3):
                stacked[copies * stride + channels : (copies + 1) * stride, :] = jnp.zeros(
                    (stride - channels, stacked.shape[1]), stacked.dtype
                )
        for side, rim, row in ((0, above, 0), (1, below, height + 1)):
            blocks = []
            for j in range(count):
                start = lax.rem(turns[side] + j, count) * depth
                blocks.append(rim[0, pl.ds(pl.multiple_of(start, depth), depth), :])
            put(row, jnp.concatenate(blocks))

        def body(row, carry):
            lanes = pl.ds(pl.multiple_of(row * width, width), width)
            put(row + 1, slope[:, lanes])
            return carry

        lax.fori_loop(0, height, body, 0)
        fetch.wait()

    windows = [
        stacked[:, pl.ds(pl.multiple_of((step * rows + a) * width, width), rows * width)]
        for a in range(3)
    ]
    order = [weights[lax.rem(turns[2] + j, count)] for j in range(count)]
    grad = jnp.dot(
        jnp.concatenate(order), jnp.concatenate(windows), preferred_element_type=jnp.float32
    )
    for row in range(rows):
        lanes = slice(row * width, (row + 1) * width)
        for j in range(count):
            outs[j][row] = grad[j * depth : (j + 1) * depth, lanes].astype(outs[j].dtype)


def backward(turns, slope, above, below, kernels, count, slab):
    channels = slope.shape[0]
    width = above.shape[2]
    height = slope.shape[1] // width
    depth = channels // count
    rows = 4 if height % 4 == 0 else 1
    flops = 2 * 9 * channels * channels * height * width
    steps = height // rows
    return pl.pallas_call(
        functools.partial(backward_body, count, lax.axis_size("row"), rows),
        grid_spec=pltpu.PrefetchScalarGridSpec(
            num_scalar_prefetch=1,
            grid=(steps,),
            in_specs=[
                whole(slope.shape),
                whole(above.shape),
                whole(below.shape),
                pl.BlockSpec(memory_space=pl.ANY),
            ],
            out_specs=[pl.BlockSpec((rows, depth, width), lambda g, turns: (turns[4] * steps + g, 0, 0))]
            + [pl.BlockSpec((rows, depth, width), lambda g, _: (g, 0, 0))] * (count - 1),
            scratch_shapes=[
                pltpu.VMEM((kernels.shape[2] // 3, (height + 2) * width), jnp.bfloat16),
                pltpu.VMEM(kernels.shape, kernels.dtype),
                pltpu.SemaphoreType.DMA,
            ],
        ),
        out_shape=[jax.ShapeDtypeStruct((slab, depth, width), jnp.float32)]
        + [jax.ShapeDtypeStruct((height, depth, width), jnp.bfloat16)] * (count - 1),
        compiler_params=pltpu.CompilerParams(vmem_limit_bytes=VMEM_LIMIT),
        cost_estimate=pl.CostEstimate(
            flops=flops, bytes_accessed=8 * 1024 * 1024, transcendentals=0
        ),
        name="conv_backward",
    )(turns, slope, above, below, kernels)


def gathered_kernel(kernel):
    dp, row = lax.axis_index("dp"), lax.axis_index("row")
    dps, chans, rows = (lax.axis_size(a) for a in ("dp", "chan", "row"))
    _, inner, outer = kernel.shape
    size = outer // rows
    mine = part(kernel, row, size, 2)
    mine = jnp.transpose(mine, (2, 0, 1)).reshape(size, 9 * inner)
    over_chan = jnp.concatenate([mine] + [receive(mine, "chan", j) for j in range(1, chans)], axis=0)
    over_dp = jnp.stack([over_chan] + [receive(over_chan, "dp", j) for j in range(1, dps)])
    if dps != chans:
        each = dps // chans
        over_dp = rotated(over_dp, (dps - dp) % dps, 0)
        over_dp = over_dp.reshape(chans, each, chans * size, 9, inner)
        over_dp = jnp.transpose(over_dp, (0, 2, 3, 1, 4)).reshape(chans, chans * size, 9 * each * inner)
    return [over_dp] + [receive(over_dp, "row", j) for j in range(1, rows)]


def summed_over_images(shares):
    dp = lax.axis_index("dp")
    dps, chans, rows = (lax.axis_size(a) for a in ("dp", "chan", "row"))
    halves = shares[0]
    for j in range(1, rows):
        halves = halves + receive(shares[j], "row", j)

    def of_dp(ahead):
        if dps == chans:
            return halves[ahead % dps]
        return lax.dynamic_index_in_dim(halves, (dp + ahead) % dps, 0, keepdims=False)

    total = of_dp(0)
    for j in range(1, dps):
        total = total + receive(of_dp(-j), "dp", j)
    return total


def kernel_grad_of(total, inner, outer):
    row = lax.axis_index("row")
    chans, rows = lax.axis_size("chan"), lax.axis_size("row")
    taps, share, channels = total.shape
    total = jnp.transpose(total, (2, 0, 1)).reshape(channels, taps * share)
    own = total[:outer]
    for j in range(1, chans):
        start = (chans - j) * outer
        own = own + receive(total[start : start + outer], "chan", j)
    both = jnp.stack([own] + [receive(own, "row", j) for j in range(1, rows)])
    both = rotated(both, (rows - row) % rows, 0).reshape(rows, outer, taps, share)
    return jnp.transpose(both, (2, 0, 3, 1)).reshape(taps, inner, outer)


def shards(images, kernel, cotangent):
    row, chan = lax.axis_index("row"), lax.axis_index("chan")
    rows, chans = lax.axis_size("row"), lax.axis_size("chan")
    _, slab, _, _ = images.shape
    height = slab // chans
    images, cotangent = images[0], cotangent[0]

    def home(ahead):
        return home_of(row, (chan + ahead) % chans, chans)

    def to_homes(array, size):
        return [part(array, home(0), size, 0)] + [
            receive(part(array, home(-j), size, 0), "chan", j) for j in range(1, chans)
        ]

    halves = gathered_kernel(kernel)
    pieces = to_homes(images, height)
    if rows == 2:
        edge = jnp.where(row == 0, images[slab - 1 :], images[:1])
        edge = receive(edge, "row", 1)
        low = jnp.where(row == 0, jnp.zeros_like(edge), edge)
        high = jnp.where(row == 0, edge, jnp.zeros_like(edge))
    else:
        low = lax.ppermute(images[slab - 1 :], "row", [(i, i + 1) for i in range(rows - 1)])
        high = lax.ppermute(images[:1], "row", [(i + 1, i) for i in range(rows - 1)])

    def rim_of(at):
        begin = at * height
        above = part(images, jnp.maximum(begin - 1, 0), 1, 0)
        below = part(images, jnp.minimum(begin + height, slab - 1), 1, 0)
        return jnp.concatenate(
            [
                jnp.where(at == 0, low, above),
                jnp.where(at == chans - 1, high, below),
                part(cotangent, begin, 1, 0),
                part(cotangent, begin + height - 1, 1, 0),
            ]
        )

    rims = [rim_of(home(0))]
    rims += [receive(rim_of(home(-j)), "chan", j) for j in range(1, chans)]

    def inside(ahead):
        return lax.dynamic_slice_in_dim(cotangent, home(ahead) * height + 1, height - 2, 0)

    cotangents = [inside(0)] + [receive(inside(-j), "chan", j) for j in range(1, chans)]

    shift = (chan - stacking_base()) % chans
    place_at = home(0)
    forth = jnp.where(row % 2 == 0, 1, chans - 1)
    above_turn = jnp.where(place_at == 0, 0, forth)
    below_turn = jnp.where(place_at == chans - 1, 0, chans - forth)
    turns = jnp.stack([shift, row, place_at]).astype(jnp.int32)
    back_turns = jnp.stack([above_turn, below_turn, shift, row, place_at]).astype(jnp.int32)

    results = forward(turns, pieces, rims, halves, slab)
    activated, factor, stacked, first, last = results
    back_kernel = turned(halves)

    def snake(place_at):
        r, k = place_at // chans, place_at % chans
        return (k if r % 2 == 0 else chans - 1 - k) * rows + r

    line = [(snake(i), snake(i + 1)) for i in range(rows * chans - 1)]
    above = lax.ppermute(last, ("chan", "row"), line)
    below = lax.ppermute(first, ("chan", "row"), [(b, a) for a, b in line])

    lead, slope = correlate((0, 6), stacked, None, factor, cotangents, rims)
    lead = summed_over_images(lead)
    input_grads = list(backward(back_turns, slope, above, below, back_kernel, chans, slab))
    slope, input_grads[1] = lax.optimization_barrier((slope, input_grads[1]))
    (rest,) = correlate((6, 3), stacked, slope)
    rest = summed_over_images(rest)
    inner, outer = kernel.shape[1:]
    kernel_grad = jnp.concatenate([kernel_grad_of(lead, inner, outer), kernel_grad_of(rest, inner, outer)])

    def to_owners(blocks):
        out = blocks[0]
        for j in range(1, chans):
            arrived = receive(blocks[j], "chan", chans - j).astype(out.dtype)
            out = lax.dynamic_update_slice_in_dim(out, arrived, home(-j) * height, 0)
        return out[None]

    return to_owners(activated), to_owners(input_grads), kernel_grad


def solution(mesh):
    placed = (P("dp", "row", "chan", None), P(None, "dp", "chan"), P("dp", "row", "chan", None))
    return jax.shard_map(
        shards,
        mesh=mesh,
        in_specs=placed,
        out_specs=(
            P("dp", "row", "chan", None),
            P("dp", "row", "chan", None),
            P(None, "dp", "chan"),
        ),
        check_vma=False,
    )
```

```python
import functools

import jax
import jax.numpy as jnp
from jax import lax
from jax.experimental import pallas as pl
from jax.experimental.pallas import tpu as pltpu
from jax.sharding import PartitionSpec as P


VMEM_LIMIT = 60 * 1024 * 1024


def receive(block, axis, ahead):
    count = lax.axis_size(axis)
    return lax.ppermute(block, axis, [(i, (i - ahead) % count) for i in range(count)])


def swapped(block, axis, bit):
    return lax.ppermute(block, axis, [(i, i ^ bit) for i in range(lax.axis_size(axis))])


def summed_over_chan(total, outer, in_steps):
    chans = lax.axis_size("chan")
    blocks = [total[j * outer : (j + 1) * outer] for j in range(chans)]
    if chans != 4 or not in_steps:
        own = blocks[0]
        for j in range(1, chans):
            own = own + receive(blocks[chans - j], "chan", j)
        return own
    odd = lax.axis_index("chan") % 2 == 1
    beside = swapped(jnp.concatenate([blocks[1], blocks[3]]), "chan", 1)
    first, second = beside[:outer], beside[outer:]
    other = blocks[2] + jnp.where(odd, second, first)
    return blocks[0] + jnp.where(odd, first, second) + swapped(other, "chan", 2)


def home_of(row, chan, chans):
    return jnp.where(row % 2 == 0, chan, chans - 1 - chan)


def part(array, index, size, axis):
    return lax.dynamic_slice_in_dim(array, index * size, size, axis=axis)


def rotated(array, start, axis):
    twice = jnp.concatenate([array, array], axis=axis)
    return lax.dynamic_slice_in_dim(twice, start, array.shape[axis], axis=axis)


def stacking_base():
    matched = lax.axis_size("dp") == lax.axis_size("chan")
    return lax.axis_index("dp") if matched else jnp.int32(0)


def columns_moved(block, step):
    width = block.shape[-1]
    lane = lax.broadcasted_iota(jnp.int32, block.shape, block.ndim - 1)
    if step < 0:
        moved = pltpu.roll(block, 1, block.ndim - 1)
        return jnp.where(lane == 0, jnp.zeros_like(block), moved)
    moved = pltpu.roll(block, width - 1, block.ndim - 1)
    return jnp.where(lane == width - 1, jnp.zeros_like(block), moved)


def place(stacked, channel, row, block, channels):
    depth, width = block.shape
    lanes = pl.ds(pl.multiple_of(row * width, width), width)
    wide = block.astype(jnp.float32)

    def below(copies):
        start = copies * channels + channel
        return pl.ds(start if isinstance(channel, int) else pl.multiple_of(start, 16), depth)

    stacked[below(0), lanes] = columns_moved(wide, -1).astype(block.dtype)
    stacked[below(1), lanes] = block
    stacked[below(2), lanes] = columns_moved(wide, 1).astype(block.dtype)


def window(stacked, tap_row, tap_col, channel, depth, first, rows, width, channels):
    start = pl.multiple_of((first + tap_row) * width, width)
    return stacked[tap_col * channels + channel : tap_col * channels + channel + depth, pl.ds(start, rows * width)]


def forward_taps(halves, stacked, first, rows, width):
    count = halves[0].shape[0]
    depth = halves[0].shape[2] // 9
    total = None
    for block in range(count):
        windows = [
            window(stacked, a, b, block * depth, depth, first, rows, width, count * depth)
            for a in range(3)
            for b in range(3)
        ]
        term = jnp.dot(
            jnp.concatenate([half[block] for half in halves]),
            jnp.concatenate(windows),
            preferred_element_type=jnp.float32,
        )
        total = term if total is None else total + term
    return total


def forward_body(count, shares, rows, turns, *refs):
    pieces, rims = refs[:count], refs[count : 2 * count]
    halves = refs[2 * count : 2 * count + shares]
    outs = refs[2 * count + shares : 3 * count + shares]
    factor, stacked, first, last = refs[3 * count + shares :]
    height, depth, width = pieces[0].shape
    channels = count * depth
    step = pl.program_id(0)

    @pl.when(step == 0)
    def _():
        slots = [lax.rem(turns[0] + j, count) * depth for j in range(count)]
        for j in range(count):
            place(stacked, slots[j], 0, rims[j][0], channels)
            place(stacked, slots[j], height + 1, rims[j][1], channels)

        def body(row, carry):
            for j in range(count):
                place(stacked, slots[j], row + 1, pieces[j][row], channels)
            return carry

        lax.fori_loop(0, height, body, 0)

    mixed = forward_taps(halves, stacked, step * rows, rows, width)
    size = depth // shares
    for j in range(count):
        parts = []
        for share in range(shares):
            chosen = None
            for at in range(shares):
                start = at * count * size + j * size
                value = mixed[start : start + size]
                here = turns[1] == (share - at) % shares
                chosen = value if chosen is None else jnp.where(here, value, chosen)
            parts.append(chosen)
        pre = jnp.concatenate(parts) if shares > 1 else parts[0]
        sigma = jax.nn.sigmoid(pre)
        activated = (pre * sigma).astype(jnp.bfloat16)
        slope = sigma * (1.0 + pre * (1.0 - sigma))
        for row in range(rows):
            lanes = slice(row * width, (row + 1) * width)
            factor[row, j * depth : (j + 1) * depth, :] = slope[:, lanes]
            outs[j][row] = activated[:, lanes]

    def end(out, side, row):
        for j in range(count):
            part_of = slice(j * depth, (j + 1) * depth)
            value = rims[j][side].astype(jnp.float32) * factor[row, part_of, :]
            out[0, part_of, :] = value.astype(jnp.bfloat16)

    @pl.when(step == 0)
    def _():
        end(first, 2, 0)

    @pl.when(step == pl.num_programs(0) - 1)
    def _():
        end(last, 3, rows - 1)


def whole(shape):
    return pl.BlockSpec(shape, lambda *_: (0,) * len(shape), pipeline_mode=pl.Buffered(1))


def forward(turns, pieces, rims, halves, slab):
    count = len(pieces)
    height, depth, width = pieces[0].shape
    channels = count * depth
    rows = 4 if height % 4 == 0 else 1
    flops = 2 * 9 * channels * channels * height * width
    steps = height // rows
    call = pl.pallas_call(
        functools.partial(forward_body, count, len(halves), rows),
        grid_spec=pltpu.PrefetchScalarGridSpec(
            num_scalar_prefetch=1,
            grid=(steps,),
            in_specs=[whole(pieces[0].shape)] * count
            + [whole(rims[0].shape)] * count
            + [whole(halves[0].shape)] * len(halves),
            out_specs=[pl.BlockSpec((rows, depth, width), lambda g, turns: (turns[2] * steps + g, 0, 0))]
            + [pl.BlockSpec((rows, depth, width), lambda g, _: (g, 0, 0))] * (count - 1)
            + [
                pl.BlockSpec((rows, channels, width), lambda g, _: (g, 0, 0)),
                whole((3 * channels, (height + 2) * width)),
                whole((1, channels, width)),
                whole((1, channels, width)),
            ],
        ),
        out_shape=[
            jax.ShapeDtypeStruct((height if j else slab, depth, width), jnp.bfloat16)
            for j in range(count)
        ]
        + [
            jax.ShapeDtypeStruct((height, channels, width), jnp.float32),
            jax.ShapeDtypeStruct((3 * channels, (height + 2) * width), jnp.bfloat16),
            jax.ShapeDtypeStruct((1, channels, width), jnp.bfloat16),
            jax.ShapeDtypeStruct((1, channels, width), jnp.bfloat16),
        ],
        compiler_params=pltpu.CompilerParams(vmem_limit_bytes=VMEM_LIMIT),
        cost_estimate=pl.CostEstimate(
            flops=flops, bytes_accessed=16 * 1024 * 1024, transcendentals=0
        ),
        name="conv_forward",
    )
    results = call(turns, *pieces, *rims, *halves)
    return list(results[:count]), *results[count:]


def slope_rows(factor, pieces, ends, slope):
    count = len(pieces)
    height, _, width = factor.shape
    depth = pieces[0].shape[1]

    def put(row, blocks):
        lanes = pl.ds(pl.multiple_of(row * width, width), width)
        for j in range(count):
            part_of = pl.ds(j * depth, depth)
            value = blocks[j].astype(jnp.float32) * factor[row, part_of, :]
            slope[part_of, lanes] = value.astype(jnp.bfloat16)

    def body(row, carry):
        put(row + 1, [piece[row] for piece in pieces])
        return carry

    put(0, [end[2] for end in ends])
    lax.fori_loop(0, height - 2, body, 0)
    put(height - 1, [end[3] for end in ends])


def correlate_body(first_tap, count, groups, rows, turn, stacked, *refs):
    if count:
        factor, pieces, ends = refs[0], refs[1 : 1 + count], refs[1 + count : 1 + 2 * count]
        shares, slope = refs[1 + 2 * count : -1], refs[-1]
    else:
        slope, shares = refs[0], refs[1:]
    channels, pixels = slope.shape
    width = stacked.shape[1] - pixels
    width = width // 2
    tap_row = (first_tap + pl.program_id(0)) // 3
    if count:

        @pl.when(pl.program_id(0) == 0)
        def _():
            slope_rows(factor, pieces, ends, slope)

    tap_col = lax.rem(first_tap + pl.program_id(0), 3) if count else 0
    source = stacked[
        pl.ds(pl.multiple_of(tap_col * channels, channels), channels),
        pl.ds(pl.multiple_of(tap_row * width, width), pixels),
    ]
    grads = lax.dot_general(
        source, slope[...], (((1,), (1,)), ((), ())), preferred_element_type=jnp.float32
    )
    size = channels // (groups * rows)
    for own in range(rows):

        @pl.when(turn[0] == own)
        def _():
            for j in range(rows):
                for group in range(groups):
                    start = (group * rows + (own - j) % rows) * size
                    shares[j][group, 0] = grads[start : start + size]


def correlate(taps, stacked, slope=None, factor=None, pieces=(), ends=()):
    first_tap, tap_count = taps
    channels = stacked.shape[0] // 3
    groups, rows = lax.axis_size("dp"), lax.axis_size("row")
    size = channels // (groups * rows)
    if slope is None:
        height, _, width = factor.shape
        pixels = height * width
        operands = [factor, *pieces, *ends]
        made = [jax.ShapeDtypeStruct((channels, pixels), jnp.bfloat16)]
    else:
        pixels = slope.shape[1]
        operands, made = [slope], []
    call = pl.pallas_call(
        functools.partial(correlate_body, first_tap, len(pieces), groups, rows),
        grid=(tap_count,),
        in_specs=[
            pl.BlockSpec(memory_space=pltpu.SMEM),
            pl.BlockSpec((channels, stacked.shape[1]), lambda t: ((first_tap + t) % 3, 0))
            if made == []
            else whole(stacked.shape),
        ]
        + [whole(operand.shape) for operand in operands],
        out_specs=[pl.BlockSpec((groups, 1, size, channels), lambda t: (0, t, 0, 0))] * rows
        + [whole(each.shape) for each in made],
        out_shape=[jax.ShapeDtypeStruct((groups, tap_count, size, channels), jnp.float32)] * rows
        + made,
        compiler_params=pltpu.CompilerParams(vmem_limit_bytes=VMEM_LIMIT),
        cost_estimate=pl.CostEstimate(
            flops=2 * tap_count * channels * channels * pixels,
            bytes_accessed=8 * 1024 * 1024,
            transcendentals=0,
        ),
    )
    turn = lax.axis_index("row").astype(jnp.int32)[None]
    results = call(turn, stacked, *operands)
    return (results[:rows], *results[rows:])


def padded_depth(depth):
    return -(-depth // 128) * 128


def turned_body(shares, *refs):
    halves, out = refs[:shares], refs[shares]
    _, depth, lanes = out.shape
    stride = lanes // 9
    total = halves[0].shape[2]
    both = [jnp.concatenate([half[0] for half in halves])]
    channels = both[0].shape[0]
    rows = []
    for start in range(0, total, 128):
        size = min(128, total - start)
        unit = (
            lax.broadcasted_iota(jnp.int32, (size, size), 0)
            == lax.broadcasted_iota(jnp.int32, (size, size), 1)
        ).astype(jnp.bfloat16)
        rows.append(
            lax.dot_general(
                unit,
                both[0][:, start : start + size],
                (((1,), (1,)), ((), ())),
                preferred_element_type=jnp.float32,
            )
        )
    turned = jnp.concatenate(rows)
    for tap in range(9):
        begin = (8 - tap) * depth
        value = turned[begin : begin + depth].astype(jnp.bfloat16)
        out[0, :, tap * stride : tap * stride + channels] = value
        if stride > channels:
            out[0, :, tap * stride + channels : (tap + 1) * stride] = jnp.zeros(
                (depth, stride - channels), jnp.bfloat16
            )


def turned(halves):
    shares = len(halves)
    blocks, outs, lanes = halves[0].shape
    depth = lanes // 9
    stride = padded_depth(outs * shares)
    return pl.pallas_call(
        functools.partial(turned_body, shares),
        grid=(blocks,),
        in_specs=[pl.BlockSpec((1, outs, lanes), lambda g: (g, 0, 0))] * shares,
        out_specs=pl.BlockSpec((1, depth, 9 * stride), lambda g: (g, 0, 0)),
        out_shape=jax.ShapeDtypeStruct((blocks, depth, 9 * stride), jnp.bfloat16),
        compiler_params=pltpu.CompilerParams(vmem_limit_bytes=VMEM_LIMIT),
        cost_estimate=pl.CostEstimate(
            flops=2 * 128 * blocks * outs * shares * lanes,
            bytes_accessed=4 * 1024 * 1024,
            transcendentals=0,
        ),
        name="turn_kernel",
    )(*halves)


def backward_body(count, shares, rows, turns, slope, above, below, kernels, *refs):
    outs, (stacked, weights, arrived) = refs[:count], refs[count:]
    channels = slope.shape[0]
    _, _, width = above.shape
    height = slope.shape[1] // width
    depth = channels // count
    size = depth // shares
    stride = stacked.shape[0] // 3
    step = pl.program_id(0)

    def in_share_order(wide):
        parts = []
        for at in range(shares):
            chosen = None
            for share in range(shares):
                value = jnp.concatenate(
                    [wide[j * depth + share * size : j * depth + (share + 1) * size] for j in range(count)]
                )
                here = turns[1] == (share - at) % shares
                chosen = value if chosen is None else jnp.where(here, value, chosen)
            parts.append(chosen)
        return jnp.concatenate(parts)

    def put(row, block):
        lanes = pl.ds(pl.multiple_of(row * width, width), width)
        wide = in_share_order(block.astype(jnp.float32))
        for copies, moved in enumerate((columns_moved(wide, -1), wide, columns_moved(wide, 1))):
            stacked[copies * stride : copies * stride + channels, lanes] = moved.astype(slope.dtype)

    @pl.when(step == 0)
    def _():
        fetch = pltpu.make_async_copy(kernels, weights, arrived)
        fetch.start()
        if stride > channels:
            for copies in range(3):
                stacked[copies * stride + channels : (copies + 1) * stride, :] = jnp.zeros(
                    (stride - channels, stacked.shape[1]), stacked.dtype
                )
        for side, rim, row in ((3, above, 0), (4, below, height + 1)):
            blocks = []
            for j in range(count):
                start = lax.rem(turns[side] + j, count) * depth
                blocks.append(rim[0, pl.ds(pl.multiple_of(start, depth), depth), :])
            put(row, jnp.concatenate(blocks))

        def body(row, carry):
            lanes = pl.ds(pl.multiple_of(row * width, width), width)
            put(row + 1, slope[:, lanes])
            return carry

        lax.fori_loop(0, height, body, 0)
        fetch.wait()

    windows = [
        stacked[:, pl.ds(pl.multiple_of((step * rows + a) * width, width), rows * width)]
        for a in range(3)
    ]
    order = [weights[lax.rem(turns[0] + j, count)] for j in range(count)]
    grad = jnp.dot(
        jnp.concatenate(order), jnp.concatenate(windows), preferred_element_type=jnp.float32
    )
    for row in range(rows):
        lanes = slice(row * width, (row + 1) * width)
        for j in range(count):
            outs[j][row] = grad[j * depth : (j + 1) * depth, lanes].astype(outs[j].dtype)


def backward(turns, slope, above, below, kernels, count, slab):
    channels = slope.shape[0]
    width = above.shape[2]
    height = slope.shape[1] // width
    depth = channels // count
    rows = 4 if height % 4 == 0 else 1
    flops = 2 * 9 * channels * channels * height * width
    steps = height // rows
    return pl.pallas_call(
        functools.partial(backward_body, count, lax.axis_size("row"), rows),
        grid_spec=pltpu.PrefetchScalarGridSpec(
            num_scalar_prefetch=1,
            grid=(steps,),
            in_specs=[
                whole(slope.shape),
                whole(above.shape),
                whole(below.shape),
                pl.BlockSpec(memory_space=pl.ANY),
            ],
            out_specs=[pl.BlockSpec((rows, depth, width), lambda g, turns: (turns[2] * steps + g, 0, 0))]
            + [pl.BlockSpec((rows, depth, width), lambda g, _: (g, 0, 0))] * (count - 1),
            scratch_shapes=[
                pltpu.VMEM((kernels.shape[2] // 3, (height + 2) * width), jnp.bfloat16),
                pltpu.VMEM(kernels.shape, kernels.dtype),
                pltpu.SemaphoreType.DMA,
            ],
        ),
        out_shape=[jax.ShapeDtypeStruct((slab, depth, width), jnp.float32)]
        + [jax.ShapeDtypeStruct((height, depth, width), jnp.bfloat16)] * (count - 1),
        compiler_params=pltpu.CompilerParams(vmem_limit_bytes=VMEM_LIMIT),
        cost_estimate=pl.CostEstimate(
            flops=flops, bytes_accessed=8 * 1024 * 1024, transcendentals=0
        ),
        name="conv_backward",
    )(turns, slope, above, below, kernels)


def gathered_kernel(kernel):
    dp, row = lax.axis_index("dp"), lax.axis_index("row")
    dps, chans, rows = (lax.axis_size(a) for a in ("dp", "chan", "row"))
    _, inner, outer = kernel.shape
    size = outer // rows
    mine = part(kernel, row, size, 2)
    mine = jnp.transpose(mine, (2, 0, 1)).reshape(size, 9 * inner)
    over_chan = jnp.concatenate([mine] + [receive(mine, "chan", j) for j in range(1, chans)], axis=0)
    over_dp = jnp.stack([over_chan] + [receive(over_chan, "dp", j) for j in range(1, dps)])
    if dps != chans:
        each = dps // chans
        over_dp = rotated(over_dp, (dps - dp) % dps, 0)
        over_dp = over_dp.reshape(chans, each, chans * size, 9, inner)
        over_dp = jnp.transpose(over_dp, (0, 2, 3, 1, 4)).reshape(chans, chans * size, 9 * each * inner)
    return [over_dp] + [receive(over_dp, "row", j) for j in range(1, rows)]


def summed_over_images(shares):
    dp = lax.axis_index("dp")
    dps, chans, rows = (lax.axis_size(a) for a in ("dp", "chan", "row"))
    halves = shares[0]
    for j in range(1, rows):
        halves = halves + receive(shares[j], "row", j)

    def of_dp(ahead):
        if dps == chans:
            return halves[ahead % dps]
        return lax.dynamic_index_in_dim(halves, (dp + ahead) % dps, 0, keepdims=False)

    total = of_dp(0)
    for j in range(1, dps):
        total = total + receive(of_dp(-j), "dp", j)
    return total


def kernel_grad_of(total, inner, outer, in_steps):
    row, rows = lax.axis_index("row"), lax.axis_size("row")
    taps, share, channels = total.shape
    total = jnp.transpose(total, (2, 0, 1)).reshape(channels, taps * share)
    own = summed_over_chan(total, outer, in_steps)
    both = jnp.stack([own] + [receive(own, "row", j) for j in range(1, rows)])
    both = rotated(both, (rows - row) % rows, 0).reshape(rows, outer, taps, share)
    return jnp.transpose(both, (2, 0, 3, 1)).reshape(taps, inner, outer)


def shards(images, kernel, cotangent):
    row, chan = lax.axis_index("row"), lax.axis_index("chan")
    rows, chans = lax.axis_size("row"), lax.axis_size("chan")
    _, slab, _, _ = images.shape
    height = slab // chans
    images, cotangent = images[0], cotangent[0]

    def home(ahead):
        return home_of(row, (chan + ahead) % chans, chans)

    def to_homes(array, size):
        return [part(array, home(0), size, 0)] + [
            receive(part(array, home(-j), size, 0), "chan", j) for j in range(1, chans)
        ]

    halves = gathered_kernel(kernel)
    pieces = to_homes(images, height)
    if rows == 2:
        edge = jnp.where(row == 0, images[slab - 1 :], images[:1])
        edge = receive(edge, "row", 1)
        low = jnp.where(row == 0, jnp.zeros_like(edge), edge)
        high = jnp.where(row == 0, edge, jnp.zeros_like(edge))
    else:
        low = lax.ppermute(images[slab - 1 :], "row", [(i, i + 1) for i in range(rows - 1)])
        high = lax.ppermute(images[:1], "row", [(i + 1, i) for i in range(rows - 1)])

    def rim_of(at):
        begin = at * height
        above = part(images, jnp.maximum(begin - 1, 0), 1, 0)
        below = part(images, jnp.minimum(begin + height, slab - 1), 1, 0)
        return jnp.concatenate(
            [
                jnp.where(at == 0, low, above),
                jnp.where(at == chans - 1, high, below),
                part(cotangent, begin, 1, 0),
                part(cotangent, begin + height - 1, 1, 0),
            ]
        )

    rims = [rim_of(home(0))]
    rims += [receive(rim_of(home(-j)), "chan", j) for j in range(1, chans)]

    def inside(ahead):
        return lax.dynamic_slice_in_dim(cotangent, home(ahead) * height + 1, height - 2, 0)

    cotangents = [inside(0)] + [receive(inside(-j), "chan", j) for j in range(1, chans)]

    shift = (chan - stacking_base()) % chans
    place_at = home(0)
    forth = jnp.where(row % 2 == 0, 1, chans - 1)
    above_turn = jnp.where(place_at == 0, 0, forth)
    below_turn = jnp.where(place_at == chans - 1, 0, chans - forth)
    turns = jnp.stack([shift, row, place_at, above_turn, below_turn]).astype(jnp.int32)

    results = forward(turns, pieces, rims, halves, slab)
    activated, factor, stacked, first, last = results
    back_kernel = turned(halves)

    def snake(place_at):
        r, k = place_at // chans, place_at % chans
        return (k if r % 2 == 0 else chans - 1 - k) * rows + r

    line = [(snake(i), snake(i + 1)) for i in range(rows * chans - 1)]
    above = lax.ppermute(last, ("chan", "row"), line)
    below = lax.ppermute(first, ("chan", "row"), [(b, a) for a, b in line])

    lead, slope = correlate((0, 6), stacked, None, factor, cotangents, rims)
    lead = summed_over_images(lead)
    input_grads = list(backward(turns, slope, above, below, back_kernel, chans, slab))
    slope, input_grads[1] = lax.optimization_barrier((slope, input_grads[1]))
    (rest,) = correlate((6, 3), stacked, slope)
    rest = summed_over_images(rest)
    inner, outer = kernel.shape[1:]
    kernel_grad = jnp.concatenate([kernel_grad_of(lead, inner, outer, True), kernel_grad_of(rest, inner, outer, False)])

    def to_owners(blocks):
        out = blocks[0]
        for j in range(1, chans):
            arrived = receive(blocks[j], "chan", chans - j).astype(out.dtype)
            out = lax.dynamic_update_slice_in_dim(out, arrived, home(-j) * height, 0)
        return out[None]

    return to_owners(activated), to_owners(input_grads), kernel_grad


def solution(mesh):
    placed = (P("dp", "row", "chan", None), P(None, "dp", "chan"), P("dp", "row", "chan", None))
    return jax.shard_map(
        shards,
        mesh=mesh,
        in_specs=placed,
        out_specs=(
            P("dp", "row", "chan", None),
            P("dp", "row", "chan", None),
            P(None, "dp", "chan"),
        ),
        check_vma=False,
    )
```

```python
import functools

import jax
import jax.numpy as jnp
from jax import lax
from jax.experimental import pallas as pl
from jax.experimental.pallas import tpu as pltpu
from jax.sharding import PartitionSpec as P


VMEM_LIMIT = 60 * 1024 * 1024


def receive(block, axis, ahead):
    count = lax.axis_size(axis)
    return lax.ppermute(block, axis, [(i, (i - ahead) % count) for i in range(count)])


def swapped(block, axis, bit):
    return lax.ppermute(block, axis, [(i, i ^ bit) for i in range(lax.axis_size(axis))])


def summed_over_chan(total, outer, in_steps):
    chans = lax.axis_size("chan")
    blocks = [total[j * outer : (j + 1) * outer] for j in range(chans)]
    if chans != 4 or not in_steps:
        own = blocks[0]
        for j in range(1, chans):
            own = own + receive(blocks[chans - j], "chan", j)
        return own
    odd = lax.axis_index("chan") % 2 == 1
    beside = swapped(jnp.concatenate([blocks[1], blocks[3]]), "chan", 1)
    first, second = beside[:outer], beside[outer:]
    other = blocks[2] + jnp.where(odd, second, first)
    return blocks[0] + jnp.where(odd, first, second) + swapped(other, "chan", 2)


def home_of(row, chan, chans):
    return jnp.where(row % 2 == 0, chan, chans - 1 - chan)


def part(array, index, size, axis):
    return lax.dynamic_slice_in_dim(array, index * size, size, axis=axis)


def rotated(array, start, axis):
    twice = jnp.concatenate([array, array], axis=axis)
    return lax.dynamic_slice_in_dim(twice, start, array.shape[axis], axis=axis)


def stacking_base():
    matched = lax.axis_size("dp") == lax.axis_size("chan")
    return lax.axis_index("dp") if matched else jnp.int32(0)


def columns_moved(block, step):
    width = block.shape[-1]
    lane = lax.broadcasted_iota(jnp.int32, block.shape, block.ndim - 1)
    if step < 0:
        moved = pltpu.roll(block, 1, block.ndim - 1)
        return jnp.where(lane == 0, jnp.zeros_like(block), moved)
    moved = pltpu.roll(block, width - 1, block.ndim - 1)
    return jnp.where(lane == width - 1, jnp.zeros_like(block), moved)


def place(stacked, channel, row, block, channels):
    depth, width = block.shape
    lanes = pl.ds(pl.multiple_of(row * width, width), width)
    wide = block.astype(jnp.float32)

    def below(copies):
        start = copies * channels + channel
        return pl.ds(start if isinstance(channel, int) else pl.multiple_of(start, 16), depth)

    stacked[below(0), lanes] = columns_moved(wide, -1).astype(block.dtype)
    stacked[below(1), lanes] = block
    stacked[below(2), lanes] = columns_moved(wide, 1).astype(block.dtype)


def window(stacked, tap_row, tap_col, channel, depth, first, rows, width, channels):
    start = pl.multiple_of((first + tap_row) * width, width)
    return stacked[tap_col * channels + channel : tap_col * channels + channel + depth, pl.ds(start, rows * width)]


def forward_taps(halves, stacked, first, rows, width):
    count = halves[0].shape[0]
    depth = halves[0].shape[2] // 9
    total = None
    for block in range(count):
        windows = [
            window(stacked, a, b, block * depth, depth, first, rows, width, count * depth)
            for a in range(3)
            for b in range(3)
        ]
        term = jnp.dot(
            jnp.concatenate([half[block] for half in halves]),
            jnp.concatenate(windows),
            preferred_element_type=jnp.float32,
        )
        total = term if total is None else total + term
    return total


def forward_body(count, shares, rows, turns, *refs):
    pieces, rims = refs[:count], refs[count : 2 * count]
    halves = refs[2 * count : 2 * count + shares]
    outs = refs[2 * count + shares : 3 * count + shares]
    factor, stacked, first, last = refs[3 * count + shares :]
    height, depth, width = pieces[0].shape
    channels = count * depth
    step = pl.program_id(0)

    @pl.when(step == 0)
    def _():
        slots = [lax.rem(turns[0] + j, count) * depth for j in range(count)]
        for j in range(count):
            place(stacked, slots[j], 0, rims[j][0], channels)
            place(stacked, slots[j], height + 1, rims[j][1], channels)

        def body(row, carry):
            for j in range(count):
                place(stacked, slots[j], row + 1, pieces[j][row], channels)
            return carry

        lax.fori_loop(0, height, body, 0)

    mixed = forward_taps(halves, stacked, step * rows, rows, width)
    size = depth // shares
    for j in range(count):
        parts = []
        for share in range(shares):
            chosen = None
            for at in range(shares):
                start = at * count * size + j * size
                value = mixed[start : start + size]
                here = turns[1] == (share - at) % shares
                chosen = value if chosen is None else jnp.where(here, value, chosen)
            parts.append(chosen)
        pre = jnp.concatenate(parts) if shares > 1 else parts[0]
        sigma = jax.nn.sigmoid(pre)
        activated = (pre * sigma).astype(jnp.bfloat16)
        slope = sigma * (1.0 + pre * (1.0 - sigma))
        for row in range(rows):
            lanes = slice(row * width, (row + 1) * width)
            factor[row, j * depth : (j + 1) * depth, :] = slope[:, lanes]
            outs[j][row] = activated[:, lanes]

    def end(out, side, row):
        for j in range(count):
            part_of = slice(j * depth, (j + 1) * depth)
            value = rims[j][side].astype(jnp.float32) * factor[row, part_of, :]
            out[0, part_of, :] = value.astype(jnp.bfloat16)

    @pl.when(step == 0)
    def _():
        end(first, 2, 0)

    @pl.when(step == pl.num_programs(0) - 1)
    def _():
        end(last, 3, rows - 1)


def whole(shape):
    return pl.BlockSpec(shape, lambda *_: (0,) * len(shape), pipeline_mode=pl.Buffered(1))


def forward(turns, pieces, rims, halves, slab):
    count = len(pieces)
    height, depth, width = pieces[0].shape
    channels = count * depth
    rows = 4 if height % 4 == 0 else 1
    flops = 2 * 9 * channels * channels * height * width
    steps = height // rows
    call = pl.pallas_call(
        functools.partial(forward_body, count, len(halves), rows),
        grid_spec=pltpu.PrefetchScalarGridSpec(
            num_scalar_prefetch=1,
            grid=(steps,),
            in_specs=[whole(pieces[0].shape)] * count
            + [whole(rims[0].shape)] * count
            + [whole(halves[0].shape)] * len(halves),
            out_specs=[pl.BlockSpec((rows, depth, width), lambda g, turns: (turns[2] * steps + g, 0, 0))]
            + [pl.BlockSpec((rows, depth, width), lambda g, _: (g, 0, 0))] * (count - 1)
            + [
                pl.BlockSpec((rows, channels, width), lambda g, _: (g, 0, 0)),
                whole((3 * channels, (height + 2) * width)),
                whole((1, channels, width)),
                whole((1, channels, width)),
            ],
        ),
        out_shape=[
            jax.ShapeDtypeStruct((height if j else slab, depth, width), jnp.bfloat16)
            for j in range(count)
        ]
        + [
            jax.ShapeDtypeStruct((height, channels, width), jnp.float32),
            jax.ShapeDtypeStruct((3 * channels, (height + 2) * width), jnp.bfloat16),
            jax.ShapeDtypeStruct((1, channels, width), jnp.bfloat16),
            jax.ShapeDtypeStruct((1, channels, width), jnp.bfloat16),
        ],
        compiler_params=pltpu.CompilerParams(vmem_limit_bytes=VMEM_LIMIT),
        cost_estimate=pl.CostEstimate(
            flops=flops, bytes_accessed=16 * 1024 * 1024, transcendentals=0
        ),
        name="conv_forward",
    )
    results = call(turns, *pieces, *rims, *halves)
    return list(results[:count]), *results[count:]


def slope_rows(factor, pieces, ends, slope):
    count = len(pieces)
    height, _, width = factor.shape
    depth = pieces[0].shape[1]

    def put(row, blocks):
        lanes = pl.ds(pl.multiple_of(row * width, width), width)
        for j in range(count):
            part_of = pl.ds(j * depth, depth)
            value = blocks[j].astype(jnp.float32) * factor[row, part_of, :]
            slope[part_of, lanes] = value.astype(jnp.bfloat16)

    def body(row, carry):
        put(row + 1, [piece[row] for piece in pieces])
        return carry

    put(0, [end[2] for end in ends])
    lax.fori_loop(0, height - 2, body, 0)
    put(height - 1, [end[3] for end in ends])


def correlate_body(first_tap, count, groups, rows, turn, stacked, *refs):
    if count:
        factor, pieces, ends = refs[0], refs[1 : 1 + count], refs[1 + count : 1 + 2 * count]
        shares, slope = refs[1 + 2 * count : -1], refs[-1]
    else:
        slope, shares = refs[0], refs[1:]
    channels, pixels = slope.shape
    width = stacked.shape[1] - pixels
    width = width // 2
    tap_row = (first_tap + pl.program_id(0)) // 3
    if count:

        @pl.when(pl.program_id(0) == 0)
        def _():
            slope_rows(factor, pieces, ends, slope)

    tap_col = lax.rem(first_tap + pl.program_id(0), 3) if count else 0
    source = stacked[
        pl.ds(pl.multiple_of(tap_col * channels, channels), channels),
        pl.ds(pl.multiple_of(tap_row * width, width), pixels),
    ]
    grads = lax.dot_general(
        source, slope[...], (((1,), (1,)), ((), ())), preferred_element_type=jnp.float32
    )
    size = channels // (groups * rows)
    for own in range(rows):

        @pl.when(turn[0] == own)
        def _():
            for j in range(rows):
                for group in range(groups):
                    start = (group * rows + (own - j) % rows) * size
                    shares[j][group, 0] = grads[start : start + size]


def correlate(taps, stacked, slope=None, factor=None, pieces=(), ends=()):
    first_tap, tap_count = taps
    channels = stacked.shape[0] // 3
    groups, rows = lax.axis_size("dp"), lax.axis_size("row")
    size = channels // (groups * rows)
    if slope is None:
        height, _, width = factor.shape
        pixels = height * width
        operands = [factor, *pieces, *ends]
        made = [jax.ShapeDtypeStruct((channels, pixels), jnp.bfloat16)]
    else:
        pixels = slope.shape[1]
        operands, made = [slope], []
    call = pl.pallas_call(
        functools.partial(correlate_body, first_tap, len(pieces), groups, rows),
        grid=(tap_count,),
        in_specs=[
            pl.BlockSpec(memory_space=pltpu.SMEM),
            pl.BlockSpec((channels, stacked.shape[1]), lambda t: ((first_tap + t) % 3, 0))
            if made == []
            else whole(stacked.shape),
        ]
        + [whole(operand.shape) for operand in operands],
        out_specs=[pl.BlockSpec((groups, 1, size, channels), lambda t: (0, t, 0, 0))] * rows
        + [whole(each.shape) for each in made],
        out_shape=[jax.ShapeDtypeStruct((groups, tap_count, size, channels), jnp.float32)] * rows
        + made,
        compiler_params=pltpu.CompilerParams(vmem_limit_bytes=VMEM_LIMIT),
        cost_estimate=pl.CostEstimate(
            flops=2 * tap_count * channels * channels * pixels,
            bytes_accessed=8 * 1024 * 1024,
            transcendentals=0,
        ),
    )
    turn = lax.axis_index("row").astype(jnp.int32)[None]
    results = call(turn, stacked, *operands)
    return (results[:rows], *results[rows:])


def padded_depth(depth):
    return -(-depth // 128) * 128


def turned_body(shares, *refs):
    halves, out = refs[:shares], refs[shares]
    _, depth, lanes = out.shape
    stride = lanes // 9
    total = halves[0].shape[2]
    both = [jnp.concatenate([half[0] for half in halves])]
    channels = both[0].shape[0]
    rows = []
    for start in range(0, total, 128):
        size = min(128, total - start)
        unit = (
            lax.broadcasted_iota(jnp.int32, (size, size), 0)
            == lax.broadcasted_iota(jnp.int32, (size, size), 1)
        ).astype(jnp.bfloat16)
        rows.append(
            lax.dot_general(
                unit,
                both[0][:, start : start + size],
                (((1,), (1,)), ((), ())),
                preferred_element_type=jnp.float32,
            )
        )
    turned = jnp.concatenate(rows)
    for tap in range(9):
        begin = (8 - tap) * depth
        value = turned[begin : begin + depth].astype(jnp.bfloat16)
        out[0, :, tap * stride : tap * stride + channels] = value
        if stride > channels:
            out[0, :, tap * stride + channels : (tap + 1) * stride] = jnp.zeros(
                (depth, stride - channels), jnp.bfloat16
            )


def turned(halves):
    shares = len(halves)
    blocks, outs, lanes = halves[0].shape
    depth = lanes // 9
    stride = padded_depth(outs * shares)
    return pl.pallas_call(
        functools.partial(turned_body, shares),
        grid=(blocks,),
        in_specs=[pl.BlockSpec((1, outs, lanes), lambda g: (g, 0, 0))] * shares,
        out_specs=pl.BlockSpec((1, depth, 9 * stride), lambda g: (g, 0, 0)),
        out_shape=jax.ShapeDtypeStruct((blocks, depth, 9 * stride), jnp.bfloat16),
        compiler_params=pltpu.CompilerParams(vmem_limit_bytes=VMEM_LIMIT),
        cost_estimate=pl.CostEstimate(
            flops=2 * 128 * blocks * outs * shares * lanes,
            bytes_accessed=4 * 1024 * 1024,
            transcendentals=0,
        ),
        name="turn_kernel",
    )(*halves)


def backward_body(count, shares, rows, turns, slope, above, below, kernels, *refs):
    outs, (stacked, weights, arrived) = refs[:count], refs[count:]
    channels = slope.shape[0]
    _, _, width = above.shape
    height = slope.shape[1] // width
    depth = channels // count
    size = depth // shares
    stride = stacked.shape[0] // 3
    step = pl.program_id(0)

    def in_share_order(wide):
        parts = []
        for at in range(shares):
            chosen = None
            for share in range(shares):
                value = jnp.concatenate(
                    [wide[j * depth + share * size : j * depth + (share + 1) * size] for j in range(count)]
                )
                here = turns[1] == (share - at) % shares
                chosen = value if chosen is None else jnp.where(here, value, chosen)
            parts.append(chosen)
        return jnp.concatenate(parts)

    def put(row, block):
        lanes = pl.ds(pl.multiple_of(row * width, width), width)
        wide = in_share_order(block.astype(jnp.float32))
        for copies, moved in enumerate((columns_moved(wide, -1), wide, columns_moved(wide, 1))):
            stacked[copies * stride : copies * stride + channels, lanes] = moved.astype(slope.dtype)

    @pl.when(step == 0)
    def _():
        fetch = pltpu.make_async_copy(kernels, weights, arrived)
        fetch.start()
        if stride > channels:
            for copies in range(3):
                stacked[copies * stride + channels : (copies + 1) * stride, :] = jnp.zeros(
                    (stride - channels, stacked.shape[1]), stacked.dtype
                )
        for side, rim, row in ((3, above, 0), (4, below, height + 1)):
            blocks = []
            for j in range(count):
                start = lax.rem(turns[side] + j, count) * depth
                blocks.append(rim[0, pl.ds(pl.multiple_of(start, depth), depth), :])
            put(row, jnp.concatenate(blocks))

        def body(row, carry):
            lanes = pl.ds(pl.multiple_of(row * width, width), width)
            put(row + 1, slope[:, lanes])
            return carry

        lax.fori_loop(0, height, body, 0)
        fetch.wait()

    windows = [
        stacked[:, pl.ds(pl.multiple_of((step * rows + a) * width, width), rows * width)]
        for a in range(3)
    ]
    order = [weights[lax.rem(turns[0] + j, count)] for j in range(count)]
    grad = jnp.dot(
        jnp.concatenate(order), jnp.concatenate(windows), preferred_element_type=jnp.float32
    )
    for row in range(rows):
        lanes = slice(row * width, (row + 1) * width)
        for j in range(count):
            outs[j][row] = grad[j * depth : (j + 1) * depth, lanes].astype(outs[j].dtype)


def backward(turns, slope, above, below, kernels, count, slab):
    channels = slope.shape[0]
    width = above.shape[2]
    height = slope.shape[1] // width
    depth = channels // count
    rows = 4 if height % 4 == 0 else 1
    flops = 2 * 9 * channels * channels * height * width
    steps = height // rows
    return pl.pallas_call(
        functools.partial(backward_body, count, lax.axis_size("row"), rows),
        grid_spec=pltpu.PrefetchScalarGridSpec(
            num_scalar_prefetch=1,
            grid=(steps,),
            in_specs=[
                whole(slope.shape),
                whole(above.shape),
                whole(below.shape),
                pl.BlockSpec(memory_space=pl.ANY),
            ],
            out_specs=[pl.BlockSpec((rows, depth, width), lambda g, turns: (turns[2] * steps + g, 0, 0))]
            + [pl.BlockSpec((rows, depth, width), lambda g, _: (g, 0, 0))] * (count - 1),
            scratch_shapes=[
                pltpu.VMEM((kernels.shape[2] // 3, (height + 2) * width), jnp.bfloat16),
                pltpu.VMEM(kernels.shape, kernels.dtype),
                pltpu.SemaphoreType.DMA,
            ],
        ),
        out_shape=[jax.ShapeDtypeStruct((slab, depth, width), jnp.float32)]
        + [jax.ShapeDtypeStruct((height, depth, width), jnp.bfloat16)] * (count - 1),
        compiler_params=pltpu.CompilerParams(vmem_limit_bytes=VMEM_LIMIT),
        cost_estimate=pl.CostEstimate(
            flops=flops, bytes_accessed=8 * 1024 * 1024, transcendentals=0
        ),
        name="conv_backward",
    )(turns, slope, above, below, kernels)


def put_body(count, places, *refs):
    out = refs[count + 1]
    for j in range(count):

        @pl.when(pl.program_id(0) == j)
        def _():
            out[...] = refs[j][...].astype(out.dtype)


def put(places, arrived, whole_array):
    count = len(arrived)
    height, depth, width = arrived[0].shape
    rows = 8 if height % 8 == 0 else 1
    steps = height // rows

    def from_block(j):
        def index(block, step, places):
            return jnp.where(block == j, step, jnp.where(block < j, 0, steps - 1)), 0, 0

        return pl.BlockSpec((rows, depth, width), index)

    return pl.pallas_call(
        functools.partial(put_body, count),
        grid_spec=pltpu.PrefetchScalarGridSpec(
            num_scalar_prefetch=1,
            grid=(count, steps),
            in_specs=[from_block(j) for j in range(count)] + [pl.BlockSpec(memory_space=pl.ANY)],
            out_specs=pl.BlockSpec(
                (rows, depth, width), lambda block, step, places: (places[block] * steps + step, 0, 0)
            ),
        ),
        out_shape=jax.ShapeDtypeStruct(whole_array.shape, whole_array.dtype),
        input_output_aliases={count + 1: 0},
        cost_estimate=pl.CostEstimate(flops=0, bytes_accessed=4 * 1024 * 1024, transcendentals=0),
        name="put_rows",
    )(places, *arrived, whole_array)


def gathered_kernel(kernel):
    dp, row = lax.axis_index("dp"), lax.axis_index("row")
    dps, chans, rows = (lax.axis_size(a) for a in ("dp", "chan", "row"))
    _, inner, outer = kernel.shape
    size = outer // rows
    mine = part(kernel, row, size, 2)
    mine = jnp.transpose(mine, (2, 0, 1)).reshape(size, 9 * inner)
    over_chan = jnp.concatenate([mine] + [receive(mine, "chan", j) for j in range(1, chans)], axis=0)
    over_dp = jnp.stack([over_chan] + [receive(over_chan, "dp", j) for j in range(1, dps)])
    if dps != chans:
        each = dps // chans
        over_dp = rotated(over_dp, (dps - dp) % dps, 0)
        over_dp = over_dp.reshape(chans, each, chans * size, 9, inner)
        over_dp = jnp.transpose(over_dp, (0, 2, 3, 1, 4)).reshape(chans, chans * size, 9 * each * inner)
    return [over_dp] + [receive(over_dp, "row", j) for j in range(1, rows)]


def summed_over_images(shares):
    dp = lax.axis_index("dp")
    dps, chans, rows = (lax.axis_size(a) for a in ("dp", "chan", "row"))
    halves = shares[0]
    for j in range(1, rows):
        halves = halves + receive(shares[j], "row", j)

    def of_dp(ahead):
        if dps == chans:
            return halves[ahead % dps]
        return lax.dynamic_index_in_dim(halves, (dp + ahead) % dps, 0, keepdims=False)

    total = of_dp(0)
    for j in range(1, dps):
        total = total + receive(of_dp(-j), "dp", j)
    return total


def kernel_grad_of(total, inner, outer, in_steps):
    row, rows = lax.axis_index("row"), lax.axis_size("row")
    taps, share, channels = total.shape
    total = jnp.transpose(total, (2, 0, 1)).reshape(channels, taps * share)
    own = summed_over_chan(total, outer, in_steps)
    both = jnp.stack([own] + [receive(own, "row", j) for j in range(1, rows)])
    both = rotated(both, (rows - row) % rows, 0).reshape(rows, outer, taps, share)
    return jnp.transpose(both, (2, 0, 3, 1)).reshape(taps, inner, outer)


def shards(images, kernel, cotangent):
    row, chan = lax.axis_index("row"), lax.axis_index("chan")
    rows, chans = lax.axis_size("row"), lax.axis_size("chan")
    _, slab, _, _ = images.shape
    height = slab // chans
    images, cotangent = images[0], cotangent[0]

    def home(ahead):
        return home_of(row, (chan + ahead) % chans, chans)

    def to_homes(array, size):
        return [part(array, home(0), size, 0)] + [
            receive(part(array, home(-j), size, 0), "chan", j) for j in range(1, chans)
        ]

    halves = gathered_kernel(kernel)
    pieces = to_homes(images, height)
    if rows == 2:
        edge = jnp.where(row == 0, images[slab - 1 :], images[:1])
        edge = receive(edge, "row", 1)
        low = jnp.where(row == 0, jnp.zeros_like(edge), edge)
        high = jnp.where(row == 0, edge, jnp.zeros_like(edge))
    else:
        low = lax.ppermute(images[slab - 1 :], "row", [(i, i + 1) for i in range(rows - 1)])
        high = lax.ppermute(images[:1], "row", [(i + 1, i) for i in range(rows - 1)])

    def rim_of(at):
        begin = at * height
        above = part(images, jnp.maximum(begin - 1, 0), 1, 0)
        below = part(images, jnp.minimum(begin + height, slab - 1), 1, 0)
        return jnp.concatenate(
            [
                jnp.where(at == 0, low, above),
                jnp.where(at == chans - 1, high, below),
                part(cotangent, begin, 1, 0),
                part(cotangent, begin + height - 1, 1, 0),
            ]
        )

    rims = [rim_of(home(0))]
    rims += [receive(rim_of(home(-j)), "chan", j) for j in range(1, chans)]

    def inside(ahead):
        return lax.dynamic_slice_in_dim(cotangent, home(ahead) * height + 1, height - 2, 0)

    cotangents = [inside(0)] + [receive(inside(-j), "chan", j) for j in range(1, chans)]

    shift = (chan - stacking_base()) % chans
    place_at = home(0)
    forth = jnp.where(row % 2 == 0, 1, chans - 1)
    above_turn = jnp.where(place_at == 0, 0, forth)
    below_turn = jnp.where(place_at == chans - 1, 0, chans - forth)
    turns = jnp.stack([shift, row, place_at, above_turn, below_turn]).astype(jnp.int32)

    results = forward(turns, pieces, rims, halves, slab)
    activated, factor, stacked, first, last = results
    back_kernel = turned(halves)

    def snake(place_at):
        r, k = place_at // chans, place_at % chans
        return (k if r % 2 == 0 else chans - 1 - k) * rows + r

    line = [(snake(i), snake(i + 1)) for i in range(rows * chans - 1)]
    above = lax.ppermute(last, ("chan", "row"), line)
    below = lax.ppermute(first, ("chan", "row"), [(b, a) for a, b in line])

    lead, slope = correlate((0, 6), stacked, None, factor, cotangents, rims)
    lead = summed_over_images(lead)
    input_grads = list(backward(turns, slope, above, below, back_kernel, chans, slab))
    slope, input_grads[1] = lax.optimization_barrier((slope, input_grads[1]))
    (rest,) = correlate((6, 3), stacked, slope)
    rest = summed_over_images(rest)
    inner, outer = kernel.shape[1:]
    kernel_grad = jnp.concatenate(
        [kernel_grad_of(lead, inner, outer, False), kernel_grad_of(rest, inner, outer, False)]
    )

    places = jnp.stack([home(-j) for j in range(1, chans)]).astype(jnp.int32)

    def to_owners(blocks):
        arrived = [receive(blocks[j], "chan", chans - j) for j in range(1, chans)]
        return put(places, arrived, blocks[0])[None]

    return to_owners(activated), to_owners(input_grads), kernel_grad


def solution(mesh):
    placed = (P("dp", "row", "chan", None), P(None, "dp", "chan"), P("dp", "row", "chan", None))
    return jax.shard_map(
        shards,
        mesh=mesh,
        in_specs=placed,
        out_specs=(
            P("dp", "row", "chan", None),
            P("dp", "row", "chan", None),
            P(None, "dp", "chan"),
        ),
        check_vma=False,
    )
```

```python
import functools

import jax
import jax.numpy as jnp
from jax import lax
from jax.experimental import pallas as pl
from jax.experimental.pallas import tpu as pltpu
from jax.sharding import PartitionSpec as P


VMEM_LIMIT = 60 * 1024 * 1024


def receive(block, axis, ahead):
    count = lax.axis_size(axis)
    return lax.ppermute(block, axis, [(i, (i - ahead) % count) for i in range(count)])


def swapped(block, axis, bit):
    return lax.ppermute(block, axis, [(i, i ^ bit) for i in range(lax.axis_size(axis))])


def summed_over_chan(total, outer, in_steps):
    chans = lax.axis_size("chan")
    blocks = [total[j * outer : (j + 1) * outer] for j in range(chans)]
    if chans != 4 or not in_steps:
        own = blocks[0]
        for j in range(1, chans):
            own = own + receive(blocks[chans - j], "chan", j)
        return own
    odd = lax.axis_index("chan") % 2 == 1
    beside = swapped(jnp.concatenate([blocks[1], blocks[3]]), "chan", 1)
    first, second = beside[:outer], beside[outer:]
    other = blocks[2] + jnp.where(odd, second, first)
    return blocks[0] + jnp.where(odd, first, second) + swapped(other, "chan", 2)


def home_of(row, chan, chans):
    return jnp.where(row % 2 == 0, chan, chans - 1 - chan)


def part(array, index, size, axis):
    return lax.dynamic_slice_in_dim(array, index * size, size, axis=axis)


def rotated(array, start, axis):
    twice = jnp.concatenate([array, array], axis=axis)
    return lax.dynamic_slice_in_dim(twice, start, array.shape[axis], axis=axis)


def stacking_base():
    matched = lax.axis_size("dp") == lax.axis_size("chan")
    return lax.axis_index("dp") if matched else jnp.int32(0)


def columns_moved(block, step):
    width = block.shape[-1]
    lane = lax.broadcasted_iota(jnp.int32, block.shape, block.ndim - 1)
    if step < 0:
        moved = pltpu.roll(block, 1, block.ndim - 1)
        return jnp.where(lane == 0, jnp.zeros_like(block), moved)
    moved = pltpu.roll(block, width - 1, block.ndim - 1)
    return jnp.where(lane == width - 1, jnp.zeros_like(block), moved)


def place(stacked, channel, row, block, channels):
    depth, width = block.shape
    lanes = pl.ds(pl.multiple_of(row * width, width), width)
    wide = block.astype(jnp.float32)

    def below(copies):
        start = copies * channels + channel
        return pl.ds(start if isinstance(channel, int) else pl.multiple_of(start, 16), depth)

    stacked[below(0), lanes] = columns_moved(wide, -1).astype(block.dtype)
    stacked[below(1), lanes] = block
    stacked[below(2), lanes] = columns_moved(wide, 1).astype(block.dtype)


def window(stacked, tap_row, tap_col, channel, depth, first, rows, width, channels):
    start = pl.multiple_of((first + tap_row) * width, width)
    return stacked[tap_col * channels + channel : tap_col * channels + channel + depth, pl.ds(start, rows * width)]


def forward_taps(halves, stacked, first, rows, width):
    count = halves[0].shape[0]
    depth = halves[0].shape[2] // 9
    total = None
    for block in range(count):
        windows = [
            window(stacked, a, b, block * depth, depth, first, rows, width, count * depth)
            for a in range(3)
            for b in range(3)
        ]
        term = jnp.dot(
            jnp.concatenate([half[block] for half in halves]),
            jnp.concatenate(windows),
            preferred_element_type=jnp.float32,
        )
        total = term if total is None else total + term
    return total


def forward_body(count, shares, rows, turns, *refs):
    pieces, rims = refs[:count], refs[count : 2 * count]
    halves = refs[2 * count : 2 * count + shares]
    outs = refs[2 * count + shares : 3 * count + shares]
    factor, stacked, first, last = refs[3 * count + shares :]
    height, depth, width = pieces[0].shape
    channels = count * depth
    step = pl.program_id(0)

    @pl.when(step == 0)
    def _():
        slots = [lax.rem(turns[0] + j, count) * depth for j in range(count)]
        for j in range(count):
            place(stacked, slots[j], 0, rims[j][0], channels)
            place(stacked, slots[j], height + 1, rims[j][1], channels)

        def body(row, carry):
            for j in range(count):
                place(stacked, slots[j], row + 1, pieces[j][row], channels)
            return carry

        lax.fori_loop(0, height, body, 0)

    mixed = forward_taps(halves, stacked, step * rows, rows, width)
    size = depth // shares
    for j in range(count):
        parts = []
        for share in range(shares):
            chosen = None
            for at in range(shares):
                start = at * count * size + j * size
                value = mixed[start : start + size]
                here = turns[1] == (share - at) % shares
                chosen = value if chosen is None else jnp.where(here, value, chosen)
            parts.append(chosen)
        pre = jnp.concatenate(parts) if shares > 1 else parts[0]
        sigma = jax.nn.sigmoid(pre)
        activated = (pre * sigma).astype(jnp.bfloat16)
        slope = sigma * (1.0 + pre * (1.0 - sigma))
        for row in range(rows):
            lanes = slice(row * width, (row + 1) * width)
            factor[row, j * depth : (j + 1) * depth, :] = slope[:, lanes]
            outs[j][row] = activated[:, lanes]

    def end(out, side, row):
        for j in range(count):
            part_of = slice(j * depth, (j + 1) * depth)
            value = rims[j][side].astype(jnp.float32) * factor[row, part_of, :]
            out[0, part_of, :] = value.astype(jnp.bfloat16)

    @pl.when(step == 0)
    def _():
        end(first, 2, 0)

    @pl.when(step == pl.num_programs(0) - 1)
    def _():
        end(last, 3, rows - 1)


def whole(shape):
    return pl.BlockSpec(shape, lambda *_: (0,) * len(shape), pipeline_mode=pl.Buffered(1))


def forward(turns, pieces, rims, halves, slab):
    count = len(pieces)
    height, depth, width = pieces[0].shape
    channels = count * depth
    rows = 4 if height % 4 == 0 else 1
    flops = 2 * 9 * channels * channels * height * width
    steps = height // rows
    call = pl.pallas_call(
        functools.partial(forward_body, count, len(halves), rows),
        grid_spec=pltpu.PrefetchScalarGridSpec(
            num_scalar_prefetch=1,
            grid=(steps,),
            in_specs=[whole(pieces[0].shape)] * count
            + [whole(rims[0].shape)] * count
            + [whole(halves[0].shape)] * len(halves),
            out_specs=[pl.BlockSpec((rows, depth, width), lambda g, turns: (turns[2] * steps + g, 0, 0))]
            + [pl.BlockSpec((rows, depth, width), lambda g, _: (g, 0, 0))] * (count - 1)
            + [
                pl.BlockSpec((rows, channels, width), lambda g, _: (g, 0, 0)),
                whole((3 * channels, (height + 2) * width)),
                whole((1, channels, width)),
                whole((1, channels, width)),
            ],
        ),
        out_shape=[
            jax.ShapeDtypeStruct((height if j else slab, depth, width), jnp.bfloat16)
            for j in range(count)
        ]
        + [
            jax.ShapeDtypeStruct((height, channels, width), jnp.float32),
            jax.ShapeDtypeStruct((3 * channels, (height + 2) * width), jnp.bfloat16),
            jax.ShapeDtypeStruct((1, channels, width), jnp.bfloat16),
            jax.ShapeDtypeStruct((1, channels, width), jnp.bfloat16),
        ],
        compiler_params=pltpu.CompilerParams(vmem_limit_bytes=VMEM_LIMIT),
        cost_estimate=pl.CostEstimate(
            flops=flops, bytes_accessed=16 * 1024 * 1024, transcendentals=0
        ),
        name="conv_forward",
    )
    results = call(turns, *pieces, *rims, *halves)
    return list(results[:count]), *results[count:]


def slope_rows(factor, pieces, ends, slope):
    count = len(pieces)
    height, _, width = factor.shape
    depth = pieces[0].shape[1]

    def put(row, blocks):
        lanes = pl.ds(pl.multiple_of(row * width, width), width)
        for j in range(count):
            part_of = pl.ds(j * depth, depth)
            value = blocks[j].astype(jnp.float32) * factor[row, part_of, :]
            slope[part_of, lanes] = value.astype(jnp.bfloat16)

    def body(row, carry):
        put(row + 1, [piece[row] for piece in pieces])
        return carry

    put(0, [end[2] for end in ends])
    lax.fori_loop(0, height - 2, body, 0)
    put(height - 1, [end[3] for end in ends])


def correlate_body(first_tap, count, groups, rows, turn, stacked, *refs):
    if count:
        factor, pieces, ends = refs[0], refs[1 : 1 + count], refs[1 + count : 1 + 2 * count]
        shares, slope = refs[1 + 2 * count : -1], refs[-1]
    else:
        slope, shares = refs[0], refs[1:]
    channels, pixels = slope.shape
    width = stacked.shape[1] - pixels
    width = width // 2
    tap_row = (first_tap + pl.program_id(0)) // 3
    if count:

        @pl.when(pl.program_id(0) == 0)
        def _():
            slope_rows(factor, pieces, ends, slope)

    tap_col = lax.rem(first_tap + pl.program_id(0), 3) if count else 0
    source = stacked[
        pl.ds(pl.multiple_of(tap_col * channels, channels), channels),
        pl.ds(pl.multiple_of(tap_row * width, width), pixels),
    ]
    grads = lax.dot_general(
        source, slope[...], (((1,), (1,)), ((), ())), preferred_element_type=jnp.float32
    )
    size = channels // (groups * rows)
    for own in range(rows):

        @pl.when(turn[0] == own)
        def _():
            for j in range(rows):
                for group in range(groups):
                    start = (group * rows + (own - j) % rows) * size
                    shares[j][group, 0] = grads[start : start + size]


def correlate(taps, stacked, slope=None, factor=None, pieces=(), ends=()):
    first_tap, tap_count = taps
    channels = stacked.shape[0] // 3
    groups, rows = lax.axis_size("dp"), lax.axis_size("row")
    size = channels // (groups * rows)
    if slope is None:
        height, _, width = factor.shape
        pixels = height * width
        operands = [factor, *pieces, *ends]
        made = [jax.ShapeDtypeStruct((channels, pixels), jnp.bfloat16)]
    else:
        pixels = slope.shape[1]
        operands, made = [slope], []
    call = pl.pallas_call(
        functools.partial(correlate_body, first_tap, len(pieces), groups, rows),
        grid=(tap_count,),
        in_specs=[
            pl.BlockSpec(memory_space=pltpu.SMEM),
            pl.BlockSpec((channels, stacked.shape[1]), lambda t: ((first_tap + t) % 3, 0))
            if made == []
            else whole(stacked.shape),
        ]
        + [whole(operand.shape) for operand in operands],
        out_specs=[pl.BlockSpec((groups, 1, size, channels), lambda t: (0, t, 0, 0))] * rows
        + [whole(each.shape) for each in made],
        out_shape=[jax.ShapeDtypeStruct((groups, tap_count, size, channels), jnp.float32)] * rows
        + made,
        compiler_params=pltpu.CompilerParams(vmem_limit_bytes=VMEM_LIMIT),
        cost_estimate=pl.CostEstimate(
            flops=2 * tap_count * channels * channels * pixels,
            bytes_accessed=8 * 1024 * 1024,
            transcendentals=0,
        ),
    )
    turn = lax.axis_index("row").astype(jnp.int32)[None]
    results = call(turn, stacked, *operands)
    return (results[:rows], *results[rows:])


def padded_depth(depth):
    return -(-depth // 128) * 128


def turned_body(shares, *refs):
    halves, out = refs[:shares], refs[shares]
    _, depth, lanes = out.shape
    stride = lanes // 9
    total = halves[0].shape[2]
    both = [jnp.concatenate([half[0] for half in halves])]
    channels = both[0].shape[0]
    rows = []
    for start in range(0, total, 128):
        size = min(128, total - start)
        unit = (
            lax.broadcasted_iota(jnp.int32, (size, size), 0)
            == lax.broadcasted_iota(jnp.int32, (size, size), 1)
        ).astype(jnp.bfloat16)
        rows.append(
            lax.dot_general(
                unit,
                both[0][:, start : start + size],
                (((1,), (1,)), ((), ())),
                preferred_element_type=jnp.float32,
            )
        )
    turned = jnp.concatenate(rows)
    for tap in range(9):
        begin = (8 - tap) * depth
        value = turned[begin : begin + depth].astype(jnp.bfloat16)
        out[0, :, tap * stride : tap * stride + channels] = value
        if stride > channels:
            out[0, :, tap * stride + channels : (tap + 1) * stride] = jnp.zeros(
                (depth, stride - channels), jnp.bfloat16
            )


def turned(halves):
    shares = len(halves)
    blocks, outs, lanes = halves[0].shape
    depth = lanes // 9
    stride = padded_depth(outs * shares)
    return pl.pallas_call(
        functools.partial(turned_body, shares),
        grid=(blocks,),
        in_specs=[pl.BlockSpec((1, outs, lanes), lambda g: (g, 0, 0))] * shares,
        out_specs=pl.BlockSpec((1, depth, 9 * stride), lambda g: (g, 0, 0)),
        out_shape=jax.ShapeDtypeStruct((blocks, depth, 9 * stride), jnp.bfloat16),
        compiler_params=pltpu.CompilerParams(vmem_limit_bytes=VMEM_LIMIT),
        cost_estimate=pl.CostEstimate(
            flops=2 * 128 * blocks * outs * shares * lanes,
            bytes_accessed=4 * 1024 * 1024,
            transcendentals=0,
        ),
        name="turn_kernel",
    )(*halves)


def backward_body(count, shares, rows, turns, slope, above, below, kernels, *refs):
    outs, (stacked, weights, arrived) = refs[:count], refs[count:]
    channels = slope.shape[0]
    _, _, width = above.shape
    height = slope.shape[1] // width
    depth = channels // count
    size = depth // shares
    stride = stacked.shape[0] // 3
    step = pl.program_id(0)

    def in_share_order(wide):
        parts = []
        for at in range(shares):
            chosen = None
            for share in range(shares):
                value = jnp.concatenate(
                    [wide[j * depth + share * size : j * depth + (share + 1) * size] for j in range(count)]
                )
                here = turns[1] == (share - at) % shares
                chosen = value if chosen is None else jnp.where(here, value, chosen)
            parts.append(chosen)
        return jnp.concatenate(parts)

    def put(row, block):
        lanes = pl.ds(pl.multiple_of(row * width, width), width)
        wide = in_share_order(block.astype(jnp.float32))
        for copies, moved in enumerate((columns_moved(wide, -1), wide, columns_moved(wide, 1))):
            stacked[copies * stride : copies * stride + channels, lanes] = moved.astype(slope.dtype)

    @pl.when(step == 0)
    def _():
        fetch = pltpu.make_async_copy(kernels, weights, arrived)
        fetch.start()
        if stride > channels:
            for copies in range(3):
                stacked[copies * stride + channels : (copies + 1) * stride, :] = jnp.zeros(
                    (stride - channels, stacked.shape[1]), stacked.dtype
                )
        for side, rim, row in ((3, above, 0), (4, below, height + 1)):
            blocks = []
            for j in range(count):
                start = lax.rem(turns[side] + j, count) * depth
                blocks.append(rim[0, pl.ds(pl.multiple_of(start, depth), depth), :])
            put(row, jnp.concatenate(blocks))

        def body(row, carry):
            lanes = pl.ds(pl.multiple_of(row * width, width), width)
            put(row + 1, slope[:, lanes])
            return carry

        lax.fori_loop(0, height, body, 0)
        fetch.wait()

    windows = [
        stacked[:, pl.ds(pl.multiple_of((step * rows + a) * width, width), rows * width)]
        for a in range(3)
    ]
    order = [weights[lax.rem(turns[0] + j, count)] for j in range(count)]
    grad = jnp.dot(
        jnp.concatenate(order), jnp.concatenate(windows), preferred_element_type=jnp.float32
    )
    for row in range(rows):
        lanes = slice(row * width, (row + 1) * width)
        for j in range(count):
            outs[j][row] = grad[j * depth : (j + 1) * depth, lanes].astype(outs[j].dtype)


def backward(turns, slope, above, below, kernels, count, slab):
    channels = slope.shape[0]
    width = above.shape[2]
    height = slope.shape[1] // width
    depth = channels // count
    rows = 4 if height % 4 == 0 else 1
    flops = 2 * 9 * channels * channels * height * width
    steps = height // rows
    return pl.pallas_call(
        functools.partial(backward_body, count, lax.axis_size("row"), rows),
        grid_spec=pltpu.PrefetchScalarGridSpec(
            num_scalar_prefetch=1,
            grid=(steps,),
            in_specs=[
                whole(slope.shape),
                whole(above.shape),
                whole(below.shape),
                pl.BlockSpec(memory_space=pl.ANY),
            ],
            out_specs=[pl.BlockSpec((rows, depth, width), lambda g, turns: (turns[2] * steps + g, 0, 0))]
            + [pl.BlockSpec((rows, depth, width), lambda g, _: (g, 0, 0))] * (count - 1),
            scratch_shapes=[
                pltpu.VMEM((kernels.shape[2] // 3, (height + 2) * width), jnp.bfloat16),
                pltpu.VMEM(kernels.shape, kernels.dtype),
                pltpu.SemaphoreType.DMA,
            ],
        ),
        out_shape=[jax.ShapeDtypeStruct((slab, depth, width), jnp.float32)]
        + [jax.ShapeDtypeStruct((height, depth, width), jnp.bfloat16)] * (count - 1),
        compiler_params=pltpu.CompilerParams(vmem_limit_bytes=VMEM_LIMIT),
        cost_estimate=pl.CostEstimate(
            flops=flops, bytes_accessed=8 * 1024 * 1024, transcendentals=0
        ),
        name="conv_backward",
    )(turns, slope, above, below, kernels)


def put_body(count, places, *refs):
    arrived, out = refs[:count], refs[count + 1]
    taken, made, in_sems, out_sems = refs[count + 2 :]
    height = taken.shape[1]
    fetches = [pltpu.make_async_copy(arrived[j], taken.at[j], in_sems.at[j]) for j in range(count)]
    for fetch in fetches:
        fetch.start()
    stores = []
    for j in range(count):
        fetches[j].wait()
        made[j] = taken[j].astype(made.dtype)
        store = pltpu.make_async_copy(
            made.at[j], out.at[pl.ds(places[j] * height, height)], out_sems.at[j]
        )
        store.start()
        stores.append(store)
    for store in stores:
        store.wait()


def put(places, arrived, whole_array):
    count = len(arrived)
    shape = (count, *arrived[0].shape)
    return pl.pallas_call(
        functools.partial(put_body, count),
        in_specs=[pl.BlockSpec(memory_space=pltpu.SMEM)]
        + [pl.BlockSpec(memory_space=pl.ANY)] * (count + 1),
        out_specs=pl.BlockSpec(memory_space=pl.ANY),
        out_shape=jax.ShapeDtypeStruct(whole_array.shape, whole_array.dtype),
        scratch_shapes=[
            pltpu.VMEM(shape, arrived[0].dtype),
            pltpu.VMEM(shape, whole_array.dtype),
            pltpu.SemaphoreType.DMA((count,)),
            pltpu.SemaphoreType.DMA((count,)),
        ],
        input_output_aliases={count + 1: 0},
        compiler_params=pltpu.CompilerParams(vmem_limit_bytes=VMEM_LIMIT),
        cost_estimate=pl.CostEstimate(flops=0, bytes_accessed=4 * 1024 * 1024, transcendentals=0),
        name="put_rows",
    )(places, *arrived, whole_array)


def gathered_kernel(kernel):
    dp, row = lax.axis_index("dp"), lax.axis_index("row")
    dps, chans, rows = (lax.axis_size(a) for a in ("dp", "chan", "row"))
    _, inner, outer = kernel.shape
    size = outer // rows
    mine = part(kernel, row, size, 2)
    mine = jnp.transpose(mine, (2, 0, 1)).reshape(size, 9 * inner)
    over_chan = jnp.concatenate([mine] + [receive(mine, "chan", j) for j in range(1, chans)], axis=0)
    over_dp = jnp.stack([over_chan] + [receive(over_chan, "dp", j) for j in range(1, dps)])
    if dps != chans:
        each = dps // chans
        over_dp = rotated(over_dp, (dps - dp) % dps, 0)
        over_dp = over_dp.reshape(chans, each, chans * size, 9, inner)
        over_dp = jnp.transpose(over_dp, (0, 2, 3, 1, 4)).reshape(chans, chans * size, 9 * each * inner)
    return [over_dp] + [receive(over_dp, "row", j) for j in range(1, rows)]


def summed_over_images(shares):
    dp = lax.axis_index("dp")
    dps, chans, rows = (lax.axis_size(a) for a in ("dp", "chan", "row"))
    halves = shares[0]
    for j in range(1, rows):
        halves = halves + receive(shares[j], "row", j)

    def of_dp(ahead):
        if dps == chans:
            return halves[ahead % dps]
        return lax.dynamic_index_in_dim(halves, (dp + ahead) % dps, 0, keepdims=False)

    total = of_dp(0)
    for j in range(1, dps):
        total = total + receive(of_dp(-j), "dp", j)
    return total


def kernel_grad_of(total, inner, outer, in_steps):
    row, rows = lax.axis_index("row"), lax.axis_size("row")
    taps, share, channels = total.shape
    total = jnp.transpose(total, (2, 0, 1)).reshape(channels, taps * share)
    own = summed_over_chan(total, outer, in_steps)
    both = jnp.stack([own] + [receive(own, "row", j) for j in range(1, rows)])
    both = rotated(both, (rows - row) % rows, 0).reshape(rows, outer, taps, share)
    return jnp.transpose(both, (2, 0, 3, 1)).reshape(taps, inner, outer)


def shards(images, kernel, cotangent):
    row, chan = lax.axis_index("row"), lax.axis_index("chan")
    rows, chans = lax.axis_size("row"), lax.axis_size("chan")
    _, slab, _, _ = images.shape
    height = slab // chans
    images, cotangent = images[0], cotangent[0]

    def home(ahead):
        return home_of(row, (chan + ahead) % chans, chans)

    def to_homes(array, size):
        return [part(array, home(0), size, 0)] + [
            receive(part(array, home(-j), size, 0), "chan", j) for j in range(1, chans)
        ]

    halves = gathered_kernel(kernel)
    pieces = to_homes(images, height)
    if rows == 2:
        edge = jnp.where(row == 0, images[slab - 1 :], images[:1])
        edge = receive(edge, "row", 1)
        low = jnp.where(row == 0, jnp.zeros_like(edge), edge)
        high = jnp.where(row == 0, edge, jnp.zeros_like(edge))
    else:
        low = lax.ppermute(images[slab - 1 :], "row", [(i, i + 1) for i in range(rows - 1)])
        high = lax.ppermute(images[:1], "row", [(i + 1, i) for i in range(rows - 1)])

    def rim_of(at):
        begin = at * height
        above = part(images, jnp.maximum(begin - 1, 0), 1, 0)
        below = part(images, jnp.minimum(begin + height, slab - 1), 1, 0)
        return jnp.concatenate(
            [
                jnp.where(at == 0, low, above),
                jnp.where(at == chans - 1, high, below),
                part(cotangent, begin, 1, 0),
                part(cotangent, begin + height - 1, 1, 0),
            ]
        )

    rims = [rim_of(home(0))]
    rims += [receive(rim_of(home(-j)), "chan", j) for j in range(1, chans)]

    def inside(ahead):
        return lax.dynamic_slice_in_dim(cotangent, home(ahead) * height + 1, height - 2, 0)

    cotangents = [inside(0)] + [receive(inside(-j), "chan", j) for j in range(1, chans)]

    shift = (chan - stacking_base()) % chans
    place_at = home(0)
    forth = jnp.where(row % 2 == 0, 1, chans - 1)
    above_turn = jnp.where(place_at == 0, 0, forth)
    below_turn = jnp.where(place_at == chans - 1, 0, chans - forth)
    turns = jnp.stack([shift, row, place_at, above_turn, below_turn]).astype(jnp.int32)

    results = forward(turns, pieces, rims, halves, slab)
    activated, factor, stacked, first, last = results
    back_kernel = turned(halves)

    def snake(place_at):
        r, k = place_at // chans, place_at % chans
        return (k if r % 2 == 0 else chans - 1 - k) * rows + r

    line = [(snake(i), snake(i + 1)) for i in range(rows * chans - 1)]
    above = lax.ppermute(last, ("chan", "row"), line)
    below = lax.ppermute(first, ("chan", "row"), [(b, a) for a, b in line])

    lead, slope = correlate((0, 6), stacked, None, factor, cotangents, rims)
    lead = summed_over_images(lead)
    input_grads = list(backward(turns, slope, above, below, back_kernel, chans, slab))
    slope, input_grads[1] = lax.optimization_barrier((slope, input_grads[1]))
    (rest,) = correlate((6, 3), stacked, slope)
    rest = summed_over_images(rest)
    inner, outer = kernel.shape[1:]
    kernel_grad = jnp.concatenate(
        [kernel_grad_of(lead, inner, outer, False), kernel_grad_of(rest, inner, outer, False)]
    )

    places = jnp.stack([home(-j) for j in range(1, chans)]).astype(jnp.int32)

    def to_owners(blocks):
        arrived = [receive(blocks[j], "chan", chans - j) for j in range(1, chans)]
        return put(places, arrived, blocks[0])[None]

    return to_owners(activated), to_owners(input_grads), kernel_grad


def solution(mesh):
    placed = (P("dp", "row", "chan", None), P(None, "dp", "chan"), P("dp", "row", "chan", None))
    return jax.shard_map(
        shards,
        mesh=mesh,
        in_specs=placed,
        out_specs=(
            P("dp", "row", "chan", None),
            P("dp", "row", "chan", None),
            P(None, "dp", "chan"),
        ),
        check_vma=False,
    )
```

```python
import functools

import jax
import jax.numpy as jnp
from jax import lax
from jax.experimental import pallas as pl
from jax.experimental.pallas import tpu as pltpu
from jax.sharding import PartitionSpec as P


VMEM_LIMIT = 60 * 1024 * 1024


def receive(block, axis, ahead):
    count = lax.axis_size(axis)
    return lax.ppermute(block, axis, [(i, (i - ahead) % count) for i in range(count)])


def swapped(block, axis, bit):
    return lax.ppermute(block, axis, [(i, i ^ bit) for i in range(lax.axis_size(axis))])


def summed_over_chan(lead, rest, outer):
    chans = lax.axis_size("chan")

    def blocks_of(total):
        return [total[j * outer : (j + 1) * outer] for j in range(chans)]

    lead, rest = blocks_of(lead), blocks_of(rest)
    if chans != 4:
        owns = []
        for blocks in (lead, rest):
            own = blocks[0]
            for j in range(1, chans):
                own = own + receive(blocks[chans - j], "chan", j)
            owns.append(own)
        return jnp.concatenate(owns, axis=1)
    odd = lax.axis_index("chan") % 2 == 1
    beside = swapped(jnp.concatenate([lead[1], lead[3]]), "chan", 1)
    first, second = beside[:outer], beside[outer:]
    other = lead[2] + jnp.where(odd, second, first)
    last = jnp.concatenate([other, rest[2]], axis=1)
    near = rest[0] + receive(rest[3], "chan", 1) + receive(rest[1], "chan", 3)
    mine = jnp.concatenate([lead[0] + jnp.where(odd, first, second), near], axis=1)
    return mine + receive(last, "chan", 2)


def home_of(row, chan, chans):
    return jnp.where(row % 2 == 0, chan, chans - 1 - chan)


def part(array, index, size, axis):
    return lax.dynamic_slice_in_dim(array, index * size, size, axis=axis)


def rotated(array, start, axis):
    twice = jnp.concatenate([array, array], axis=axis)
    return lax.dynamic_slice_in_dim(twice, start, array.shape[axis], axis=axis)


def stacking_base():
    matched = lax.axis_size("dp") == lax.axis_size("chan")
    return lax.axis_index("dp") if matched else jnp.int32(0)


def columns_moved(block, step):
    width = block.shape[-1]
    lane = lax.broadcasted_iota(jnp.int32, block.shape, block.ndim - 1)
    if step < 0:
        moved = pltpu.roll(block, 1, block.ndim - 1)
        return jnp.where(lane == 0, jnp.zeros_like(block), moved)
    moved = pltpu.roll(block, width - 1, block.ndim - 1)
    return jnp.where(lane == width - 1, jnp.zeros_like(block), moved)


def place(stacked, channel, row, block, channels):
    depth, width = block.shape
    lanes = pl.ds(pl.multiple_of(row * width, width), width)
    wide = block.astype(jnp.float32)

    def below(copies):
        start = copies * channels + channel
        return pl.ds(start if isinstance(channel, int) else pl.multiple_of(start, 16), depth)

    stacked[below(0), lanes] = columns_moved(wide, -1).astype(block.dtype)
    stacked[below(1), lanes] = block
    stacked[below(2), lanes] = columns_moved(wide, 1).astype(block.dtype)


def window(stacked, tap_row, tap_col, channel, depth, first, rows, width, channels):
    start = pl.multiple_of((first + tap_row) * width, width)
    return stacked[tap_col * channels + channel : tap_col * channels + channel + depth, pl.ds(start, rows * width)]


def forward_taps(halves, stacked, first, rows, width):
    count = halves[0].shape[0]
    depth = halves[0].shape[2] // 9
    total = None
    for block in range(count):
        windows = [
            window(stacked, a, b, block * depth, depth, first, rows, width, count * depth)
            for a in range(3)
            for b in range(3)
        ]
        term = jnp.dot(
            jnp.concatenate([half[block] for half in halves]),
            jnp.concatenate(windows),
            preferred_element_type=jnp.float32,
        )
        total = term if total is None else total + term
    return total


def forward_body(count, shares, rows, turns, *refs):
    pieces, rims = refs[:count], refs[count : 2 * count]
    halves = refs[2 * count : 2 * count + shares]
    outs = refs[2 * count + shares : 3 * count + shares]
    factor, stacked, first, last = refs[3 * count + shares :]
    height, depth, width = pieces[0].shape
    channels = count * depth
    step = pl.program_id(0)

    @pl.when(step == 0)
    def _():
        slots = [lax.rem(turns[0] + j, count) * depth for j in range(count)]
        for j in range(count):
            place(stacked, slots[j], 0, rims[j][0], channels)
            place(stacked, slots[j], height + 1, rims[j][1], channels)

        def body(row, carry):
            for j in range(count):
                place(stacked, slots[j], row + 1, pieces[j][row], channels)
            return carry

        lax.fori_loop(0, height, body, 0)

    mixed = forward_taps(halves, stacked, step * rows, rows, width)
    size = depth // shares
    for j in range(count):
        parts = []
        for share in range(shares):
            chosen = None
            for at in range(shares):
                start = at * count * size + j * size
                value = mixed[start : start + size]
                here = turns[1] == (share - at) % shares
                chosen = value if chosen is None else jnp.where(here, value, chosen)
            parts.append(chosen)
        pre = jnp.concatenate(parts) if shares > 1 else parts[0]
        sigma = jax.nn.sigmoid(pre)
        activated = (pre * sigma).astype(jnp.bfloat16)
        slope = sigma * (1.0 + pre * (1.0 - sigma))
        for row in range(rows):
            lanes = slice(row * width, (row + 1) * width)
            factor[row, j * depth : (j + 1) * depth, :] = slope[:, lanes]
            outs[j][row] = activated[:, lanes]

    def end(out, side, row):
        for j in range(count):
            part_of = slice(j * depth, (j + 1) * depth)
            value = rims[j][side].astype(jnp.float32) * factor[row, part_of, :]
            out[0, part_of, :] = value.astype(jnp.bfloat16)

    @pl.when(step == 0)
    def _():
        end(first, 2, 0)

    @pl.when(step == pl.num_programs(0) - 1)
    def _():
        end(last, 3, rows - 1)


def whole(shape):
    return pl.BlockSpec(shape, lambda *_: (0,) * len(shape), pipeline_mode=pl.Buffered(1))


def forward(turns, pieces, rims, halves, slab):
    count = len(pieces)
    height, depth, width = pieces[0].shape
    channels = count * depth
    rows = 4 if height % 4 == 0 else 1
    flops = 2 * 9 * channels * channels * height * width
    steps = height // rows
    call = pl.pallas_call(
        functools.partial(forward_body, count, len(halves), rows),
        grid_spec=pltpu.PrefetchScalarGridSpec(
            num_scalar_prefetch=1,
            grid=(steps,),
            in_specs=[whole(pieces[0].shape)] * count
            + [whole(rims[0].shape)] * count
            + [whole(halves[0].shape)] * len(halves),
            out_specs=[pl.BlockSpec((rows, depth, width), lambda g, turns: (turns[2] * steps + g, 0, 0))]
            + [pl.BlockSpec((rows, depth, width), lambda g, _: (g, 0, 0))] * (count - 1)
            + [
                pl.BlockSpec((rows, channels, width), lambda g, _: (g, 0, 0)),
                whole((3 * channels, (height + 2) * width)),
                whole((1, channels, width)),
                whole((1, channels, width)),
            ],
        ),
        out_shape=[
            jax.ShapeDtypeStruct((height if j else slab, depth, width), jnp.bfloat16)
            for j in range(count)
        ]
        + [
            jax.ShapeDtypeStruct((height, channels, width), jnp.float32),
            jax.ShapeDtypeStruct((3 * channels, (height + 2) * width), jnp.bfloat16),
            jax.ShapeDtypeStruct((1, channels, width), jnp.bfloat16),
            jax.ShapeDtypeStruct((1, channels, width), jnp.bfloat16),
        ],
        compiler_params=pltpu.CompilerParams(vmem_limit_bytes=VMEM_LIMIT),
        cost_estimate=pl.CostEstimate(
            flops=flops, bytes_accessed=16 * 1024 * 1024, transcendentals=0
        ),
        name="conv_forward",
    )
    results = call(turns, *pieces, *rims, *halves)
    return list(results[:count]), *results[count:]


def slope_rows(factor, pieces, ends, slope):
    count = len(pieces)
    height, _, width = factor.shape
    depth = pieces[0].shape[1]

    def put(row, blocks):
        lanes = pl.ds(pl.multiple_of(row * width, width), width)
        for j in range(count):
            part_of = pl.ds(j * depth, depth)
            value = blocks[j].astype(jnp.float32) * factor[row, part_of, :]
            slope[part_of, lanes] = value.astype(jnp.bfloat16)

    def body(row, carry):
        put(row + 1, [piece[row] for piece in pieces])
        return carry

    put(0, [end[2] for end in ends])
    lax.fori_loop(0, height - 2, body, 0)
    put(height - 1, [end[3] for end in ends])


def correlate_body(first_tap, count, groups, rows, turn, stacked, *refs):
    if count:
        factor, pieces, ends = refs[0], refs[1 : 1 + count], refs[1 + count : 1 + 2 * count]
        shares, slope = refs[1 + 2 * count : -1], refs[-1]
    else:
        slope, shares = refs[0], refs[1:]
    channels, pixels = slope.shape
    width = stacked.shape[1] - pixels
    width = width // 2
    tap_row = (first_tap + pl.program_id(0)) // 3
    if count:

        @pl.when(pl.program_id(0) == 0)
        def _():
            slope_rows(factor, pieces, ends, slope)

    tap_col = lax.rem(first_tap + pl.program_id(0), 3) if count else 0
    source = stacked[
        pl.ds(pl.multiple_of(tap_col * channels, channels), channels),
        pl.ds(pl.multiple_of(tap_row * width, width), pixels),
    ]
    grads = lax.dot_general(
        source, slope[...], (((1,), (1,)), ((), ())), preferred_element_type=jnp.float32
    )
    size = channels // (groups * rows)
    for own in range(rows):

        @pl.when(turn[0] == own)
        def _():
            for j in range(rows):
                for group in range(groups):
                    start = (group * rows + (own - j) % rows) * size
                    shares[j][group, 0] = grads[start : start + size]


def correlate(taps, stacked, slope=None, factor=None, pieces=(), ends=()):
    first_tap, tap_count = taps
    channels = stacked.shape[0] // 3
    groups, rows = lax.axis_size("dp"), lax.axis_size("row")
    size = channels // (groups * rows)
    if slope is None:
        height, _, width = factor.shape
        pixels = height * width
        operands = [factor, *pieces, *ends]
        made = [jax.ShapeDtypeStruct((channels, pixels), jnp.bfloat16)]
    else:
        pixels = slope.shape[1]
        operands, made = [slope], []
    call = pl.pallas_call(
        functools.partial(correlate_body, first_tap, len(pieces), groups, rows),
        grid=(tap_count,),
        in_specs=[
            pl.BlockSpec(memory_space=pltpu.SMEM),
            pl.BlockSpec((channels, stacked.shape[1]), lambda t: ((first_tap + t) % 3, 0))
            if made == []
            else whole(stacked.shape),
        ]
        + [whole(operand.shape) for operand in operands],
        out_specs=[pl.BlockSpec((groups, 1, size, channels), lambda t: (0, t, 0, 0))] * rows
        + [whole(each.shape) for each in made],
        out_shape=[jax.ShapeDtypeStruct((groups, tap_count, size, channels), jnp.float32)] * rows
        + made,
        compiler_params=pltpu.CompilerParams(vmem_limit_bytes=VMEM_LIMIT),
        cost_estimate=pl.CostEstimate(
            flops=2 * tap_count * channels * channels * pixels,
            bytes_accessed=8 * 1024 * 1024,
            transcendentals=0,
        ),
    )
    turn = lax.axis_index("row").astype(jnp.int32)[None]
    results = call(turn, stacked, *operands)
    return (results[:rows], *results[rows:])


def padded_depth(depth):
    return -(-depth // 128) * 128


def turned_body(shares, *refs):
    halves, out = refs[:shares], refs[shares]
    _, depth, lanes = out.shape
    stride = lanes // 9
    total = halves[0].shape[2]
    both = [jnp.concatenate([half[0] for half in halves])]
    channels = both[0].shape[0]
    rows = []
    for start in range(0, total, 128):
        size = min(128, total - start)
        unit = (
            lax.broadcasted_iota(jnp.int32, (size, size), 0)
            == lax.broadcasted_iota(jnp.int32, (size, size), 1)
        ).astype(jnp.bfloat16)
        rows.append(
            lax.dot_general(
                unit,
                both[0][:, start : start + size],
                (((1,), (1,)), ((), ())),
                preferred_element_type=jnp.float32,
            )
        )
    turned = jnp.concatenate(rows)
    for tap in range(9):
        begin = (8 - tap) * depth
        value = turned[begin : begin + depth].astype(jnp.bfloat16)
        out[0, :, tap * stride : tap * stride + channels] = value
        if stride > channels:
            out[0, :, tap * stride + channels : (tap + 1) * stride] = jnp.zeros(
                (depth, stride - channels), jnp.bfloat16
            )


def turned(halves):
    shares = len(halves)
    blocks, outs, lanes = halves[0].shape
    depth = lanes // 9
    stride = padded_depth(outs * shares)
    return pl.pallas_call(
        functools.partial(turned_body, shares),
        grid=(blocks,),
        in_specs=[pl.BlockSpec((1, outs, lanes), lambda g: (g, 0, 0))] * shares,
        out_specs=pl.BlockSpec((1, depth, 9 * stride), lambda g: (g, 0, 0)),
        out_shape=jax.ShapeDtypeStruct((blocks, depth, 9 * stride), jnp.bfloat16),
        compiler_params=pltpu.CompilerParams(vmem_limit_bytes=VMEM_LIMIT),
        cost_estimate=pl.CostEstimate(
            flops=2 * 128 * blocks * outs * shares * lanes,
            bytes_accessed=4 * 1024 * 1024,
            transcendentals=0,
        ),
        name="turn_kernel",
    )(*halves)


def backward_body(count, shares, rows, turns, slope, above, below, kernels, *refs):
    outs, (stacked, weights, arrived) = refs[:count], refs[count:]
    channels = slope.shape[0]
    _, _, width = above.shape
    height = slope.shape[1] // width
    depth = channels // count
    size = depth // shares
    stride = stacked.shape[0] // 3
    step = pl.program_id(0)

    def in_share_order(wide):
        parts = []
        for at in range(shares):
            chosen = None
            for share in range(shares):
                value = jnp.concatenate(
                    [wide[j * depth + share * size : j * depth + (share + 1) * size] for j in range(count)]
                )
                here = turns[1] == (share - at) % shares
                chosen = value if chosen is None else jnp.where(here, value, chosen)
            parts.append(chosen)
        return jnp.concatenate(parts)

    def put(row, block):
        lanes = pl.ds(pl.multiple_of(row * width, width), width)
        wide = in_share_order(block.astype(jnp.float32))
        for copies, moved in enumerate((columns_moved(wide, -1), wide, columns_moved(wide, 1))):
            stacked[copies * stride : copies * stride + channels, lanes] = moved.astype(slope.dtype)

    @pl.when(step == 0)
    def _():
        fetch = pltpu.make_async_copy(kernels, weights, arrived)
        fetch.start()
        if stride > channels:
            for copies in range(3):
                stacked[copies * stride + channels : (copies + 1) * stride, :] = jnp.zeros(
                    (stride - channels, stacked.shape[1]), stacked.dtype
                )
        for side, rim, row in ((3, above, 0), (4, below, height + 1)):
            blocks = []
            for j in range(count):
                start = lax.rem(turns[side] + j, count) * depth
                blocks.append(rim[0, pl.ds(pl.multiple_of(start, depth), depth), :])
            put(row, jnp.concatenate(blocks))

        def body(row, carry):
            lanes = pl.ds(pl.multiple_of(row * width, width), width)
            put(row + 1, slope[:, lanes])
            return carry

        lax.fori_loop(0, height, body, 0)
        fetch.wait()

    windows = [
        stacked[:, pl.ds(pl.multiple_of((step * rows + a) * width, width), rows * width)]
        for a in range(3)
    ]
    order = [weights[lax.rem(turns[0] + j, count)] for j in range(count)]
    grad = jnp.dot(
        jnp.concatenate(order), jnp.concatenate(windows), preferred_element_type=jnp.float32
    )
    for row in range(rows):
        lanes = slice(row * width, (row + 1) * width)
        for j in range(count):
            outs[j][row] = grad[j * depth : (j + 1) * depth, lanes].astype(outs[j].dtype)


def backward(turns, slope, above, below, kernels, count, slab):
    channels = slope.shape[0]
    width = above.shape[2]
    height = slope.shape[1] // width
    depth = channels // count
    rows = 4 if height % 4 == 0 else 1
    flops = 2 * 9 * channels * channels * height * width
    steps = height // rows
    return pl.pallas_call(
        functools.partial(backward_body, count, lax.axis_size("row"), rows),
        grid_spec=pltpu.PrefetchScalarGridSpec(
            num_scalar_prefetch=1,
            grid=(steps,),
            in_specs=[
                whole(slope.shape),
                whole(above.shape),
                whole(below.shape),
                pl.BlockSpec(memory_space=pl.ANY),
            ],
            out_specs=[pl.BlockSpec((rows, depth, width), lambda g, turns: (turns[2] * steps + g, 0, 0))]
            + [pl.BlockSpec((rows, depth, width), lambda g, _: (g, 0, 0))] * (count - 1),
            scratch_shapes=[
                pltpu.VMEM((kernels.shape[2] // 3, (height + 2) * width), jnp.bfloat16),
                pltpu.VMEM(kernels.shape, kernels.dtype),
                pltpu.SemaphoreType.DMA,
            ],
        ),
        out_shape=[jax.ShapeDtypeStruct((slab, depth, width), jnp.float32)]
        + [jax.ShapeDtypeStruct((height, depth, width), jnp.bfloat16)] * (count - 1),
        compiler_params=pltpu.CompilerParams(vmem_limit_bytes=VMEM_LIMIT),
        cost_estimate=pl.CostEstimate(
            flops=flops, bytes_accessed=8 * 1024 * 1024, transcendentals=0
        ),
        name="conv_backward",
    )(turns, slope, above, below, kernels)


def put_body(count, places, *refs):
    arrived, out = refs[:count], refs[count + 1]
    taken, made, in_sems, out_sems = refs[count + 2 :]
    height = taken.shape[1]
    fetches = [pltpu.make_async_copy(arrived[j], taken.at[j], in_sems.at[j]) for j in range(count)]
    for fetch in fetches:
        fetch.start()
    stores = []
    for j in range(count):
        fetches[j].wait()
        made[j] = taken[j].astype(made.dtype)
        store = pltpu.make_async_copy(
            made.at[j], out.at[pl.ds(places[j] * height, height)], out_sems.at[j]
        )
        store.start()
        stores.append(store)
    for store in stores:
        store.wait()


def put(places, arrived, whole_array):
    count = len(arrived)
    shape = (count, *arrived[0].shape)
    return pl.pallas_call(
        functools.partial(put_body, count),
        in_specs=[pl.BlockSpec(memory_space=pltpu.SMEM)]
        + [pl.BlockSpec(memory_space=pl.ANY)] * (count + 1),
        out_specs=pl.BlockSpec(memory_space=pl.ANY),
        out_shape=jax.ShapeDtypeStruct(whole_array.shape, whole_array.dtype),
        scratch_shapes=[
            pltpu.VMEM(shape, arrived[0].dtype),
            pltpu.VMEM(shape, whole_array.dtype),
            pltpu.SemaphoreType.DMA((count,)),
            pltpu.SemaphoreType.DMA((count,)),
        ],
        input_output_aliases={count + 1: 0},
        compiler_params=pltpu.CompilerParams(vmem_limit_bytes=VMEM_LIMIT),
        cost_estimate=pl.CostEstimate(flops=0, bytes_accessed=4 * 1024 * 1024, transcendentals=0),
        name="put_rows",
    )(places, *arrived, whole_array)


def gathered_kernel(kernel):
    dp, row = lax.axis_index("dp"), lax.axis_index("row")
    dps, chans, rows = (lax.axis_size(a) for a in ("dp", "chan", "row"))
    _, inner, outer = kernel.shape
    size = outer // rows
    mine = part(kernel, row, size, 2)
    mine = jnp.transpose(mine, (2, 0, 1)).reshape(size, 9 * inner)
    over_chan = jnp.concatenate([mine] + [receive(mine, "chan", j) for j in range(1, chans)], axis=0)
    over_dp = jnp.stack([over_chan] + [receive(over_chan, "dp", j) for j in range(1, dps)])
    if dps != chans:
        each = dps // chans
        over_dp = rotated(over_dp, (dps - dp) % dps, 0)
        over_dp = over_dp.reshape(chans, each, chans * size, 9, inner)
        over_dp = jnp.transpose(over_dp, (0, 2, 3, 1, 4)).reshape(chans, chans * size, 9 * each * inner)
    return [over_dp] + [receive(over_dp, "row", j) for j in range(1, rows)]


def summed_over_images(shares):
    dp = lax.axis_index("dp")
    dps, chans, rows = (lax.axis_size(a) for a in ("dp", "chan", "row"))
    halves = shares[0]
    for j in range(1, rows):
        halves = halves + receive(shares[j], "row", j)

    def of_dp(ahead):
        if dps == chans:
            return halves[ahead % dps]
        return lax.dynamic_index_in_dim(halves, (dp + ahead) % dps, 0, keepdims=False)

    total = of_dp(0)
    for j in range(1, dps):
        total = total + receive(of_dp(-j), "dp", j)
    return total


def kernel_grad_of(lead, rest, inner, outer):
    row, rows = lax.axis_index("row"), lax.axis_size("row")
    share, channels = lead.shape[1:]
    taps = lead.shape[0] + rest.shape[0]

    def turned_rows(total):
        return jnp.transpose(total, (2, 0, 1)).reshape(channels, -1)

    own = summed_over_chan(turned_rows(lead), turned_rows(rest), outer)
    both = jnp.stack([own] + [receive(own, "row", j) for j in range(1, rows)])
    both = rotated(both, (rows - row) % rows, 0).reshape(rows, outer, taps, share)
    return jnp.transpose(both, (2, 0, 3, 1)).reshape(taps, inner, outer)


def shards(images, kernel, cotangent):
    row, chan = lax.axis_index("row"), lax.axis_index("chan")
    rows, chans = lax.axis_size("row"), lax.axis_size("chan")
    _, slab, _, _ = images.shape
    height = slab // chans
    images, cotangent = images[0], cotangent[0]

    def home(ahead):
        return home_of(row, (chan + ahead) % chans, chans)

    def to_homes(array, size):
        return [part(array, home(0), size, 0)] + [
            receive(part(array, home(-j), size, 0), "chan", j) for j in range(1, chans)
        ]

    halves = gathered_kernel(kernel)
    pieces = to_homes(images, height)
    if rows == 2:
        edge = jnp.where(row == 0, images[slab - 1 :], images[:1])
        edge = receive(edge, "row", 1)
        low = jnp.where(row == 0, jnp.zeros_like(edge), edge)
        high = jnp.where(row == 0, edge, jnp.zeros_like(edge))
    else:
        low = lax.ppermute(images[slab - 1 :], "row", [(i, i + 1) for i in range(rows - 1)])
        high = lax.ppermute(images[:1], "row", [(i + 1, i) for i in range(rows - 1)])

    def rim_of(at):
        begin = at * height
        above = part(images, jnp.maximum(begin - 1, 0), 1, 0)
        below = part(images, jnp.minimum(begin + height, slab - 1), 1, 0)
        return jnp.concatenate(
            [
                jnp.where(at == 0, low, above),
                jnp.where(at == chans - 1, high, below),
                part(cotangent, begin, 1, 0),
                part(cotangent, begin + height - 1, 1, 0),
            ]
        )

    rims = [rim_of(home(0))]
    rims += [receive(rim_of(home(-j)), "chan", j) for j in range(1, chans)]

    def inside(ahead):
        return lax.dynamic_slice_in_dim(cotangent, home(ahead) * height + 1, height - 2, 0)

    cotangents = [inside(0)] + [receive(inside(-j), "chan", j) for j in range(1, chans)]

    shift = (chan - stacking_base()) % chans
    place_at = home(0)
    forth = jnp.where(row % 2 == 0, 1, chans - 1)
    above_turn = jnp.where(place_at == 0, 0, forth)
    below_turn = jnp.where(place_at == chans - 1, 0, chans - forth)
    turns = jnp.stack([shift, row, place_at, above_turn, below_turn]).astype(jnp.int32)

    results = forward(turns, pieces, rims, halves, slab)
    activated, factor, stacked, first, last = results
    back_kernel = turned(halves)

    def snake(place_at):
        r, k = place_at // chans, place_at % chans
        return (k if r % 2 == 0 else chans - 1 - k) * rows + r

    line = [(snake(i), snake(i + 1)) for i in range(rows * chans - 1)]
    above = lax.ppermute(last, ("chan", "row"), line)
    below = lax.ppermute(first, ("chan", "row"), [(b, a) for a, b in line])

    lead, slope = correlate((0, 6), stacked, None, factor, cotangents, rims)
    lead = summed_over_images(lead)
    input_grads = list(backward(turns, slope, above, below, back_kernel, chans, slab))
    slope, input_grads[1] = lax.optimization_barrier((slope, input_grads[1]))
    (rest,) = correlate((6, 3), stacked, slope)
    rest = summed_over_images(rest)
    inner, outer = kernel.shape[1:]
    kernel_grad = kernel_grad_of(lead, rest, inner, outer)

    places = jnp.stack([home(-j) for j in range(1, chans)]).astype(jnp.int32)

    def to_owners(blocks):
        arrived = [receive(blocks[j], "chan", chans - j) for j in range(1, chans)]
        return put(places, arrived, blocks[0])[None]

    return to_owners(activated), to_owners(input_grads), kernel_grad


def solution(mesh):
    placed = (P("dp", "row", "chan", None), P(None, "dp", "chan"), P("dp", "row", "chan", None))
    return jax.shard_map(
        shards,
        mesh=mesh,
        in_specs=placed,
        out_specs=(
            P("dp", "row", "chan", None),
            P("dp", "row", "chan", None),
            P(None, "dp", "chan"),
        ),
        check_vma=False,
    )
```
